32 devices in a mesh: shard: 2 (over x), ctx: 4 (over y, core), tp: 4 (over z).
Axes of the slice: x: 2, y: 2, z: 4, core: 2. Of those that a mesh axis runs over, the one named last changes fastest.
Arguments:
- tokens: bfloat16 [4, 4096, 1024], P('shard', ('ctx', 'tp')), may hold values from -6 to 6
- positions: int32 [4, 4096], P('shard', 'ctx'), may hold values from 0 to 12287, as said below
- first_gain: float32 [1024], replicated, may hold values from 0.5 to 1.5
- query_weight: bfloat16 [1024, 1024], P(('shard', 'ctx'), 'tp'), may hold values from -0.1875 to 0.1875
- key_weight: bfloat16 [1024, 512], P(('shard', 'ctx'), 'tp'), may hold values from -0.1875 to 0.1875
- value_weight: bfloat16 [1024, 512], P(('shard', 'ctx'), 'tp'), may hold values from -0.1875 to 0.1875
- query_gain: float32 [64], replicated, may hold values from 0.1 to 1.9
- key_gain: float32 [64], replicated, may hold values from 0.1 to 1.9
- output_weight: bfloat16 [1024, 1024], P('tp', ('shard', 'ctx')), may hold values from -1 to 1
- second_gain: float32 [1024], replicated, may hold values from 0.5 to 1.5
- gate_weight: bfloat16 [1024, 4608], P(('shard', 'ctx'), 'tp'), may hold values from -0.1875 to 0.1875
- up_weight: bfloat16 [1024, 4608], P(('shard', 'ctx'), 'tp'), may hold values from -0.1875 to 0.1875
- down_weight: bfloat16 [4608, 1024], P('tp', ('shard', 'ctx')), may hold values from -0.09375 to 0.09375
- upstream: bfloat16 [4, 4096, 1024], P('shard', ('ctx', 'tp')), may hold values from -6 to 6
Outputs:
- block_output: bfloat16 [4, 4096, 1024], P('shard', ('ctx', 'tp'))
- token_gradient: float32 [4, 4096, 1024], P('shard', ('ctx', 'tp'))
- query_gradient: float32 [1024, 1024], P(('shard', 'ctx'), 'tp')
- key_gradient: float32 [1024, 512], P(('shard', 'ctx'), 'tp')
- value_gradient: float32 [1024, 512], P(('shard', 'ctx'), 'tp')
- output_gradient: float32 [1024, 1024], P('tp', ('shard', 'ctx'))
- gate_gradient: float32 [1024, 4608], P(('shard', 'ctx'), 'tp')
- up_gradient: float32 [1024, 4608], P(('shard', 'ctx'), 'tp')
- down_gradient: float32 [4608, 1024], P('tp', ('shard', 'ctx'))
- first_gain_gradient: float32 [1024], replicated
- second_gain_gradient: float32 [1024], replicated
- query_gain_gradient: float32 [64], replicated
- key_gain_gradient: float32 [64], replicated
The draws below stay inside these ranges and needn't reach their ends.
Inputs may be any that keep to these rules, and one draw needn't show every extreme that they name: `positions`: along each sequence a position exceeds the one before it by 1 to 3; the first is at most 2.
All inputs are finite; a program needn't handle non-finite values.
Results may differ from the reference program's by a relative error of at most 0.02.
Values may be sent and summed in bfloat16 or wider, within the bound.
No kernel may reach another device: no remote copies, remote signals or barrier semaphores. Data moves between devices by JAX's collectives and lax.ppermute only.
A program may use at most 192 MiB of HBM per device.

```python
import math
import jax
import jax.numpy as jnp
from jax import lax

D = 1024
HEADS = 16
KV_HEADS = 8
HEAD_DIM = 64
FF = 4608
LEN = 4096
SEQS = 4


def draw_positions(key, part):
    steps = jax.random.randint(key, (SEQS, LEN), 1, 4).astype(jnp.int32)
    rising = jnp.cumsum(steps, axis=1).astype(jnp.int32)
    started = (rising - steps[:, :1]).astype(jnp.int32)
    widest = (3 * jnp.arange(LEN, dtype=jnp.int32) + 2).astype(jnp.int32)
    rows = jnp.arange(SEQS, dtype=jnp.int32)[:, None]
    return jnp.where(rows == 0, widest[None, :], started).astype(jnp.int32)


def levels(rng, shape, shards, low, high):
    factor_of, own = 1.0, jax.random.fold_in(rng, 6)
    for position, parts in shards:
        draws = jnp.exp(jax.random.uniform(jax.random.fold_in(own, position), (parts,), jnp.float32, low / len(shards), high / len(shards)))
        factor_of = factor_of * jnp.repeat(draws, shape[position] // parts).reshape([-1 if axis == position else 1 for axis in range(len(shape))])
    return factor_of


def noise(own_key, shape, scale, most, split=(), kind=jnp.bfloat16):
    factor_of = levels(own_key, shape, split, -0.22, 0.18) if split else 1.0
    entries = jax.random.normal(own_key, shape, jnp.float32) * scale * factor_of
    return jnp.minimum(jnp.maximum(entries, -most), most).astype(kind)


def setup_inputs(seed: int = 0) -> dict:
    seeds = jax.random.split(jax.random.key(seed), 15)
    return {
        "tokens": noise(seeds[0], (SEQS, LEN, D), 1.0, 6.0, ((0, 2), (1, 16))),
        "positions": draw_positions(jax.random.fold_in(seeds[14], 71), 0),
        "first_gain": jnp.clip(1.0 + 0.1 * jax.random.normal(seeds[2], (D,), jnp.float32), 0.5, 1.5),
        "query_weight": noise(seeds[3], (D, HEADS * HEAD_DIM), D ** -0.5, 0.1875, ((0, 8), (1, 4))),
        "key_weight": noise(seeds[4], (D, KV_HEADS * HEAD_DIM), D ** -0.5, 0.1875, ((0, 8), (1, 4))),
        "value_weight": noise(seeds[5], (D, KV_HEADS * HEAD_DIM), D ** -0.5, 0.1875, ((0, 8), (1, 4))),
        "query_gain": jnp.clip(1.0 + 0.18 * jax.random.normal(seeds[6], (HEAD_DIM,), jnp.float32), 0.1, 1.9),
        "key_gain": jnp.clip(1.0 + 0.18 * jax.random.normal(seeds[7], (HEAD_DIM,), jnp.float32), 0.1, 1.9),
        "output_weight": noise(seeds[8], (HEADS * HEAD_DIM, D), (HEADS * HEAD_DIM // 32) ** -0.5, 1.0, ((0, 4), (1, 8))),
        "second_gain": jnp.clip(1.0 + 0.1 * jax.random.normal(seeds[9], (D,), jnp.float32), 0.5, 1.5),
        "gate_weight": noise(seeds[10], (D, FF), D ** -0.5, 0.1875, ((0, 8), (1, 4))),
        "up_weight": noise(seeds[11], (D, FF), D ** -0.5, 0.1875, ((0, 8), (1, 4))),
        "down_weight": noise(seeds[12], (FF, D), FF ** -0.5, 0.09375, ((0, 4), (1, 8))),
        "upstream": noise(seeds[13], (SEQS, LEN, D), 1.0, 6.0, ((0, 2), (1, 16))),
    }


EPS = 1e-05
THETA = 1000000.0
NEGATIVE = -1e+30

@jax.custom_vjp
def low(v):
    return lax.optimization_barrier(v.astype(jnp.bfloat16)).astype(jnp.float32)

@jax.custom_vjp
def low_back(v):
    return v

def low_keep(v):
    return (low(v), None)

def low_pass(kept, grad):
    return (grad,)

def back_keep(v):
    return (v, None)

def back_low(kept, grad):
    return (low(grad),)
low.defvjp(low_keep, low_pass)
low_back.defvjp(back_keep, back_low)

def product(left, right):
    return jnp.dot(left, right, precision=lax.Precision.HIGHEST, preferred_element_type=jnp.float32)

def norm_rows(values, gain):
    return values * lax.rsqrt(lax.optimization_barrier(jnp.mean(values * values, axis=-1, keepdims=True)) + EPS) * gain

def rotary_tables(places, width):
    freqs = jnp.exp(-math.log(THETA) * jnp.arange(0, width, 2).astype(jnp.float32) / width)
    angles = places.astype(jnp.float32)[:, None] * freqs[None, :]
    cosine = jnp.concatenate([jnp.cos(angles), jnp.cos(angles)], axis=-1)[:, None, :]
    sine = jnp.concatenate([jnp.sin(angles), jnp.sin(angles)], axis=-1)[:, None, :]
    return (cosine, sine)

def shape_heads(raw, gain, cosine, sine):
    normed = norm_rows(raw, gain)
    half = normed.shape[-1] // 2
    turned = jnp.concatenate([-normed[..., half:], normed[..., :half]], axis=-1)
    return normed * cosine + turned * sine

def reference(tokens, positions, first_gain, query_weight, key_weight, value_weight, query_gain, key_gain, output_weight, second_gain, gate_weight, up_weight, down_weight, upstream):
    params = (first_gain.astype(jnp.float32), query_weight.astype(jnp.float32), key_weight.astype(jnp.float32), value_weight.astype(jnp.float32), query_gain.astype(jnp.float32), key_gain.astype(jnp.float32), output_weight.astype(jnp.float32), second_gain.astype(jnp.float32), gate_weight.astype(jnp.float32), up_weight.astype(jnp.float32), down_weight.astype(jnp.float32))
    block = min(512, LEN)
    count = LEN // block
    group = HEADS // KV_HEADS
    scale = 1.0 / math.sqrt(HEAD_DIM)

    def per_sequence(carry, inputs):
        token_rows, places, cotangent = inputs
        cosine, sine = rotary_tables(places, HEAD_DIM)

        def forward(xrows, g_first, w_query, w_key, w_value, g_query, g_key, w_output, g_second, w_gate, w_up, w_down):
            first = low(norm_rows(xrows, g_first))
            query_raw = low_back(product(first, w_query)).reshape(LEN, HEADS, HEAD_DIM)
            key_raw = low_back(product(first, w_key)).reshape(LEN, KV_HEADS, HEAD_DIM)
            value = low(low_back(product(first, w_value))).reshape(LEN, KV_HEADS, HEAD_DIM)
            query = low(shape_heads(query_raw, g_query, cosine, sine))
            key = low(shape_heads(key_raw, g_key, cosine, sine))
            keys_wide = jnp.repeat(key, group, axis=1)
            values_wide = jnp.repeat(value, group, axis=1)

            def attend_pair(pair):
                query_block, start = pair
                scores = jnp.einsum('qhd,khd->hqk', query_block, keys_wide, precision=lax.Precision.HIGHEST) * scale
                scores = low_back(scores)
                allowed = jnp.arange(LEN, dtype=jnp.int32)[None, :] <= (start + jnp.arange(block, dtype=jnp.int32))[:, None]
                masked = jnp.where(allowed[None], scores, NEGATIVE)
                probs = low(jax.nn.softmax(masked, axis=-1))
                return jnp.einsum('hqk,khd->qhd', probs, values_wide, precision=lax.Precision.HIGHEST)
            starts = jnp.arange(count, dtype=jnp.int32) * block
            outputs = lax.map(jax.checkpoint(attend_pair), (query.reshape(count, block, HEADS, HEAD_DIM), starts))
            mixed = low(low_back(outputs.reshape(LEN, HEADS * HEAD_DIM)))
            middle = xrows + low_back(product(mixed, w_output))
            second = low(norm_rows(middle, g_second))
            gate = low_back(product(second, w_gate))
            up = low_back(product(second, w_up))
            hidden = low(jax.nn.silu(gate) * up)
            return middle + low_back(product(hidden, w_down))
        result, pullback = jax.vjp(forward, token_rows.astype(jnp.float32), *params)
        grads = pullback(cotangent.astype(jnp.float32))
        carry = jax.tree.map(jnp.add, carry, tuple(grads[1:]))
        return (carry, (result.astype(jnp.bfloat16), grads[0]))
    zeros = tuple((jnp.zeros(p.shape, jnp.float32) for p in params))
    totals, (block_output, token_gradient) = lax.scan(per_sequence, zeros, (tokens, positions, upstream))
    return (block_output, token_gradient, totals[1], totals[2], totals[3], totals[6], totals[8], totals[9], totals[10], totals[0], totals[7], totals[4], totals[5])
```

```python
import functools
import math

import jax
import jax.numpy as jnp
from jax import lax
from jax.experimental import pallas as pl
from jax.experimental.pallas import tpu as pltpu
from jax.sharding import PartitionSpec as P

EPS = 1e-05
THETA = 1000000.0
LOG2E = 1.4426950408889634
F32 = jnp.float32
BF16 = jnp.bfloat16
NEAR = [(0, 1), (1, 0), (2, 3), (3, 2)]
FAR = [(0, 2), (2, 0), (1, 3), (3, 1)]
LIMIT = 56 * 1024 * 1024


def dot_nn(left, right):
    return lax.dot_general(left, right, (((1,), (0,)), ((), ())), preferred_element_type=F32)


def dot_nt(left, right):
    return lax.dot_general(left, right, (((1,), (1,)), ((), ())), preferred_element_type=F32)


def dot_tn(left, right):
    return lax.dot_general(left, right, (((0,), (0,)), ((), ())), preferred_element_type=F32)


def swap_bits(j):
    return ((j & 1) << 1) | (j >> 1)


def gather_ctx(own):
    far = lax.ppermute(own, "ctx", FAR)
    near = lax.ppermute(own, "ctx", NEAR)
    both = lax.ppermute(far, "ctx", NEAR)
    return jnp.stack([own, far, near, both])


def reduce_ctx(parts):
    got = lax.ppermute(parts[2:], "ctx", NEAR)
    mine = parts[0].astype(F32) + got[0].astype(F32)
    away = (parts[1].astype(F32) + got[1].astype(F32)).astype(BF16)
    return mine + lax.ppermute(away, "ctx", FAR).astype(F32)


def gather_tp(own, count):
    up = [(i, i + 1) for i in range(count - 1)]
    down = [(i + 1, i) for i in range(count - 1)]
    from_low, from_high = [], []
    low = high = own
    for _ in range(count - 1):
        low = lax.ppermute(low, "tp", up)
        high = lax.ppermute(high, "tp", down)
        from_low.append(low)
        from_high.append(high)
    index = lax.axis_index("tp")
    slots = [own]
    for i in range(1, count):
        slots.append(jnp.where(index >= i, from_low[i - 1], from_high[count - i - 1]))
    return jnp.stack(slots)


def reduce_tp(parts, count):
    up = [(i, i + 1) for i in range(count - 1)]
    down = [(i + 1, i) for i in range(count - 1)]
    going_up = going_down = None
    for k in range(count - 1, 0, -1):
        high, low = parts[count - k], parts[k]
        if going_up is not None:
            high = (high.astype(F32) + going_up.astype(F32)).astype(BF16)
            low = (low.astype(F32) + going_down.astype(F32)).astype(BF16)
        going_up = lax.ppermute(high, "tp", up)
        going_down = lax.ppermute(low, "tp", down)
    return parts[0].astype(F32) + going_up.astype(F32) + going_down.astype(F32)


def sum_all(vector, sizes):
    for name, size in sizes:
        step = 1
        while step < size:
            other = lax.ppermute(vector, name, [(i, i ^ step) for i in range(size)])
            vector = vector + other
            step *= 2
    return vector


def params():
    return pltpu.CompilerParams(vmem_limit_bytes=LIMIT)


def head_sums(values):
    rows = lax.broadcasted_iota(jnp.int32, (128, 128), 0) >> 6
    columns = lax.broadcasted_iota(jnp.int32, (128, 128), 1) >> 6
    ones = jnp.where(rows == columns, 1.0, 0.0).astype(BF16)
    high = values.astype(BF16)
    rest = values - high.astype(F32)
    low = rest.astype(BF16)
    return dot_nn(high, ones) + dot_nn(low, ones)


def pad_heads(pair, low):
    zero = jnp.zeros_like(pair)
    return jnp.where(low, pair, zero), jnp.where(low, pltpu.roll(pair, 64, 1), zero)


def pad_heads_high(pair, low):
    zero = jnp.zeros_like(pair)
    return jnp.where(low, zero, pltpu.roll(pair, 64, 1)), jnp.where(low, zero, pair)


def pad_four(first, second, low):
    a, b = pad_heads(first, low)
    c, d = pad_heads_high(second, low)
    return a, b, c, d


def join_four(values, rows, low):
    a, b, c, d = (values[h * rows : (h + 1) * rows] for h in range(4))
    return jnp.where(low, a, pltpu.roll(b, 64, 1)), jnp.where(low, pltpu.roll(c, 64, 1), d)


def qkv_kernel(x_ref, w_ref, cos_ref, sin_ref, gain_ref, q_ref, kv_ref, raw_ref):
    rows = x_ref.shape[1]
    y = dot_nn(x_ref[0], w_ref[:, :512])
    raw_ref[0] = y[:, :384]
    lane = lax.broadcasted_iota(jnp.int32, (rows, 128), 1)
    early, low = (lane & 32) == 0, lane < 64
    cosine, sine = cos_ref[0], sin_ref[0]
    turned = []
    for b in range(3):
        u = y[:, b * 128 : (b + 1) * 128]
        r = lax.rsqrt(head_sums(u * u) * (1.0 / 64.0) + EPS)
        n = u * r * gain_ref[:, b * 128 : (b + 1) * 128]
        other = jnp.where(early, -pltpu.roll(n, 96, 1), pltpu.roll(n, 32, 1))
        turned.append(n * cosine + other * sine)
    heads = pad_four(turned[0] * 0.125, turned[1] * 0.125, low)
    for h in range(4):
        q_ref[0, h] = heads[h].astype(BF16)
    kv_ref[0, :, 0:128] = turned[2].astype(BF16)
    kv_ref[0, :, 128:256] = y[:, 384:512].astype(BF16)


def qkv_call(x, w, cosine, sine, gains):
    slots, rows, width = x.shape
    return pl.pallas_call(
        qkv_kernel,
        grid=(slots,),
        in_specs=[
            pl.BlockSpec((1, rows, width), lambda j: (j, 0, 0)),
            pl.BlockSpec(w.shape, lambda j: (0, 0)),
            pl.BlockSpec((1, rows, 128), lambda j: (j, 0, 0)),
            pl.BlockSpec((1, rows, 128), lambda j: (j, 0, 0)),
            pl.BlockSpec((1, 384), lambda j: (0, 0)),
        ],
        out_specs=[
            pl.BlockSpec((1, 4, rows, 128), lambda j: (j, 0, 0, 0)),
            pl.BlockSpec((1, rows, 256), lambda j: (j, 0, 0)),
            pl.BlockSpec((1, rows, 384), lambda j: (j, 0, 0)),
        ],
        out_shape=[
            jax.ShapeDtypeStruct((slots, 4, rows, 128), BF16),
            jax.ShapeDtypeStruct((slots, rows, 256), BF16),
            jax.ShapeDtypeStruct((slots, rows, 384), F32),
        ],
        compiler_params=params(),
        name="qkv",
    )(x, w, cosine, sine, gains)


def slot_of(n, c, t):
    return (t - (n & 3)) & 3, swap_bits(c ^ (n >> 2))


def attend_kernel(place_ref, q_ref, kv_ref, w_ref, o_ref, lse_ref, mixed_ref, part_ref, acc_ref, sum_ref):
    c, t, j = place_ref[0], place_ref[1], pl.program_id(0)
    rows = q_ref.shape[2]
    wide = 4 * rows
    queries = q_ref[0].reshape(wide, 128)
    acc_ref[...] = jnp.zeros_like(acc_ref)
    sum_ref[...] = jnp.zeros_like(sum_ref)

    def scores(n):
        i, jj = slot_of(n, c, t)
        keys = kv_ref[i, jj, :, 0:128]
        values = kv_ref[i, jj, :, 128:256]
        return jnp.exp2(dot_nt(keys, queries) * LOG2E), values

    def add(weights, values):
        sum_ref[...] += jnp.sum(weights, axis=0, keepdims=True)
        acc_ref[...] += dot_tn(values, weights.astype(BF16))

    last = 4 * (c ^ swap_bits(j)) + t

    def body(n, carry):
        add(*scores(n))
        return carry

    lax.fori_loop(0, last, body, 0)
    weights, values = scores(last)
    key = lax.broadcasted_iota(jnp.int32, (rows, wide), 0)
    query = lax.broadcasted_iota(jnp.int32, (rows, wide), 1) & (rows - 1)
    add(jnp.where(key <= query, weights, 0.0), values)
    total = sum_ref[...]
    out = acc_ref[...] / total
    o_ref[0] = out
    lse_ref[0] = jnp.log(total) * LOG2E
    low = lax.broadcasted_iota(jnp.int32, (rows, 128), 1) < 64
    first, second = join_four(jnp.transpose(out), rows, low)
    mixed = jnp.concatenate([first, second], axis=1).astype(BF16)
    mixed_ref[0] = mixed
    part_ref[0] = dot_nt(mixed, w_ref[:, 512:768]).astype(BF16)


def attend_call(place, q, kv, w):
    slots, _, rows, _ = q.shape
    width = w.shape[0]
    return pl.pallas_call(
        attend_kernel,
        grid=(slots,),
        in_specs=[
            pl.BlockSpec(memory_space=pltpu.SMEM),
            pl.BlockSpec((1, 4, rows, 128), lambda j: (j, 0, 0, 0)),
            pl.BlockSpec(kv.shape, lambda j: (0, 0, 0, 0)),
            pl.BlockSpec(w.shape, lambda j: (0, 0)),
        ],
        out_specs=[
            pl.BlockSpec((1, 128, 4 * rows), lambda j: (j, 0, 0)),
            pl.BlockSpec((1, 1, 4 * rows), lambda j: (j, 0, 0)),
            pl.BlockSpec((1, rows, 256), lambda j: (j, 0, 0)),
            pl.BlockSpec((1, rows, width), lambda j: (j, 0, 0)),
        ],
        out_shape=[
            jax.ShapeDtypeStruct((slots, 128, 4 * rows), F32),
            jax.ShapeDtypeStruct((slots, 1, 4 * rows), F32),
            jax.ShapeDtypeStruct((slots, rows, 256), BF16),
            jax.ShapeDtypeStruct((slots, rows, width), BF16),
        ],
        scratch_shapes=[pltpu.VMEM((128, 4 * rows), F32), pltpu.VMEM((1, 4 * rows), F32)],
        compiler_params=params(),
        name="attend",
    )(place, q, kv, w)


def attend_back_kernel(
    place_ref, q_ref, kv_ref, w_ref, o_ref, lse_ref, back_ref, dq_ref, dkv_ref, dk_ref, dv_ref, acc_ref
):
    c, t, j = place_ref[0], place_ref[1], pl.program_id(0)
    rows = q_ref.shape[2]
    wide = 4 * rows

    @pl.when(j == 0)
    def _():
        dk_ref[...] = jnp.zeros_like(dk_ref)
        dv_ref[...] = jnp.zeros_like(dv_ref)

    queries = q_ref[0].reshape(wide, 128)
    low = lax.broadcasted_iota(jnp.int32, (rows, 128), 1) < 64
    flat = dot_nn(back_ref[0], w_ref[:, 512:768])
    wide_back = jnp.concatenate(pad_four(flat[:, 0:128], flat[:, 128:256], low), axis=0).astype(BF16)
    delta = jnp.sum(jnp.transpose(wide_back.astype(F32)) * o_ref[0], axis=0, keepdims=True)
    lse = lse_ref[0]
    acc_ref[...] = jnp.zeros_like(acc_ref)

    def block(n, allowed):
        i, jj = slot_of(n, c, t)
        keys = kv_ref[i, jj, :, 0:128]
        values = kv_ref[i, jj, :, 128:256]
        probs = jnp.exp2(dot_nt(keys, queries) * LOG2E - lse)
        if allowed is not None:
            probs = jnp.where(allowed, probs, 0.0)
        slopes = dot_nt(values, wide_back)
        score_back = (probs * (slopes - delta)).astype(BF16)
        dv_ref[i, jj] += dot_nn(probs.astype(BF16), wide_back)
        dk_ref[i, jj] += dot_nn(score_back, queries)
        acc_ref[...] += dot_tn(score_back, keys)

    last = 4 * (c ^ swap_bits(j)) + t

    def body(n, carry):
        block(n, None)
        return carry

    lax.fori_loop(0, last, body, 0)
    key = lax.broadcasted_iota(jnp.int32, (rows, wide), 0)
    query = lax.broadcasted_iota(jnp.int32, (rows, wide), 1) & (rows - 1)
    block(last, key <= query)
    first, second = join_four(acc_ref[...] * 0.125, rows, low)
    dq_ref[0, :, 0:128] = first
    dq_ref[0, :, 128:256] = second

    @pl.when(j == pl.num_programs(0) - 1)
    def _():
        dkv_ref[:, :, :, 0:128] = dk_ref[...].astype(BF16)
        dkv_ref[:, :, :, 128:256] = dv_ref[...].astype(BF16)


def attend_back_call(place, q, kv, w, o, lse, back):
    slots, _, rows, _ = q.shape
    width = w.shape[0]
    return pl.pallas_call(
        attend_back_kernel,
        grid=(slots,),
        in_specs=[
            pl.BlockSpec(memory_space=pltpu.SMEM),
            pl.BlockSpec((1, 4, rows, 128), lambda j: (j, 0, 0, 0)),
            pl.BlockSpec(kv.shape, lambda j: (0, 0, 0, 0)),
            pl.BlockSpec(w.shape, lambda j: (0, 0)),
            pl.BlockSpec((1, 128, 4 * rows), lambda j: (j, 0, 0)),
            pl.BlockSpec((1, 1, 4 * rows), lambda j: (j, 0, 0)),
            pl.BlockSpec((1, rows, width), lambda j: (j, 0, 0)),
        ],
        out_specs=[
            pl.BlockSpec((1, rows, 256), lambda j: (j, 0, 0)),
            pl.BlockSpec(kv.shape, lambda j: (0, 0, 0, 0)),
        ],
        out_shape=[
            jax.ShapeDtypeStruct((slots, rows, 256), F32),
            jax.ShapeDtypeStruct(kv.shape, BF16),
        ],
        scratch_shapes=[
            pltpu.VMEM((*kv.shape[:3], 128), F32),
            pltpu.VMEM((*kv.shape[:3], 128), F32),
            pltpu.VMEM((4 * rows, 128), F32),
        ],
        compiler_params=params(),
        name="attend_back",
    )(place, q, kv, w, o, lse, back)


def qkv_back_kernel(dq_ref, dkv_ref, raw_ref, cos_ref, sin_ref, gain_ref, w_ref, back_ref, part_ref, share_ref):
    rows = dq_ref.shape[1]
    lane = lax.broadcasted_iota(jnp.int32, (rows, 128), 1)
    early = (lane & 32) == 0
    cosine, sine = cos_ref[0], sin_ref[0]

    @pl.when(pl.program_id(0) == 0)
    def _():
        share_ref[...] = jnp.zeros_like(share_ref)

    outs = []
    for b in range(3):
        given = dq_ref[0, :, b * 128 : (b + 1) * 128] if b < 2 else dkv_ref[0, :, 0:128]
        z = sine * given
        cotangent = given * cosine + jnp.where(early, pltpu.roll(z, 96, 1), -pltpu.roll(z, 32, 1))
        u = raw_ref[0, :, b * 128 : (b + 1) * 128]
        gain = gain_ref[:, b * 128 : (b + 1) * 128]
        r = lax.rsqrt(head_sums(u * u) * (1.0 / 64.0) + EPS)
        mean = head_sums(u * gain * cotangent) * (1.0 / 64.0)
        share_ref[:, b * 128 : (b + 1) * 128] += jnp.sum(cotangent * u * r, axis=0, keepdims=True)
        outs.append((r * gain * cotangent - u * (r * r * r) * mean).astype(BF16))
    outs.append(dkv_ref[0, :, 128:256].astype(BF16))
    back = jnp.concatenate(outs, axis=1)
    back_ref[0] = back
    part_ref[0] = dot_nt(back, w_ref[:, :512]).astype(BF16)


def qkv_back_call(dq, dkv, raw, cosine, sine, gains, w):
    slots, rows, _ = dq.shape
    width = w.shape[0]
    return pl.pallas_call(
        qkv_back_kernel,
        grid=(slots,),
        in_specs=[
            pl.BlockSpec((1, rows, 256), lambda j: (j, 0, 0)),
            pl.BlockSpec((1, rows, 256), lambda j: (j, 0, 0)),
            pl.BlockSpec((1, rows, 384), lambda j: (j, 0, 0)),
            pl.BlockSpec((1, rows, 128), lambda j: (j, 0, 0)),
            pl.BlockSpec((1, rows, 128), lambda j: (j, 0, 0)),
            pl.BlockSpec((1, 384), lambda j: (0, 0)),
            pl.BlockSpec(w.shape, lambda j: (0, 0)),
        ],
        out_specs=[
            pl.BlockSpec((1, rows, 512), lambda j: (j, 0, 0)),
            pl.BlockSpec((1, rows, width), lambda j: (j, 0, 0)),
            pl.BlockSpec((1, 384), lambda j: (0, 0)),
        ],
        out_shape=[
            jax.ShapeDtypeStruct((slots, rows, 512), BF16),
            jax.ShapeDtypeStruct((slots, rows, width), BF16),
            jax.ShapeDtypeStruct((1, 384), F32),
        ],
        compiler_params=params(),
        name="qkv_back",
    )(dq, dkv, raw, cosine, sine, gains, w)


def ffn_kernel(x_ref, up_ref, w_ref, hidden_ref, gate_back_ref, up_back_ref, part_ref, back_ref):
    slots, rows, width = x_ref.shape
    count = slots * rows
    x = x_ref[...].reshape(count, width)
    given = up_ref[...].reshape(count, width)
    gate = dot_nt(x, w_ref[0])
    up = dot_nt(x, w_ref[1])
    sig = jax.nn.sigmoid(gate)
    swish = gate * sig
    hidden = (swish * up).astype(BF16)
    hidden_ref[...] = hidden.reshape(hidden_ref.shape)
    part_ref[...] = dot_nn(hidden, w_ref[2]).astype(BF16).reshape(part_ref.shape)
    hidden_back = dot_nt(given, w_ref[2])
    gate_back = (hidden_back * up * (sig * (1.0 + gate * (1.0 - sig)))).astype(BF16)
    up_back = (hidden_back * swish).astype(BF16)
    gate_back_ref[...] = gate_back.reshape(gate_back_ref.shape)
    up_back_ref[...] = up_back.reshape(up_back_ref.shape)
    back = dot_nn(gate_back, w_ref[0]) + dot_nn(up_back, w_ref[1])
    back_ref[...] = back.astype(BF16).reshape(back_ref.shape)


def ffn_call(x, given, w):
    slots, rows, width = x.shape
    hidden = w.shape[1]
    step = 2
    token = pl.BlockSpec((step, rows, width), lambda j: (j, 0, 0))
    unit = pl.BlockSpec((step, rows, hidden), lambda j: (j, 0, 0))
    return pl.pallas_call(
        ffn_kernel,
        grid=(slots // step,),
        in_specs=[token, token, pl.BlockSpec(w.shape, lambda j: (0, 0, 0), pipeline_mode=pl.Buffered(1))],
        out_specs=[unit, unit, unit, token, token],
        out_shape=[jax.ShapeDtypeStruct((slots, rows, hidden), BF16)] * 3
        + [jax.ShapeDtypeStruct((slots, rows, width), BF16)] * 2,
        compiler_params=params(),
        name="ffn",
    )(x, given, w)


def inverse_root(values):
    return lax.rsqrt(jnp.mean(values * values, axis=-1, keepdims=True) + EPS)


def norm_back(values, root, gain, given):
    mean = jnp.mean(values * gain * given, axis=-1, keepdims=True)
    return root * gain * given - values * (root * root * root) * mean


def per_device(
    sizes,
    tokens,
    positions,
    first_gain,
    query_weight,
    key_weight,
    value_weight,
    query_gain,
    key_gain,
    output_weight,
    second_gain,
    gate_weight,
    up_weight,
    down_weight,
    upstream,
):
    shards, ctx, tp = sizes["shard"], sizes["ctx"], sizes["tp"]
    groups = ("shard", "tp")
    sequences, rows, width = tokens.shape
    head_dim = query_gain.shape[0]
    depth = query_weight.shape[0]
    units = gate_weight.shape[1]
    c, t = lax.axis_index("ctx"), lax.axis_index("tp")
    place = jnp.stack([c, t]).astype(jnp.int32)
    trade = [(i * tp + k, k * ctx + i) for i in range(ctx) for k in range(tp)]

    small = jnp.concatenate([query_weight, key_weight, value_weight, output_weight.T], axis=1)
    small = lax.ppermute(small, ("ctx", "tp"), trade)
    w_attn = lax.all_gather(small, groups, axis=0, tiled=True)

    large = jnp.stack([gate_weight.T, up_weight.T, down_weight]).reshape(3, ctx, units // ctx, depth)
    large = lax.all_to_all(large, "ctx", 1, 1, tiled=True)
    large = large.transpose(0, 2, 1, 3).reshape(3, units // ctx, ctx * depth)
    w_ffn = lax.all_gather(large, groups, axis=0, tiled=False)
    w_ffn = w_ffn.reshape(shards, tp, 3, units // ctx, ctx * depth)
    w_ffn = w_ffn.transpose(2, 1, 3, 0, 4).reshape(3, units, width)

    mine = lax.dynamic_slice_in_dim(positions, t * rows, rows, 1).astype(F32)
    places = gather_ctx(mine)
    freqs = jnp.exp(-math.log(THETA) * jnp.arange(0, head_dim, 2).astype(F32) / head_dim)
    angles = places[..., None] * freqs
    cosine, sine = jnp.cos(angles), jnp.sin(angles)
    cosine = jnp.concatenate([cosine] * 4, axis=-1)
    sine = jnp.concatenate([sine] * 4, axis=-1)
    gains = jnp.concatenate([jnp.tile(query_gain, 4), jnp.tile(key_gain, 2)])[None]

    x = tokens.astype(F32)
    root = inverse_root(x)
    first = (x * root * first_gain).astype(BF16)
    given = upstream.astype(F32)

    first_all = [gather_ctx(first[s]) for s in range(sequences)]
    q, kv, raw = [], [], []
    for s in range(sequences):
        one = qkv_call(first_all[s], w_attn, cosine[:, s], sine[:, s], gains)
        q.append(one[0])
        kv.append(gather_tp(one[1], tp))
        raw.append(one[2])
    upstream_all = [gather_ctx(upstream[s]) for s in range(sequences)]
    attended = [attend_call(place, q[s], kv[s], w_attn) for s in range(sequences)]
    results, second_share, back_rows, mixed_back_all = [], 0.0, [], []
    seconds, ffn = [], []
    for s in range(sequences):
        middle = x[s] + reduce_ctx(attended[s][3])
        middle_root = inverse_root(middle)
        second = (middle * middle_root * second_gain).astype(BF16)
        second_all = gather_ctx(second)
        seconds.append(second_all)
        hidden, gate_back, up_back, part, back_part = ffn_call(second_all, upstream_all[s], w_ffn)
        ffn.append((hidden, gate_back, up_back))
        second_back = reduce_ctx(back_part)
        middle_back = given[s] + norm_back(middle, middle_root, second_gain, second_back)
        second_share = second_share + jnp.sum(second_back * middle * middle_root, axis=0)
        back_rows.append(middle_back)
        mixed_back_all.append(gather_ctx(middle_back.astype(BF16)))
        results.append((middle + reduce_ctx(part)).astype(BF16))

    flat = lambda v: v.reshape(-1, v.shape[-1])
    grads = []
    for left, right in ((1, seconds), (2, seconds), (0, upstream_all)):
        total = 0.0
        for s in range(sequences):
            total = total + dot_tn(flat(ffn[s][left]), flat(right[s]))
        grads.append(total.astype(BF16))
    g_ffn = jnp.stack(grads).reshape(3, tp, units // ctx, shards, ctx * depth)
    g_ffn = g_ffn.transpose(3, 1, 0, 2, 4).reshape(shards * tp * 3, units // ctx, ctx * depth)
    g_ffn = lax.psum_scatter(g_ffn, groups, scatter_dimension=0, tiled=True)
    g_ffn = g_ffn.reshape(3, units // ctx, ctx, depth).transpose(0, 2, 1, 3)
    g_ffn = lax.all_to_all(g_ffn, "ctx", 1, 1, tiled=True)
    g_ffn = g_ffn.reshape(3, units, depth).astype(F32)

    gradients, first_share, head_share = [], 0.0, 0.0
    g_out, g_qkv = 0.0, 0.0
    for s in range(sequences):
        o, lse, mixed, _ = attended[s]
        dq, dkv = attend_back_call(place, q[s], kv[s], w_attn, o, lse, mixed_back_all[s])
        g_out = g_out + dot_tn(flat(mixed_back_all[s]), flat(mixed))
        dkv = reduce_tp(dkv, tp)
        back, part, share = qkv_back_call(dq, dkv, raw[s], cosine[:, s], sine[:, s], gains, w_attn)
        head_share = head_share + share
        g_qkv = g_qkv + dot_tn(flat(first_all[s]), flat(back))
        first_back = reduce_ctx(part)
        gradients.append(back_rows[s] + norm_back(x[s], root[s], first_gain, first_back))
        first_share = first_share + jnp.sum(first_back * x[s] * root[s], axis=0)

    g_attn = jnp.concatenate([g_qkv, g_out], axis=1).astype(BF16)
    g_attn = lax.psum_scatter(g_attn, groups, scatter_dimension=0, tiled=True)
    g_attn = lax.ppermute(g_attn, ("ctx", "tp"), trade).astype(F32)
    heads = query_weight.shape[1]
    pairs = key_weight.shape[1]

    shares = jnp.concatenate([first_share, second_share, head_share[0]])
    shares = sum_all(shares, [(name, sizes[name]) for name in ("ctx", "shard", "tp")])
    head_total = shares[2 * width :]
    return (
        jnp.stack(results),
        jnp.stack(gradients),
        g_attn[:, :heads],
        g_attn[:, heads : heads + pairs],
        g_attn[:, heads + pairs : heads + 2 * pairs],
        g_attn[:, heads + 2 * pairs :].T,
        g_ffn[0].T,
        g_ffn[1].T,
        g_ffn[2],
        shares[:width],
        shares[width : 2 * width],
        jnp.sum(head_total[: 4 * head_dim].reshape(4, head_dim), axis=0),
        jnp.sum(head_total[4 * head_dim :].reshape(2, head_dim), axis=0),
    )


def solution(mesh):
    rows = P("shard", ("ctx", "tp"), None)
    wide = P(("shard", "ctx"), "tp")
    tall = P("tp", ("shard", "ctx"))
    none = P()
    in_specs = (
        rows, P("shard", "ctx"), none, wide, wide, wide, none, none, tall, none, wide, wide, tall, rows,
    )
    out_specs = (rows, rows, wide, wide, wide, tall, wide, wide, tall, none, none, none, none)
    sizes = {name: mesh.shape[name] for name in ("shard", "ctx", "tp")}
    return jax.shard_map(
        functools.partial(per_device, sizes), mesh=mesh, in_specs=in_specs, out_specs=out_specs, check_vma=False
    )
```

```python
import functools
import math

import jax
import jax.numpy as jnp
from jax import lax
from jax.experimental import pallas as pl
from jax.experimental.pallas import tpu as pltpu
from jax.sharding import PartitionSpec as P

EPS = 1e-05
THETA = 1000000.0
LOG2E = 1.4426950408889634
F32 = jnp.float32
BF16 = jnp.bfloat16
NEAR = [(0, 1), (1, 0), (2, 3), (3, 2)]
FAR = [(0, 2), (2, 0), (1, 3), (3, 1)]
CROSS = [(0, 3), (3, 0), (1, 2), (2, 1)]
LIMIT = 56 * 1024 * 1024


def dot_nn(left, right):
    return lax.dot_general(left, right, (((1,), (0,)), ((), ())), preferred_element_type=F32)


def dot_nt(left, right):
    return lax.dot_general(left, right, (((1,), (1,)), ((), ())), preferred_element_type=F32)


def dot_tn(left, right):
    return lax.dot_general(left, right, (((0,), (0,)), ((), ())), preferred_element_type=F32)


def swap_bits(j):
    return ((j & 1) << 1) | (j >> 1)


def gather_ctx(own):
    far = lax.ppermute(own, "ctx", FAR)
    near = lax.ppermute(own, "ctx", NEAR)
    return [own, far, near, lax.ppermute(far, "ctx", NEAR)]


def add_near(own, got):
    return own[0].astype(F32) + got[0].astype(F32), (own[1].astype(F32) + got[1].astype(F32)).astype(BF16)


def reduce_near(own, near):
    return add_near(own, lax.ppermute(near, "ctx", NEAR))


def reduce_far(mine, away):
    return mine + lax.ppermute(away, "ctx", FAR).astype(F32)


def reduce_ctx(own, near):
    got = lax.ppermute(own[1], "ctx", FAR), lax.ppermute(near[0], "ctx", NEAR), lax.ppermute(near[1], "ctx", CROSS)
    return own[0].astype(F32) + got[0].astype(F32) + got[1].astype(F32) + got[2].astype(F32)


def to_tp(value, e):
    return lax.ppermute(value, "tp", [(i, i ^ e) for i in range(4)])


def exchange_tp(blocks):
    return [blocks[0]] + [to_tp(blocks[e], e) for e in range(1, len(blocks))]


def exchange_heads(q_same, q_other, kv):
    return [q_same, to_tp(q_other, 1), kv[0], to_tp(kv[1], 1), to_tp(kv[2], 2), to_tp(kv[3], 3)]


def gather_shard(own, shards):
    if shards == 2:
        return [own, lax.ppermute(own, "shard", [(0, 1), (1, 0)])]
    every = lax.all_gather(own, "shard", axis=0, tiled=False)
    return [every.transpose(1, 2, 0, 3).reshape(*own.shape[:2], -1)]


def send_shard(parts, shards):
    if shards == 2:
        return lax.ppermute(parts[1], "shard", [(0, 1), (1, 0)])
    blocks, units, width = parts[0].shape
    every = parts[0].reshape(blocks, units, shards, width // shards).transpose(2, 0, 1, 3)
    return lax.psum_scatter(every, "shard", scatter_dimension=0, tiled=False)


def add_shard(got, parts):
    return (parts[0].astype(F32) + got.astype(F32)).astype(BF16) if len(parts) == 2 else got


def after(value, *others):
    return lax.optimization_barrier((value, *others))[0]


class Line:
    def __init__(self):
        self.last = ()

    def run(self, call, first, *others):
        result = call(after(first, *self.last), *others)
        self.last = (jax.tree.leaves(result)[0],)
        return result


def trade_tp(own, count):
    got = [own]
    for k in range(1, count):
        got.append(lax.ppermute(own, "tp", [(i, i ^ k) for i in range(count)]))
    index = lax.axis_index("tp")
    slots = []
    for slot in range(count):
        value = got[slot]
        for at in range(1, count):
            value = jnp.where(index == at, got[slot ^ at], value)
        slots.append(value)
    return jnp.stack(slots)


def join_shard(own, shards):
    if shards == 2:
        other = lax.ppermute(own, "shard", [(0, 1), (1, 0)])
        index = lax.axis_index("shard")
        return jnp.concatenate([jnp.where(index == 0, own, other), jnp.where(index == 0, other, own)])
    return lax.all_gather(own, "shard", axis=0, tiled=True)


def sum_all(vector, sizes):
    for name, size in sizes:
        step = 1
        while step < size:
            other = lax.ppermute(vector, name, [(i, i ^ step) for i in range(size)])
            vector = vector + other
            step *= 2
    return vector


def params():
    return pltpu.CompilerParams(vmem_limit_bytes=LIMIT)


def cost(micros):
    return pl.CostEstimate(flops=int(micros * 1.0e9), transcendentals=0, bytes_accessed=int(micros * 1.0e6))


def slot_copies(refs, held, sems):
    return [pltpu.make_async_copy(ref, held.at[k], sems.at[k]) for k, ref in enumerate(refs)]


def start_slots(refs, held, sems):
    @pl.when(pl.program_id(0) == 0)
    def _():
        for copy in slot_copies(refs, held, sems):
            copy.start()


def wait_slot(refs, held, sems, step=1):
    for k, copy in enumerate(slot_copies(refs, held, sems)):

        @pl.when(pl.program_id(0) == k // step)
        def _():
            copy.wait()


def lanes_low(rows):
    return lax.broadcasted_iota(jnp.int32, (rows, 128), 1) < 64


def pack(first, second, low):
    return jnp.where(low, first, second)


def head_sums(values):
    rows = lax.broadcasted_iota(jnp.int32, (128, 128), 0) >> 6
    columns = lax.broadcasted_iota(jnp.int32, (128, 128), 1) >> 6
    ones = jnp.where(rows == columns, 1.0, 0.0).astype(BF16)
    high = values.astype(BF16)
    rest = values - high.astype(F32)
    low = rest.astype(BF16)
    return dot_nn(high, ones) + dot_nn(low, ones)


def qkv_kernel(place_ref, *refs):
    x_refs, (w_ref, cos_ref, sin_ref, gain_ref) = refs[:4], refs[4:8]
    q_same, q_other, kv_same, kv_other, raw_ref, x_ref, q_ref, kv_ref, sems = refs[8:]
    side, j = place_ref[1] & 1, pl.program_id(0)
    rows = x_ref.shape[1]
    start_slots(x_refs, x_ref, sems)
    wait_slot(x_refs, x_ref, sems)
    y = dot_nn(x_ref[j], w_ref[:, :512])
    raw_ref[0] = y[:, :384]
    low = lanes_low(rows)
    early = (lax.broadcasted_iota(jnp.int32, (rows, 128), 1) & 32) == 0
    cosine, sine = cos_ref[0, 0], sin_ref[0, 0]
    turned = []
    for b in range(3):
        u = y[:, b * 128 : (b + 1) * 128]
        r = lax.rsqrt(head_sums(u * u) * (1.0 / 64.0) + EPS)
        n = u * r * gain_ref[:, b * 128 : (b + 1) * 128]
        other = jnp.where(early, -pltpu.roll(n, 96, 1), pltpu.roll(n, 32, 1))
        turned.append(n * cosine + other * sine)
    key, value = turned[2], y[:, 384:512]
    q_ref[0] = (turned[0] * 0.125).astype(BF16)
    q_ref[1] = (turned[1] * 0.125).astype(BF16)
    kv_ref[0] = pack(key, pltpu.roll(value, 64, 1), low).astype(BF16)
    kv_ref[1] = pack(pltpu.roll(key, 64, 1), value, low).astype(BF16)
    q_same[0] = q_ref[side]
    q_other[0] = q_ref[1 - side]
    kv_same[0] = kv_ref[side]
    kv_other[0] = kv_ref[1 - side]


def qkv_call(place, at, xs, w, cosine, sine, gains):
    slots = len(xs)
    rows, width = xs[0].shape
    return pl.pallas_call(
        qkv_kernel,
        grid=(slots,),
        in_specs=[pl.BlockSpec(memory_space=pltpu.SMEM)]
        + [pl.BlockSpec(memory_space=pl.ANY)] * slots
        + [
            pl.BlockSpec(w.shape, lambda j: (0, 0)),
            pl.BlockSpec((1, 1, rows, 128), lambda j: (j, at, 0, 0)),
            pl.BlockSpec((1, 1, rows, 128), lambda j: (j, at, 0, 0)),
            pl.BlockSpec((1, 384), lambda j: (0, 0)),
        ],
        out_specs=[pl.BlockSpec((1, rows, 128), lambda j: (j, 0, 0))] * 4
        + [pl.BlockSpec((1, rows, 384), lambda j: (j, 0, 0))],
        out_shape=[jax.ShapeDtypeStruct((slots, rows, 128), BF16)] * 4
        + [jax.ShapeDtypeStruct((slots, rows, 384), F32)],
        scratch_shapes=[
            pltpu.VMEM((slots, rows, width), BF16),
            pltpu.VMEM((2, rows, 128), BF16),
            pltpu.VMEM((2, rows, 128), BF16),
            pltpu.SemaphoreType.DMA((slots,)),
        ],
        compiler_params=params(),
        cost_estimate=cost(7),
        name="qkv",
    )(place, *xs, w, cosine, sine, gains)


def lay_keys(place_ref, refs, kv_ref):
    c, t = place_ref[0], place_ref[1]
    for e, ref in enumerate(refs):
        for j in range(ref.shape[0]):
            kv_ref[4 * (c ^ swap_bits(j)) + (t ^ e)] = ref[j]


def lay_rows(place_ref, own_ref, got_ref, out_ref, high):
    c, side = place_ref[0], place_ref[1] & 1
    low = lanes_low(own_ref.shape[1])
    for ref, start in ((own_ref, 2 * side), (got_ref, 2 - 2 * side)):
        for j in range(ref.shape[0]):
            g = c ^ swap_bits(j)
            value = ref[j]
            turned = pltpu.roll(value, 64, 1)
            zero = jnp.zeros_like(value)
            if high:
                out_ref[g, start] = jnp.where(low, zero, turned)
                out_ref[g, start + 1] = jnp.where(low, zero, value)
            else:
                out_ref[g, start] = jnp.where(low, value, zero)
                out_ref[g, start + 1] = jnp.where(low, turned, zero)


def diagonal(rows, wide, edge):
    key = lax.broadcasted_iota(jnp.int32, (rows, wide), 0)
    column = lax.broadcasted_iota(jnp.int32, (rows, wide), 1)
    return (key <= (column & (rows - 1))) | (column >= edge)


def whole(shape):
    return pl.BlockSpec(shape, lambda j: (0,) * len(shape))


def attend_kernel(place_ref, *refs):
    q_own, q_got, keys = refs[0], refs[1], refs[2:6]
    own_out, other_out, o_ref, lse_ref, q_ref, kv_ref, acc_ref, sum_ref, ret_ref = refs[6:]
    c, t, g = place_ref[0], place_ref[1], pl.program_id(0)
    side, base = t & 1, t & 2
    rows = kv_ref.shape[1]
    half, wide = 2 * rows, 4 * rows

    @pl.when(g == 0)
    def _():
        lay_keys(place_ref, keys, kv_ref)
        lay_rows(place_ref, q_own, q_got, q_ref, False)

    queries = q_ref[g].reshape(wide, 128)
    acc_ref[...] = jnp.zeros_like(acc_ref)
    sum_ref[...] = jnp.zeros_like(sum_ref)

    def add(pair, skip, allowed):
        weights = jnp.exp2(dot_nt(pair, queries[skip:]) * LOG2E)
        if allowed is not None:
            weights = jnp.where(allowed, weights, 0.0)
        sum_ref[:, skip:] += jnp.sum(weights, axis=0, keepdims=True)
        acc_ref[:, skip:] += dot_tn(pair, weights.astype(BF16))

    def body(n, carry):
        add(kv_ref[pl.ds(2 * n, 2)].reshape(2 * rows, 128), 0, None)
        return carry

    last = 4 * g + base
    lax.fori_loop(0, last >> 1, body, 0)
    add(kv_ref[last], 0, diagonal(rows, wide, half))
    add(kv_ref[last + 1], half, diagonal(rows, half, half))
    total = sum_ref[...]
    out = acc_ref[...] / total
    o_ref[0] = out[64:]
    lse_ref[0] = jnp.log(total) * LOG2E
    flat = jnp.transpose(out)
    low = lanes_low(rows)
    slot = swap_bits(c ^ g)
    for u in range(2):
        first, second = (flat[(2 * u + h) * rows : (2 * u + h + 1) * rows] for h in range(2))
        ret_ref[u, slot] = pack(pltpu.roll(first, 64, 1), second, low).astype(BF16)

    @pl.when(g == pl.num_programs(0) - 1)
    def _():
        own_out[...] = ret_ref[side]
        other_out[...] = ret_ref[1 - side]


def attend_call(place, gets):
    slots, rows, _ = gets[0].shape
    wide = 4 * rows
    return pl.pallas_call(
        attend_kernel,
        grid=(4,),
        in_specs=[pl.BlockSpec(memory_space=pltpu.SMEM)] + [whole(gets[0].shape)] * 6,
        out_specs=[whole(gets[0].shape)] * 2
        + [
            pl.BlockSpec((1, 64, wide), lambda j: (j, 0, 0)),
            pl.BlockSpec((1, 1, wide), lambda j: (j, 0, 0)),
        ],
        out_shape=[jax.ShapeDtypeStruct(gets[0].shape, BF16)] * 2
        + [
            jax.ShapeDtypeStruct((4, 64, wide), F32),
            jax.ShapeDtypeStruct((4, 1, wide), F32),
        ],
        scratch_shapes=[
            pltpu.VMEM((4, 4, rows, 128), BF16),
            pltpu.VMEM((4 * slots, rows, 128), BF16),
            pltpu.VMEM((128, wide), F32),
            pltpu.VMEM((1, wide), F32),
            pltpu.VMEM((2, slots, rows, 128), BF16),
        ],
        compiler_params=params(),
        cost_estimate=cost(17),
        name="attend",
    )(place, *gets)


def out_kernel(place_ref, get_own, get_other, w_ref, mixed_ref, own_ref, near_ref, head_ref):
    side, j = place_ref[1] & 1, pl.program_id(0)
    head_ref[side] = get_own[0]
    head_ref[1 - side] = get_other[0]
    mixed = jnp.concatenate([head_ref[0], head_ref[1]], axis=1)
    mixed_ref[0] = mixed
    part = dot_nt(mixed, w_ref[:, 512:]).astype(BF16)

    @pl.when(j < 2)
    def _():
        own_ref[0] = part

    @pl.when(j >= 2)
    def _():
        near_ref[0] = part


def out_call(place, gets, w):
    slots, rows, _ = gets[0].shape
    width = w.shape[0]
    return pl.pallas_call(
        out_kernel,
        grid=(slots,),
        in_specs=[pl.BlockSpec(memory_space=pltpu.SMEM)]
        + [pl.BlockSpec((1, rows, 128), lambda j: (j, 0, 0))] * 2
        + [whole(w.shape)],
        out_specs=[
            pl.BlockSpec((1, rows, 256), lambda j: (j, 0, 0)),
            pl.BlockSpec((1, rows, width), lambda j: (jnp.minimum(j, 1), 0, 0)),
            pl.BlockSpec((1, rows, width), lambda j: (jnp.maximum(j - 2, 0), 0, 0)),
        ],
        out_shape=[
            jax.ShapeDtypeStruct((slots, rows, 256), BF16),
            jax.ShapeDtypeStruct((2, rows, width), BF16),
            jax.ShapeDtypeStruct((2, rows, width), BF16),
        ],
        scratch_shapes=[pltpu.VMEM((2, rows, 128), BF16)],
        compiler_params=params(),
        cost_estimate=cost(4),
        name="out",
    )(place, *gets, w)


def out_back_kernel(place_ref, *refs):
    x_refs, w_ref, own_out, other_out, x_ref, send_ref, sems = refs[0:4], *refs[4:]
    side, j = place_ref[1] & 1, pl.program_id(0)
    start_slots(x_refs, x_ref, sems)
    wait_slot(x_refs, x_ref, sems)
    back = dot_nn(x_ref[j], w_ref[:, 512:]).astype(BF16)
    send_ref[0] = back[:, :128]
    send_ref[1] = back[:, 128:]
    own_out[0] = send_ref[side]
    other_out[0] = send_ref[1 - side]


def out_back_call(place, xs, w):
    slots = len(xs)
    rows, width = xs[0].shape
    return pl.pallas_call(
        out_back_kernel,
        grid=(slots,),
        in_specs=[pl.BlockSpec(memory_space=pltpu.SMEM)]
        + [pl.BlockSpec(memory_space=pl.ANY)] * slots
        + [whole(w.shape)],
        out_specs=[pl.BlockSpec((1, rows, 128), lambda j: (j, 0, 0))] * 2,
        out_shape=[jax.ShapeDtypeStruct((slots, rows, 128), BF16)] * 2,
        scratch_shapes=[
            pltpu.VMEM((slots, rows, width), BF16),
            pltpu.VMEM((2, rows, 128), BF16),
            pltpu.SemaphoreType.DMA((slots,)),
        ],
        compiler_params=params(),
        cost_estimate=cost(4),
        name="out_back",
    )(place, *xs, w)


def attend_back_kernel(place_ref, *refs):
    q_own, q_got, keys, back_own, back_got = refs[0], refs[1], refs[2:6], refs[6], refs[7]
    o_ref, lse_ref, own_out, other_out, outs = refs[8], refs[9], refs[10], refs[11], refs[12:16]
    q_ref, kv_ref, back_ref, dkv_ref, acc_ref, ret_ref = refs[16:]
    c, t, g = place_ref[0], place_ref[1], pl.program_id(0)
    side, base = t & 1, t & 2
    rows = kv_ref.shape[1]
    half, wide = 2 * rows, 4 * rows

    @pl.when(g == 0)
    def _():
        lay_keys(place_ref, keys, kv_ref)
        lay_rows(place_ref, q_own, q_got, q_ref, False)
        lay_rows(place_ref, back_own, back_got, back_ref, True)
        dkv_ref[...] = jnp.zeros_like(dkv_ref)

    queries = q_ref[g].reshape(wide, 128)
    given = back_ref[g].reshape(wide, 128)
    delta = jnp.sum(jnp.transpose(given.astype(F32))[64:] * o_ref[0], axis=0, keepdims=True)
    lse = lse_ref[0]
    acc_ref[...] = jnp.zeros_like(acc_ref)

    def block(pair, skip, allowed):
        probs = jnp.exp2(dot_nt(pair, queries[skip:]) * LOG2E - lse[:, skip:])
        if allowed is not None:
            probs = jnp.where(allowed, probs, 0.0)
        slopes = dot_nt(pair, given[skip:])
        score_back = (probs * (slopes - delta[:, skip:])).astype(BF16)
        acc_ref[skip:] += dot_tn(score_back, pair)
        return dot_nn(probs.astype(BF16), given[skip:]) + dot_nn(score_back, queries[skip:])

    def body(n, carry):
        pair = kv_ref[pl.ds(2 * n, 2)].reshape(2 * rows, 128)
        dkv_ref[pl.ds(2 * n, 2)] += block(pair, 0, None).reshape(2, rows, 128)
        return carry

    last = 4 * g + base
    lax.fori_loop(0, last >> 1, body, 0)
    dkv_ref[last] += block(kv_ref[last], 0, diagonal(rows, wide, half))
    dkv_ref[last + 1] += block(kv_ref[last + 1], half, diagonal(rows, half, half))
    low = lanes_low(rows)
    slot = swap_bits(c ^ g)
    for u in range(2):
        first, second = (acc_ref[(2 * u + h) * rows : (2 * u + h + 1) * rows] * 0.125 for h in range(2))
        ret_ref[u, slot] = pack(first, pltpu.roll(second, 64, 1), low).astype(BF16)

    @pl.when(g == pl.num_programs(0) - 1)
    def _():
        own_out[...] = ret_ref[side]
        other_out[...] = ret_ref[1 - side]
        for e in range(4):
            for j in range(4):
                outs[e][j] = dkv_ref[4 * (c ^ swap_bits(j)) + (t ^ e)].astype(BF16)


def attend_back_call(place, gets, backs, o, lse):
    slots, rows, _ = gets[0].shape
    wide = 4 * rows
    return pl.pallas_call(
        attend_back_kernel,
        grid=(4,),
        in_specs=[pl.BlockSpec(memory_space=pltpu.SMEM)]
        + [whole(gets[0].shape)] * 8
        + [
            pl.BlockSpec((1, 64, wide), lambda j: (j, 0, 0)),
            pl.BlockSpec((1, 1, wide), lambda j: (j, 0, 0)),
        ],
        out_specs=[whole(gets[0].shape)] * 6,
        out_shape=[jax.ShapeDtypeStruct(gets[0].shape, BF16)] * 6,
        scratch_shapes=[
            pltpu.VMEM((4, 4, rows, 128), BF16),
            pltpu.VMEM((4 * slots, rows, 128), BF16),
            pltpu.VMEM((4, 4, rows, 128), BF16),
            pltpu.VMEM((4 * slots, rows, 128), F32),
            pltpu.VMEM((wide, 128), F32),
            pltpu.VMEM((2, slots, rows, 128), BF16),
        ],
        compiler_params=params(),
        cost_estimate=cost(36),
        name="attend_back",
    )(place, *gets, *backs, o, lse)


def qkv_back_kernel(place_ref, *refs):
    q_own, q_got, keys, (raw_ref, cos_ref, sin_ref, gain_ref, w_ref) = refs[0], refs[1], refs[2:6], refs[6:11]
    back_ref, own_ref, near_ref, share_ref, head_ref, pair_ref = refs[11:]
    side, j = place_ref[1] & 1, pl.program_id(0)
    rows = raw_ref.shape[1]
    head_ref[side] = q_own[0].astype(F32)
    head_ref[1 - side] = q_got[0].astype(F32)
    pair_ref[side] = keys[0][0].astype(F32) + keys[2][0].astype(F32)
    pair_ref[1 - side] = keys[1][0].astype(F32) + keys[3][0].astype(F32)
    low = lanes_low(rows)
    early = (lax.broadcasted_iota(jnp.int32, (rows, 128), 1) & 32) == 0
    cosine, sine = cos_ref[0, 0], sin_ref[0, 0]

    @pl.when(j == 0)
    def _():
        share_ref[...] = jnp.zeros_like(share_ref)

    even, odd = pair_ref[0], pair_ref[1]
    key = pack(even, pltpu.roll(odd, 64, 1), low)
    value = pack(pltpu.roll(even, 64, 1), odd, low)
    outs = []
    for b, given in enumerate((head_ref[0], head_ref[1], key)):
        z = sine * given
        cotangent = given * cosine + jnp.where(early, pltpu.roll(z, 96, 1), -pltpu.roll(z, 32, 1))
        u = raw_ref[0, :, b * 128 : (b + 1) * 128]
        gain = gain_ref[:, b * 128 : (b + 1) * 128]
        r = lax.rsqrt(head_sums(u * u) * (1.0 / 64.0) + EPS)
        mean = head_sums(u * gain * cotangent) * (1.0 / 64.0)
        share_ref[:, b * 128 : (b + 1) * 128] += jnp.sum(cotangent * u * r, axis=0, keepdims=True)
        outs.append((r * gain * cotangent - u * (r * r * r) * mean).astype(BF16))
    outs.append(value.astype(BF16))
    back = jnp.concatenate(outs, axis=1)
    back_ref[0] = back
    part = dot_nt(back, w_ref[:, :512]).astype(BF16)

    @pl.when(j < 2)
    def _():
        own_ref[0] = part

    @pl.when(j >= 2)
    def _():
        near_ref[0] = part


def qkv_back_call(place, at, gets, raw, cosine, sine, gains, w):
    slots, rows, _ = raw.shape
    width = w.shape[0]
    return pl.pallas_call(
        qkv_back_kernel,
        grid=(slots,),
        in_specs=[pl.BlockSpec(memory_space=pltpu.SMEM)]
        + [pl.BlockSpec((1, rows, 128), lambda j: (j, 0, 0))] * 6
        + [
            pl.BlockSpec((1, rows, 384), lambda j: (j, 0, 0)),
            pl.BlockSpec((1, 1, rows, 128), lambda j: (j, at, 0, 0)),
            pl.BlockSpec((1, 1, rows, 128), lambda j: (j, at, 0, 0)),
            whole((1, 384)),
            whole(w.shape),
        ],
        out_specs=[
            pl.BlockSpec((1, rows, 512), lambda j: (j, 0, 0)),
            pl.BlockSpec((1, rows, width), lambda j: (jnp.minimum(j, 1), 0, 0)),
            pl.BlockSpec((1, rows, width), lambda j: (jnp.maximum(j - 2, 0), 0, 0)),
            whole((1, 384)),
        ],
        out_shape=[
            jax.ShapeDtypeStruct((slots, rows, 512), BF16),
            jax.ShapeDtypeStruct((2, rows, width), BF16),
            jax.ShapeDtypeStruct((2, rows, width), BF16),
            jax.ShapeDtypeStruct((1, 384), F32),
        ],
        scratch_shapes=[pltpu.VMEM((2, rows, 128), F32), pltpu.VMEM((2, rows, 128), F32)],
        compiler_params=params(),
        cost_estimate=cost(7),
        name="qkv_back",
    )(place, *gets, raw, cosine, sine, gains, w)


def ffn_kernel(halves, *refs):
    offset_ref, x_refs, given_refs = refs[0], refs[1:5], refs[5:9]
    pieces = refs[9 : 9 + 3 * halves]
    refs = refs[9 + 3 * halves :]
    outs, (w_ref, x_ref, given_ref), held = refs[:7], refs[7:10], refs[10:17]
    sems, x_sems, given_sems, out_sems = refs[17:]
    _, rows, width = x_ref.shape
    count = 2 * rows
    blocks, depth, span = pieces[0].shape

    def copies(j):
        found = []
        for p in range(halves):
            start = pl.multiple_of(offset_ref[p], 128)
            for i in range(blocks):
                found.append(
                    pltpu.make_async_copy(
                        pieces[j * halves + p].at[i],
                        w_ref.at[j, pl.ds(i * depth, depth), pl.ds(start, span)],
                        sems.at[j, p, i],
                    )
                )
        return found

    def start(found):
        for copy in found:
            copy.start()

    def wait(found):
        for copy in found:
            copy.wait()

    tokens, givens = slot_copies(x_refs, x_ref, x_sems), slot_copies(given_refs, given_ref, given_sems)
    for found in (tokens[:2], copies(0), copies(1), copies(2), givens[:2], tokens[2:], givens[2:]):
        start(found)
    leaving = []

    def leave(at, k, value):
        ref, out = held[at], outs[at]
        if at < 3:
            ref[2 * k : 2 * k + 2] = value.reshape(2, rows, -1)
            source, target = ref.at[pl.ds(2 * k, 2)], out.at[pl.ds(2 * k, 2)]
        else:
            ref[...] = value.reshape(2, rows, -1)
            source, target = ref, out
        leaving.append(pltpu.make_async_copy(source, target, out_sems.at[at, k if at < 3 else 0]))
        leaving[-1].start()

    for k in range(2):
        wait(tokens[2 * k : 2 * k + 2])
        x = x_ref[2 * k : 2 * k + 2].reshape(count, width)
        if k == 0:
            wait(copies(0))
        gate = dot_nt(x, w_ref[0])
        if k == 0:
            wait(copies(1))
        up = dot_nt(x, w_ref[1])
        sig = jax.nn.sigmoid(gate)
        swish = gate * sig
        hidden = (swish * up).astype(BF16)
        leave(0, k, hidden)
        if k == 0:
            wait(copies(2))
        wait(givens[2 * k : 2 * k + 2])
        hidden_back = dot_nt(given_ref[2 * k : 2 * k + 2].reshape(count, width), w_ref[2])
        gate_back = (hidden_back * up * (sig * (1.0 + gate * (1.0 - sig)))).astype(BF16)
        leave(1, k, gate_back)
        up_back = (hidden_back * swish).astype(BF16)
        leave(2, k, up_back)
        leave(3 + k, k, dot_nn(hidden, w_ref[2]).astype(BF16))
        leave(5 + k, k, (dot_nn(gate_back, w_ref[0]) + dot_nn(up_back, w_ref[1])).astype(BF16))
    wait(leaving)


def ffn_call(offsets, xs, given, pieces):
    rows, width = xs[0].shape
    halves = len(pieces[0])
    blocks, depth, _ = pieces[0][0].shape
    hidden = blocks * depth
    shapes = [(4, rows, hidden)] * 3 + [(2, rows, width)] * 4
    return pl.pallas_call(
        functools.partial(ffn_kernel, halves),
        in_specs=[pl.BlockSpec(memory_space=pltpu.SMEM)] + [pl.BlockSpec(memory_space=pl.ANY)] * (8 + 3 * halves),
        out_specs=[pl.BlockSpec(memory_space=pl.ANY)] * 7,
        out_shape=[jax.ShapeDtypeStruct(shape, BF16) for shape in shapes],
        scratch_shapes=[
            pltpu.VMEM((3, hidden, width), BF16),
            pltpu.VMEM((4, rows, width), BF16),
            pltpu.VMEM((4, rows, width), BF16),
        ]
        + [pltpu.VMEM(shape, BF16) for shape in shapes]
        + [
            pltpu.SemaphoreType.DMA((3, halves, blocks)),
            pltpu.SemaphoreType.DMA((4,)),
            pltpu.SemaphoreType.DMA((4,)),
            pltpu.SemaphoreType.DMA((7, 2)),
        ],
        compiler_params=params(),
        cost_estimate=cost(22),
        name="ffn",
    )(offsets, *xs, *given, *[piece for row in pieces for piece in row])


def weight_kernel(halves, offset_ref, *refs):
    lefts, rights = refs[0:2], refs[2:10]
    outs, total_ref = refs[10 : 10 + halves], refs[10 + halves]
    blocks, depth, span = outs[0].shape
    total = 0.0
    for s, left in enumerate(lefts):
        a = left[...]
        b = jnp.concatenate([ref[...] for ref in rights[4 * s : 4 * s + 4]])
        total = total + dot_tn(a.reshape(-1, a.shape[-1]), b)
    total_ref[...] = total.astype(BF16)
    for p in range(halves):
        start = pl.multiple_of(offset_ref[p], 128)
        for i in range(blocks):
            outs[p][i] = total_ref[i * depth : (i + 1) * depth, pl.ds(start, span)]


def weight_call(offsets, lefts, rights, halves, blocks):
    units, width = lefts[0].shape[-1], rights[0][0].shape[-1]
    part = (blocks, units // blocks, width // halves)
    return pl.pallas_call(
        functools.partial(weight_kernel, halves),
        in_specs=[pl.BlockSpec(memory_space=pltpu.SMEM)] + [pl.BlockSpec(memory_space=pltpu.VMEM)] * 10,
        out_specs=[pl.BlockSpec(memory_space=pltpu.VMEM)] * halves,
        out_shape=[jax.ShapeDtypeStruct(part, BF16)] * halves,
        scratch_shapes=[pltpu.VMEM((units, width), BF16)],
        compiler_params=params(),
        cost_estimate=cost(10),
        name="weight",
    )(offsets, *lefts, *rights[0], *rights[1])


def small_weight_kernel(halves, near, place_ref, offset_ref, *refs):
    lefts, rights, outs, total_ref = refs[0:2], refs[2:10], refs[10 : 10 + halves], refs[10 + halves]
    t = place_ref[1]
    total = 0.0
    for s, left in enumerate(lefts):
        a = left[...]
        b = jnp.concatenate([ref[...] for ref in rights[4 * s : 4 * s + 4]])
        total = total + dot_tn(a.reshape(-1, a.shape[-1]), b)
    total_ref[...] = total.astype(BF16)
    blocks, _, span = outs[0].shape
    for p in range(halves):
        for e in range(blocks):
            if near:
                outs[p][e] = total_ref[:, pl.ds(pl.multiple_of(offset_ref[p] + (t ^ e) * span, 128), span)]
            else:
                outs[p][e] = total_ref[:, e * span : (e + 1) * span]


def small_weight_call(place, offsets, lefts, rights, halves, blocks, near):
    rows, width = lefts[0].shape[-1], rights[0][0].shape[-1]
    part = (blocks, rows, width // blocks // halves)
    return pl.pallas_call(
        functools.partial(small_weight_kernel, halves, near),
        in_specs=[pl.BlockSpec(memory_space=pltpu.SMEM)] * 2 + [pl.BlockSpec(memory_space=pltpu.VMEM)] * 10,
        out_specs=[pl.BlockSpec(memory_space=pltpu.VMEM)] * halves,
        out_shape=[jax.ShapeDtypeStruct(part, BF16)] * halves,
        scratch_shapes=[pltpu.VMEM((rows, width), BF16)],
        compiler_params=params(),
        cost_estimate=cost(5),
        name="small_weight",
    )(place, offsets, *lefts, *rights[0], *rights[1])


def inverse_root(values):
    return lax.rsqrt(jnp.mean(values * values, axis=-1, keepdims=True) + EPS)


def norm_back(values, root, gain, given):
    mean = jnp.mean(values * gain * given, axis=-1, keepdims=True)
    return root * gain * given - values * (root * root * root) * mean


def per_device(
    sizes,
    tokens,
    positions,
    first_gain,
    query_weight,
    key_weight,
    value_weight,
    query_gain,
    key_gain,
    output_weight,
    second_gain,
    gate_weight,
    up_weight,
    down_weight,
    upstream,
):
    shards, ctx, tp = sizes["shard"], sizes["ctx"], sizes["tp"]
    groups = ("shard", "tp")
    sequences, rows, width = tokens.shape
    head_dim = query_gain.shape[0]
    depth = query_weight.shape[0]
    units = gate_weight.shape[1]
    c, t = lax.axis_index("ctx"), lax.axis_index("tp")
    place = jnp.stack([c, t]).astype(jnp.int32)
    trade = [(i * tp + k, k * ctx + i) for i in range(ctx) for k in range(tp)]

    line = Line()
    small = jnp.concatenate([query_weight, key_weight, value_weight, output_weight.T], axis=1)
    small = lax.ppermute(small, ("ctx", "tp"), trade)
    blocks_attn = trade_tp(small, tp)
    w_attn = join_shard(blocks_attn.reshape(tp * depth, -1), shards)

    large = jnp.stack([gate_weight.T, up_weight.T, down_weight]).reshape(3, ctx, units // ctx, depth)
    large = lax.all_to_all(large, "ctx", 1, 1, tiled=True)
    large = after(large, small).transpose(0, 2, 1, 3).reshape(3, units // ctx, ctx * depth)
    halves = 2 if shards == 2 else 1
    shard = lax.axis_index("shard")
    starts = jnp.stack([shard, 1 - shard])[:halves] if halves == 2 else jnp.zeros((1,), jnp.int32)
    starts = (starts * (width // halves)).astype(jnp.int32)

    mine = lax.dynamic_slice_in_dim(positions, t * rows, rows, 1).astype(F32)
    places = jnp.stack(gather_ctx(mine))
    freqs = jnp.exp(-math.log(THETA) * jnp.arange(0, head_dim, 2).astype(F32) / head_dim)
    angles = places[..., None] * freqs
    cosine, sine = jnp.cos(angles), jnp.sin(angles)
    cosine = jnp.concatenate([cosine] * 4, axis=-1)
    sine = jnp.concatenate([sine] * 4, axis=-1)
    gains = jnp.concatenate([jnp.tile(query_gain, 4), jnp.tile(key_gain, 2)])[None]

    x = tokens.astype(F32)
    root = inverse_root(x)
    first = (x * root * first_gain).astype(BF16)
    given = upstream.astype(F32)

    pair = range(sequences)
    first_all = [gather_ctx(first[s]) for s in pair]
    heads, raw = [], []
    for s in pair:
        one = line.run(qkv_call, place, s, first_all[s], w_attn, cosine, sine, gains)
        heads.append(exchange_heads(one[0], one[1], (one[2], one[3], one[2], one[3])))
        raw.append(one[4])
    lines = [lax.all_gather(after(large[0], blocks_attn), "tp", axis=0, tiled=False)]
    for j in (1, 2):
        lines.append(lax.all_gather(after(large[j], *heads[1]), "tp", axis=0, tiled=False))
    w_ffn = [gather_shard(one, shards) for one in lines]
    upstream_all = [gather_ctx(after(upstream[s], raw[0])) for s in pair]
    heads[0] = after(heads[0], lines[0])
    heads[1] = after(heads[1], w_ffn[0][-1])

    attended, sent = [], []
    for s in pair:
        attended.append(line.run(attend_call, place, heads[s]))
        sent.append([attended[s][0], to_tp(attended[s][1], 1)])

    def middle_of(share, rows_in):
        middle = rows_in + share
        middle_root = inverse_root(middle)
        return (middle * middle_root * second_gain).astype(BF16), middle, middle_root

    mixed, shares_near, shares_far, middles, seconds = [], [], [], [], []
    for s in pair:
        one = line.run(out_call, place, sent[s], w_attn)
        mixed.append(one[0])
        shares_near.append(reduce_near(one[1], one[2]))
    shares_near[0] = after(shares_near[0], lines[1])
    shares_near[1] = after(shares_near[1], lines[2], w_ffn[1][-1])
    for s in pair:
        second, middle, middle_root = line.run(lambda a, b, rows_in: middle_of(reduce_far(a, b), rows_in), *shares_near[s], x[s])
        middles.append((middle, middle_root))
        seconds.append(gather_ctx(second))
    ffn = [line.run(ffn_call, starts, seconds[s], upstream_all[s], w_ffn) for s in pair]

    results, back_rows, mixed_back_all = [], [], []
    sums, backs_sent, got, g_ffn = [], [], [], []

    def turn_back(second_back, s):
        middle, middle_root = middles[s]
        middle_back = given[s] + norm_back(middle, middle_root, second_gain, second_back)
        return middle_back.astype(BF16), middle_back, jnp.sum(second_back * middle * middle_root, axis=0)

    def turn(s, call, *shares):
        low, middle_back, share = line.run(lambda first, *rest: turn_back(call(first, *rest), s), *shares)
        back_rows.append(middle_back)
        mixed_back_all.append(gather_ctx(low))
        return share

    def weight(j):
        at, rights = ((1, seconds), (2, seconds), (0, upstream_all))[j]
        parts = line.run(weight_call, starts, [one[at] for one in ffn], rights, halves, tp)
        sums.append((parts, send_shard(parts, shards)))

    def back_out(s):
        own, other = line.run(out_back_call, place, mixed_back_all[s], w_attn)
        backs_sent.append([own, to_tp(other, 1)])

    def back_attend(s):
        one = line.run(attend_back_call, place, heads[s], backs_sent[s], attended[s][2], attended[s][3])
        got.append(exchange_heads(one[0], one[1], one[2:]))

    def add(j):
        parts, moved = sums[j]
        g_ffn.append(lax.psum_scatter(line.run(add_shard, moved, parts), "tp", scatter_dimension=0, tiled=False))

    shares = ffn[0][5][0], *(
        lax.ppermute(value, "ctx", way) for value, way in ((ffn[0][5][1], FAR), (ffn[0][6][0], NEAR), (ffn[0][6][1], CROSS))
    )
    second_share = turn(0, lambda *parts: sum(part.astype(F32) for part in parts), *shares)
    mine, away = line.run(lambda near, own: add_near(own, near), lax.ppermute(ffn[1][6], "ctx", NEAR), ffn[1][5])
    away = lax.ppermute(away, "ctx", FAR)
    weight(0)
    weight(1)
    back_out(0)
    second_share = second_share + turn(1, lambda far, own: own + far.astype(F32), away, mine)
    weight(2)
    aligned = depth % 128 == 0
    count = shards * tp
    g_out = line.run(small_weight_call, place, starts, mixed, mixed_back_all, 1, count if aligned else 1, False)[0]
    if not aligned:
        g_out = g_out[0].reshape(-1, count, width // count).transpose(1, 0, 2)
    add(0)
    back_out(1)
    g_out = lax.psum_scatter(g_out, groups, scatter_dimension=0, tiled=False)
    back_attend(0)
    add(1)
    add(2)
    back_attend(1)

    for s in pair:
        results.append((middles[s][0] + reduce_far(*reduce_near(ffn[s][3], after(ffn[s][4], got[0][0])))).astype(BF16))

    gradients, shares, head_share, backs, firsts = [], [], 0.0, [], []
    for s in pair:
        back, own, other, share = line.run(qkv_back_call, place, s, got[s], raw[s], cosine, sine, gains, w_attn)
        backs.append(back)
        head_share = head_share + share
        firsts.append(reduce_near(own, other))
    near = aligned and halves == 2
    parts = line.run(small_weight_call, place, starts, backs, first_all, 2 if near else 1, tp if near else 1, near)
    moved = lax.ppermute(parts[1], "shard", [(0, 1), (1, 0)]) if near else None

    def last(mine, away, s):
        first_back = reduce_far(mine, away)
        gradient = back_rows[s] + norm_back(x[s], root[s], first_gain, first_back)
        return jnp.sum(first_back * x[s] * root[s], axis=0), gradient

    for s in pair:
        share, gradient = line.run(lambda a, b: last(a, b, s), *firsts[s])
        shares.append(share)
        gradients.append(gradient)
    shares = jnp.concatenate([shares[0] + shares[1], second_share, head_share[0]])
    shares = sum_all(shares, [(name, sizes[name]) for name in ("ctx", "shard", "tp")])
    if moved is None:
        g_qkv = jnp.concatenate([part[0] for part in parts], axis=1)
        g_qkv = g_qkv.reshape(-1, count, width // count).transpose(1, 0, 2)
        g_qkv = lax.psum_scatter(g_qkv, groups, scatter_dimension=0, tiled=False)
    else:
        g_qkv = line.run(lambda a, b: (a.astype(F32) + b.astype(F32)).astype(BF16), moved, parts[0])
        g_qkv = sum(part.astype(F32) for part in exchange_tp([g_qkv[e] for e in range(tp)])).astype(BF16)

    g_ffn = jnp.stack(g_ffn)
    g_ffn = g_ffn.reshape(3, units // ctx, ctx, depth).transpose(0, 2, 1, 3)
    g_ffn = lax.all_to_all(g_ffn, "ctx", 1, 1, tiled=True)
    g_ffn = g_ffn.reshape(3, units, depth).astype(F32)
    g_out = lax.ppermute(g_out, ("ctx", "tp"), trade).astype(F32)
    g_attn = lax.ppermute(g_qkv, ("ctx", "tp"), trade).astype(F32)
    heads_end = query_weight.shape[1]
    pairs = key_weight.shape[1]

    head_total = shares[2 * width :]
    return (
        jnp.stack(results),
        jnp.stack(gradients),
        g_attn[:heads_end].T,
        g_attn[heads_end : heads_end + pairs].T,
        g_attn[heads_end + pairs : heads_end + 2 * pairs].T,
        g_out,
        g_ffn[0].T,
        g_ffn[1].T,
        g_ffn[2],
        shares[:width],
        shares[width : 2 * width],
        jnp.sum(head_total[: 4 * head_dim].reshape(4, head_dim), axis=0),
        jnp.sum(head_total[4 * head_dim :].reshape(2, head_dim), axis=0),
    )


def solution(mesh):
    rows = P("shard", ("ctx", "tp"), None)
    wide = P(("shard", "ctx"), "tp")
    tall = P("tp", ("shard", "ctx"))
    none = P()
    in_specs = (
        rows, P("shard", "ctx"), none, wide, wide, wide, none, none, tall, none, wide, wide, tall, rows,
    )
    out_specs = (rows, rows, wide, wide, wide, tall, wide, wide, tall, none, none, none, none)
    sizes = {name: mesh.shape[name] for name in ("shard", "ctx", "tp")}
    return jax.shard_map(
        functools.partial(per_device, sizes), mesh=mesh, in_specs=in_specs, out_specs=out_specs, check_vma=False
    )
```

```python
import functools
import math

import jax
import jax.numpy as jnp
from jax import lax
from jax.experimental import pallas as pl
from jax.experimental.pallas import tpu as pltpu
from jax.sharding import PartitionSpec as P

EPS = 1e-05
THETA = 1000000.0
LOG2E = 1.4426950408889634
F32 = jnp.float32
BF16 = jnp.bfloat16
NEAR = [(0, 1), (1, 0), (2, 3), (3, 2)]
FAR = [(0, 2), (2, 0), (1, 3), (3, 1)]
CROSS = [(0, 3), (3, 0), (1, 2), (2, 1)]
LIMIT = 56 * 1024 * 1024


def dot_nn(left, right):
    return lax.dot_general(left, right, (((1,), (0,)), ((), ())), preferred_element_type=F32)


def dot_nt(left, right):
    return lax.dot_general(left, right, (((1,), (1,)), ((), ())), preferred_element_type=F32)


def dot_tn(left, right):
    return lax.dot_general(left, right, (((0,), (0,)), ((), ())), preferred_element_type=F32)


def swap_bits(j):
    return ((j & 1) << 1) | (j >> 1)


def gather_ctx(own):
    far = lax.ppermute(own, "ctx", FAR)
    near = lax.ppermute(own, "ctx", NEAR)
    return [own, far, near, lax.ppermute(far, "ctx", NEAR)]


def add_near(own, got):
    return own[0].astype(F32) + got[0].astype(F32), (own[1].astype(F32) + got[1].astype(F32)).astype(BF16)


def reduce_near(own, near):
    return add_near(own, lax.ppermute(near, "ctx", NEAR))


def reduce_far(mine, away):
    return mine + lax.ppermute(away, "ctx", FAR).astype(F32)


def reduce_ctx(own, near):
    got = lax.ppermute(own[1], "ctx", FAR), lax.ppermute(near[0], "ctx", NEAR), lax.ppermute(near[1], "ctx", CROSS)
    return own[0].astype(F32) + got[0].astype(F32) + got[1].astype(F32) + got[2].astype(F32)


def to_tp(value, e):
    return lax.ppermute(value, "tp", [(i, i ^ e) for i in range(4)])


def exchange_tp(blocks):
    return [blocks[0]] + [to_tp(blocks[e], e) for e in range(1, len(blocks))]


def exchange_heads(q_same, kv):
    return [q_same, *exchange_tp(kv)]


def gather_shard(own, shards):
    if shards == 2:
        return [own, lax.ppermute(own, "shard", [(0, 1), (1, 0)])]
    every = lax.all_gather(own, "shard", axis=0, tiled=False)
    return [every.transpose(1, 2, 0, 3).reshape(*own.shape[:2], -1)]


def send_shard(parts, shards):
    if shards == 2:
        return lax.ppermute(parts[1], "shard", [(0, 1), (1, 0)])
    blocks, units, width = parts[0].shape
    every = parts[0].reshape(blocks, units, shards, width // shards).transpose(2, 0, 1, 3)
    return lax.psum_scatter(every, "shard", scatter_dimension=0, tiled=False)


def add_shard(got, parts):
    return (parts[0].astype(F32) + got.astype(F32)).astype(BF16) if len(parts) == 2 else got


def after(value, *others):
    return lax.optimization_barrier((value, *others))[0]


class Line:
    def __init__(self):
        self.last = ()

    def run(self, call, first, *others):
        result = call(after(first, *self.last), *others)
        self.last = (jax.tree.leaves(result)[0],)
        return result


def trade_tp(own, count):
    got = [own]
    for k in range(1, count):
        got.append(lax.ppermute(own, "tp", [(i, i ^ k) for i in range(count)]))
    index = lax.axis_index("tp")
    slots = []
    for slot in range(count):
        value = got[slot]
        for at in range(1, count):
            value = jnp.where(index == at, got[slot ^ at], value)
        slots.append(value)
    return jnp.stack(slots)


def join_shard(own, shards):
    if shards == 2:
        other = lax.ppermute(own, "shard", [(0, 1), (1, 0)])
        index = lax.axis_index("shard")
        return jnp.concatenate([jnp.where(index == 0, own, other), jnp.where(index == 0, other, own)])
    return lax.all_gather(own, "shard", axis=0, tiled=True)


def sum_all(vector, sizes):
    for name, size in sizes:
        step = 1
        while step < size:
            other = lax.ppermute(vector, name, [(i, i ^ step) for i in range(size)])
            vector = vector + other
            step *= 2
    return vector


def params():
    return pltpu.CompilerParams(vmem_limit_bytes=LIMIT)


def cost(micros):
    return pl.CostEstimate(flops=int(micros * 1.0e9), transcendentals=0, bytes_accessed=int(micros * 1.0e6))


def slot_copies(refs, held, sems):
    return [pltpu.make_async_copy(ref, held.at[k], sems.at[k]) for k, ref in enumerate(refs)]


def start_slots(refs, held, sems):
    @pl.when(pl.program_id(0) == 0)
    def _():
        for copy in slot_copies(refs, held, sems):
            copy.start()


def wait_slot(refs, held, sems, step=1):
    for k, copy in enumerate(slot_copies(refs, held, sems)):

        @pl.when(pl.program_id(0) == k // step)
        def _():
            copy.wait()


def lanes_low(rows):
    return lax.broadcasted_iota(jnp.int32, (rows, 128), 1) < 64


def pack(first, second, low):
    return jnp.where(low, first, second)


def head_sums(values):
    rows = lax.broadcasted_iota(jnp.int32, (128, 128), 0) >> 6
    columns = lax.broadcasted_iota(jnp.int32, (128, 128), 1) >> 6
    ones = jnp.where(rows == columns, 1.0, 0.0).astype(BF16)
    high = values.astype(BF16)
    rest = values - high.astype(F32)
    low = rest.astype(BF16)
    return dot_nn(high, ones) + dot_nn(low, ones)


def qkv_kernel(place_ref, *refs):
    x_refs, (w_ref, cos_ref, sin_ref, gain_ref) = refs[:4], refs[4:8]
    q_same, kv_same, beside, kv_other, raw_ref, x_ref, q_ref, kv_ref, sems = refs[8:]
    side, s, j = place_ref[1] & 1, pl.program_id(0), pl.program_id(1)
    rows = x_ref.shape[2]
    copies = slot_copies(x_refs, x_ref, sems)

    @pl.when((s == 0) & (j == 0))
    def _():
        for copy in copies:
            copy.start()

    for k, copy in enumerate(copies):

        @pl.when((s == 0) & (j == k))
        def _():
            copy.wait()

    y = dot_nn(x_ref[j, s], w_ref[:, :512])
    raw_ref[0, 0] = y[:, :384]
    low = lanes_low(rows)
    early = (lax.broadcasted_iota(jnp.int32, (rows, 128), 1) & 32) == 0
    cosine, sine = cos_ref[0, 0], sin_ref[0, 0]
    turned = []
    for b in range(3):
        u = y[:, b * 128 : (b + 1) * 128]
        r = lax.rsqrt(head_sums(u * u) * (1.0 / 64.0) + EPS)
        n = u * r * gain_ref[:, b * 128 : (b + 1) * 128]
        other = jnp.where(early, -pltpu.roll(n, 96, 1), pltpu.roll(n, 32, 1))
        turned.append(n * cosine + other * sine)
    key, value = turned[2], y[:, 384:512]
    q_ref[0] = (turned[0] * 0.125).astype(BF16)
    q_ref[1] = (turned[1] * 0.125).astype(BF16)
    kv_ref[0] = pack(key, pltpu.roll(value, 64, 1), low).astype(BF16)
    kv_ref[1] = pack(pltpu.roll(key, 64, 1), value, low).astype(BF16)
    q_same[0, 0] = q_ref[side]
    kv_same[0, 0] = kv_ref[side]
    beside[0, 0, :rows] = q_ref[1 - side]
    beside[0, 0, rows:] = kv_ref[1 - side]
    kv_other[0, 0] = kv_ref[1 - side]


def step_block(*shape):
    return pl.BlockSpec((1, 1, *shape), lambda s, j: (s, j, 0, 0))


def table_block(*shape):
    return pl.BlockSpec((1, 1, *shape), lambda s, j: (j, s, 0, 0))


def whole2(shape):
    return pl.BlockSpec(shape, lambda s, j: (0,) * len(shape))


def qkv_call(place, xs, w, cosine, sine, gains):
    slots = len(xs)
    pair, rows, width = xs[0].shape
    talls = (rows, rows, 2 * rows, rows)
    return pl.pallas_call(
        qkv_kernel,
        grid=(pair, slots),
        in_specs=[pl.BlockSpec(memory_space=pltpu.SMEM)]
        + [pl.BlockSpec(memory_space=pl.ANY)] * slots
        + [whole2(w.shape), table_block(rows, 128), table_block(rows, 128), whole2((1, 384))],
        out_specs=[step_block(tall, 128) for tall in talls] + [step_block(rows, 384)],
        out_shape=[jax.ShapeDtypeStruct((pair, slots, tall, 128), BF16) for tall in talls]
        + [jax.ShapeDtypeStruct((pair, slots, rows, 384), F32)],
        scratch_shapes=[
            pltpu.VMEM((slots, pair, rows, width), BF16),
            pltpu.VMEM((2, rows, 128), BF16),
            pltpu.VMEM((2, rows, 128), BF16),
            pltpu.SemaphoreType.DMA((slots,)),
        ],
        compiler_params=params(),
        cost_estimate=cost(15),
        name="qkv",
    )(place, *xs, w, cosine, sine, gains)


def lay_keys(place_ref, refs, kv_ref):
    c, t = place_ref[0], place_ref[1]
    for e, ref in enumerate(refs):
        for j in range(ref.shape[1]):
            kv_ref[4 * (c ^ swap_bits(j)) + (t ^ e)] = ref[0, j, ref.shape[2] - kv_ref.shape[1] :]


def lay_rows(place_ref, own_ref, got_ref, out_ref, high):
    c, side = place_ref[0], place_ref[1] & 1
    rows = out_ref.shape[2]
    low = lanes_low(rows)
    for ref, start in ((own_ref, 2 * side), (got_ref, 2 - 2 * side)):
        for j in range(4):
            g = c ^ swap_bits(j)
            value = ref[0, j, :rows] if len(ref.shape) == 4 else ref[j, :rows]
            turned = pltpu.roll(value, 64, 1)
            zero = jnp.zeros_like(value)
            if high:
                out_ref[g, start] = jnp.where(low, zero, turned)
                out_ref[g, start + 1] = jnp.where(low, zero, value)
            else:
                out_ref[g, start] = jnp.where(low, value, zero)
                out_ref[g, start + 1] = jnp.where(low, turned, zero)


def diagonal(rows, wide, edge):
    key = lax.broadcasted_iota(jnp.int32, (rows, wide), 0)
    column = lax.broadcasted_iota(jnp.int32, (rows, wide), 1)
    return (key <= (column & (rows - 1))) | (column >= edge)


def whole(shape):
    return pl.BlockSpec(shape, lambda j: (0,) * len(shape))


def attend_kernel(place_ref, *refs):
    q_own, keys = refs[0], refs[1:5]
    own_out, other_out, o_ref, lse_ref, q_ref, kv_ref, acc_ref, sum_ref, ret_ref = refs[5:]
    c, t, g = place_ref[0], place_ref[1], pl.program_id(1)
    side, base = t & 1, t & 2
    rows = kv_ref.shape[1]
    half, wide = 2 * rows, 4 * rows

    @pl.when(g == 0)
    def _():
        lay_keys(place_ref, keys, kv_ref)
        lay_rows(place_ref, q_own, keys[1], q_ref, False)

    queries = q_ref[g].reshape(wide, 128)
    acc_ref[...] = jnp.zeros_like(acc_ref)
    sum_ref[...] = jnp.zeros_like(sum_ref)

    def add(pair, skip, allowed):
        weights = jnp.exp2(dot_nt(pair, queries[skip:]) * LOG2E)
        if allowed is not None:
            weights = jnp.where(allowed, weights, 0.0)
        sum_ref[:, skip:] += jnp.sum(weights, axis=0, keepdims=True)
        acc_ref[:, skip:] += dot_tn(pair, weights.astype(BF16))

    def body(n, carry):
        add(kv_ref[pl.ds(2 * n, 2)].reshape(2 * rows, 128), 0, None)
        return carry

    last = 4 * g + base
    lax.fori_loop(0, last >> 1, body, 0)
    add(kv_ref[last], 0, diagonal(rows, wide, half))
    add(kv_ref[last + 1], half, diagonal(rows, half, half))
    total = sum_ref[...]
    out = acc_ref[...] / total
    o_ref[0, 0] = out[64:]
    lse_ref[0, 0] = jnp.log(total) * LOG2E
    flat = jnp.transpose(out)
    low = lanes_low(rows)
    slot = swap_bits(c ^ g)
    for u in range(2):
        first, second = (flat[(2 * u + h) * rows : (2 * u + h + 1) * rows] for h in range(2))
        ret_ref[u, slot] = pack(pltpu.roll(first, 64, 1), second, low).astype(BF16)

    @pl.when(g == 3)
    def _():
        own_out[0] = ret_ref[side]
        other_out[0] = ret_ref[1 - side]


def sequence_block(shape):
    return pl.BlockSpec((1, *shape[1:]), lambda s, j: (s, 0, 0, 0))


def attend_call(place, gets):
    pair, slots, rows, _ = gets[0].shape
    wide = 4 * rows
    return pl.pallas_call(
        attend_kernel,
        grid=(pair, 4),
        in_specs=[pl.BlockSpec(memory_space=pltpu.SMEM)] + [sequence_block(one.shape) for one in gets],
        out_specs=[sequence_block(gets[0].shape)] * 2 + [step_block(64, wide), step_block(1, wide)],
        out_shape=[jax.ShapeDtypeStruct(gets[0].shape, BF16)] * 2
        + [
            jax.ShapeDtypeStruct((pair, 4, 64, wide), F32),
            jax.ShapeDtypeStruct((pair, 4, 1, wide), F32),
        ],
        scratch_shapes=[
            pltpu.VMEM((4, 4, rows, 128), BF16),
            pltpu.VMEM((4 * slots, rows, 128), BF16),
            pltpu.VMEM((128, wide), F32),
            pltpu.VMEM((1, wide), F32),
            pltpu.VMEM((2, slots, rows, 128), BF16),
        ],
        compiler_params=params(),
        cost_estimate=cost(32),
        name="attend",
    )(place, *gets)


def own_block(rows, width):
    return pl.BlockSpec((1, 1, rows, width), lambda s, j: (jnp.minimum(j, 1), s, 0, 0))


def near_block(rows, width):
    return pl.BlockSpec((1, 1, rows, width), lambda s, j: (jnp.maximum(j - 2, 0), s, 0, 0))


def store_share(j, own_ref, near_ref, part):
    @pl.when(j < 2)
    def _():
        own_ref[0, 0] = part

    @pl.when(j >= 2)
    def _():
        near_ref[0, 0] = part


def out_kernel(place_ref, get_own, get_other, w_ref, mixed_ref, own_ref, near_ref, head_ref):
    side, j = place_ref[1] & 1, pl.program_id(1)
    head_ref[side] = get_own[0, 0]
    head_ref[1 - side] = get_other[0, 0]
    mixed = jnp.concatenate([head_ref[0], head_ref[1]], axis=1)
    mixed_ref[0, 0] = mixed
    store_share(j, own_ref, near_ref, dot_nt(mixed, w_ref[:, 512:]).astype(BF16))


def out_call(place, gets, w):
    pair, slots, rows, _ = gets[0].shape
    width = w.shape[0]
    return pl.pallas_call(
        out_kernel,
        grid=(pair, slots),
        in_specs=[pl.BlockSpec(memory_space=pltpu.SMEM)] + [step_block(rows, 128)] * 2 + [whole2(w.shape)],
        out_specs=[step_block(rows, 256), own_block(rows, width), near_block(rows, width)],
        out_shape=[
            jax.ShapeDtypeStruct((pair, slots, rows, 256), BF16),
            jax.ShapeDtypeStruct((2, pair, rows, width), BF16),
            jax.ShapeDtypeStruct((2, pair, rows, width), BF16),
        ],
        scratch_shapes=[pltpu.VMEM((2, rows, 128), BF16)],
        compiler_params=params(),
        cost_estimate=cost(9),
        name="out",
    )(place, *gets, w)


def out_back_kernel(place_ref, *refs):
    x_refs, w_ref, own_out, other_out, x_ref, send_ref, sems = refs[0:4], *refs[4:]
    side, j = place_ref[1] & 1, pl.program_id(0)
    start_slots(x_refs, x_ref, sems)
    wait_slot(x_refs, x_ref, sems)
    back = dot_nn(x_ref[j], w_ref[:, 512:]).astype(BF16)
    send_ref[0] = back[:, :128]
    send_ref[1] = back[:, 128:]
    own_out[0] = send_ref[side]
    other_out[0] = send_ref[1 - side]


def out_back_call(place, xs, w):
    slots = len(xs)
    rows, width = xs[0].shape
    return pl.pallas_call(
        out_back_kernel,
        grid=(slots,),
        in_specs=[pl.BlockSpec(memory_space=pltpu.SMEM)]
        + [pl.BlockSpec(memory_space=pl.ANY)] * slots
        + [whole(w.shape)],
        out_specs=[pl.BlockSpec((1, rows, 128), lambda j: (j, 0, 0))] * 2,
        out_shape=[jax.ShapeDtypeStruct((slots, rows, 128), BF16)] * 2,
        scratch_shapes=[
            pltpu.VMEM((slots, rows, width), BF16),
            pltpu.VMEM((2, rows, 128), BF16),
            pltpu.SemaphoreType.DMA((slots,)),
        ],
        compiler_params=params(),
        cost_estimate=cost(4),
        name="out_back",
    )(place, *xs, w)


def attend_back_kernel(place_ref, *refs):
    q_own, keys, back_own, back_got = refs[0], refs[1:5], refs[5], refs[6]
    o_ref, lse_ref = refs[7], refs[8]
    own_out, outs = refs[-11], refs[-10:-6]
    q_ref, kv_ref, back_ref, dkv_ref, acc_ref, ret_ref = refs[-6:]
    c, t, g = place_ref[0], place_ref[1], pl.program_id(0)
    side, base = t & 1, t & 2
    rows = kv_ref.shape[1]
    half, wide = 2 * rows, 4 * rows

    @pl.when(g == 0)
    def _():
        lay_keys(place_ref, keys, kv_ref)
        lay_rows(place_ref, q_own, keys[1], q_ref, False)
        lay_rows(place_ref, back_own, back_got, back_ref, True)
        dkv_ref[...] = jnp.zeros_like(dkv_ref)

    queries = q_ref[g].reshape(wide, 128)
    given = back_ref[g].reshape(wide, 128)
    delta = jnp.sum(jnp.transpose(given.astype(F32))[64:] * o_ref[0, 0], axis=0, keepdims=True)
    lse = lse_ref[0, 0]
    acc_ref[...] = jnp.zeros_like(acc_ref)

    def block(pair, skip, allowed):
        probs = jnp.exp2(dot_nt(pair, queries[skip:]) * LOG2E - lse[:, skip:])
        if allowed is not None:
            probs = jnp.where(allowed, probs, 0.0)
        slopes = dot_nt(pair, given[skip:])
        score_back = (probs * (slopes - delta[:, skip:])).astype(BF16)
        acc_ref[skip:] += dot_tn(score_back, pair)
        return dot_nn(probs.astype(BF16), given[skip:]) + dot_nn(score_back, queries[skip:])

    def body(n, carry):
        pair = kv_ref[pl.ds(2 * n, 2)].reshape(2 * rows, 128)
        dkv_ref[pl.ds(2 * n, 2)] += block(pair, 0, None).reshape(2, rows, 128)
        return carry

    last = 4 * g + base
    lax.fori_loop(0, last >> 1, body, 0)
    dkv_ref[last] += block(kv_ref[last], 0, diagonal(rows, wide, half))
    dkv_ref[last + 1] += block(kv_ref[last + 1], half, diagonal(rows, half, half))
    low = lanes_low(rows)
    slot = swap_bits(c ^ g)
    for u in range(2):
        first, second = (acc_ref[(2 * u + h) * rows : (2 * u + h + 1) * rows] * 0.125 for h in range(2))
        ret_ref[u, slot] = pack(first, pltpu.roll(second, 64, 1), low).astype(BF16)

    @pl.when(g == pl.num_programs(0) - 1)
    def _():
        own_out[0] = ret_ref[side]
        outs[1][0, :, :rows] = ret_ref[1 - side]
        for e in range(4):
            for j in range(4):
                outs[e][0, j, outs[e].shape[2] - rows :] = dkv_ref[4 * (c ^ swap_bits(j)) + (t ^ e)].astype(BF16)


def attend_back_call(place, at, gets, backs, o, lse):
    _, slots, rows, _ = gets[0].shape
    wide = 4 * rows
    block = lambda one: pl.BlockSpec((1, *one.shape[1:]), lambda g: (at, 0, 0, 0))
    return pl.pallas_call(
        attend_back_kernel,
        grid=(4,),
        in_specs=[pl.BlockSpec(memory_space=pltpu.SMEM)]
        + [block(one) for one in gets]
        + [whole(one.shape) for one in backs]
        + [pl.BlockSpec((1, 1, tall, wide), lambda g: (at, g, 0, 0)) for tall in (64, 1)],
        out_specs=[whole((1, *one.shape[1:])) for one in gets],
        out_shape=[jax.ShapeDtypeStruct((1, *one.shape[1:]), BF16) for one in gets],
        scratch_shapes=[
            pltpu.VMEM((4, 4, rows, 128), BF16),
            pltpu.VMEM((4 * slots, rows, 128), BF16),
            pltpu.VMEM((4, 4, rows, 128), BF16),
            pltpu.VMEM((4 * slots, rows, 128), F32),
            pltpu.VMEM((wide, 128), F32),
            pltpu.VMEM((2, slots, rows, 128), BF16),
        ],
        compiler_params=params(),
        cost_estimate=cost(8),
        name="attend_back",
    )(place, *gets, *backs, o, lse)


def qkv_back_kernel(place_ref, *refs):
    q_own, keys, (raw_ref, cos_ref, sin_ref, gain_ref, w_ref) = refs[0], refs[1:5], refs[5:10]
    back_ref, own_ref, near_ref, share_ref, head_ref, pair_ref = refs[10:]
    side, j = place_ref[1] & 1, pl.program_id(0)
    rows = raw_ref.shape[2]
    head_ref[side] = q_own[0, 0].astype(F32)
    head_ref[1 - side] = keys[1][0, 0, :rows].astype(F32)
    pair_ref[side] = keys[0][0, 0].astype(F32) + keys[2][0, 0].astype(F32)
    pair_ref[1 - side] = keys[1][0, 0, rows:].astype(F32) + keys[3][0, 0].astype(F32)
    low = lanes_low(rows)
    early = (lax.broadcasted_iota(jnp.int32, (rows, 128), 1) & 32) == 0
    cosine, sine = cos_ref[0, 0], sin_ref[0, 0]

    @pl.when(j == 0)
    def _():
        share_ref[...] = jnp.zeros_like(share_ref)

    even, odd = pair_ref[0], pair_ref[1]
    key = pack(even, pltpu.roll(odd, 64, 1), low)
    value = pack(pltpu.roll(even, 64, 1), odd, low)
    outs = []
    for b, given in enumerate((head_ref[0], head_ref[1], key)):
        z = sine * given
        cotangent = given * cosine + jnp.where(early, pltpu.roll(z, 96, 1), -pltpu.roll(z, 32, 1))
        u = raw_ref[0, 0, :, b * 128 : (b + 1) * 128]
        gain = gain_ref[:, b * 128 : (b + 1) * 128]
        r = lax.rsqrt(head_sums(u * u) * (1.0 / 64.0) + EPS)
        mean = head_sums(u * gain * cotangent) * (1.0 / 64.0)
        share_ref[:, b * 128 : (b + 1) * 128] += jnp.sum(cotangent * u * r, axis=0, keepdims=True)
        outs.append((r * gain * cotangent - u * (r * r * r) * mean).astype(BF16))
    outs.append(value.astype(BF16))
    back = jnp.concatenate(outs, axis=1)
    back_ref[0, 0] = back
    store_share(j, own_ref, near_ref, dot_nt(back, w_ref[:, :512]).astype(BF16))


def qkv_back_call(place, at, gets, raw, cosine, sine, gains, w):
    _, slots, rows, _ = raw.shape
    width = w.shape[0]
    here = lambda *shape: pl.BlockSpec((1, 1, *shape), lambda j: (0, j, 0, 0))
    table = pl.BlockSpec((1, 1, rows, 128), lambda j: (j, at, 0, 0))
    return pl.pallas_call(
        qkv_back_kernel,
        grid=(slots,),
        in_specs=[pl.BlockSpec(memory_space=pltpu.SMEM)]
        + [here(*one.shape[2:]) for one in gets]
        + [pl.BlockSpec((1, 1, rows, 384), lambda j: (at, j, 0, 0)), table, table, whole((1, 384)), whole(w.shape)],
        out_specs=[
            here(rows, 512),
            pl.BlockSpec((1, 1, rows, width), lambda j: (jnp.minimum(j, 1), 0, 0, 0)),
            pl.BlockSpec((1, 1, rows, width), lambda j: (jnp.maximum(j - 2, 0), 0, 0, 0)),
            whole((1, 384)),
        ],
        out_shape=[
            jax.ShapeDtypeStruct((1, slots, rows, 512), BF16),
            jax.ShapeDtypeStruct((2, 1, rows, width), BF16),
            jax.ShapeDtypeStruct((2, 1, rows, width), BF16),
            jax.ShapeDtypeStruct((1, 384), F32),
        ],
        scratch_shapes=[pltpu.VMEM((2, rows, 128), F32), pltpu.VMEM((2, rows, 128), F32)],
        compiler_params=params(),
        cost_estimate=cost(8),
        name="qkv_back",
    )(place, *gets, raw, cosine, sine, gains, w)


def ffn_kernel(at, halves, *refs):
    offset_ref, x_refs, given_refs, pieces = refs[0], refs[1:5], refs[5:9], refs[9 : 9 + 3 * halves]
    refs = refs[-18:]
    act_out, outs = refs[0], refs[1:5]
    w_ref, x_ref, given_ref, act_ref, held = *refs[5:9], refs[9:13]
    sems, x_sems, given_sems, act_sems, out_sems = refs[13:]
    _, rows, width = x_ref.shape
    count = 2 * rows
    blocks, depth, span = pieces[0].shape

    def copies(j):
        return [
            pltpu.make_async_copy(
                pieces[j * halves + p].at[i],
                w_ref.at[j, pl.ds(i * depth, depth), pl.ds(pl.multiple_of(offset_ref[p], 128), span)],
                sems.at[j, p, i],
            )
            for p in range(halves)
            for i in range(blocks)
        ]

    def start(found):
        for copy in found:
            copy.start()

    def wait(found):
        for copy in found:
            copy.wait()

    tokens = slot_copies([ref.at[at] for ref in x_refs], x_ref, x_sems)
    givens = slot_copies([ref.at[at] for ref in given_refs], given_ref, given_sems)
    for found in (tokens[:2], copies(0), copies(1), copies(2), givens[:2], tokens[2:], givens[2:]):
        start(found)
    leaving = []

    def leave(source, target, sem):
        leaving.append(pltpu.make_async_copy(source, target, sem))
        leaving[-1].start()

    def leave_act(kind, k, value):
        act_ref[kind, 2 * k : 2 * k + 2] = value.reshape(2, rows, -1)
        leave(act_ref.at[kind, pl.ds(2 * k, 2)], act_out.at[kind, pl.ds(2 * k, 2)], act_sems.at[kind, k])

    def leave_part(n, value):
        held[n][...] = value.astype(BF16).reshape(2, rows, width)
        leave(held[n], outs[n].at[:, at] if n < 2 else outs[n], out_sems.at[n])

    for k in range(2):
        wait(tokens[2 * k : 2 * k + 2])
        x = x_ref[2 * k : 2 * k + 2].reshape(count, width)
        if k == 0:
            wait(copies(0))
        gate = dot_nt(x, w_ref[0])
        if k == 0:
            wait(copies(1))
        up = dot_nt(x, w_ref[1])
        sig = jax.nn.sigmoid(gate)
        swish = gate * sig
        hidden = (swish * up).astype(BF16)
        leave_act(2, k, hidden)
        if k == 0:
            wait(copies(2))
        wait(givens[2 * k : 2 * k + 2])
        hidden_back = dot_nt(given_ref[2 * k : 2 * k + 2].reshape(count, width), w_ref[2])
        gate_back = (hidden_back * up * (sig * (1.0 + gate * (1.0 - sig)))).astype(BF16)
        leave_act(0, k, gate_back)
        up_back = (hidden_back * swish).astype(BF16)
        leave_act(1, k, up_back)
        leave_part(2 + k, dot_nn(gate_back, w_ref[0]) + dot_nn(up_back, w_ref[1]))
        leave_part(k, dot_nn(hidden, w_ref[2]))
    wait(leaving)


def ffn_call(offsets, at, xs, given, pieces, before):
    pair, rows, width = xs[0].shape
    halves = len(pieces[0])
    blocks, depth, _ = pieces[0][0].shape
    hidden = blocks * depth
    part, act = (2, rows, width), (3, 4, rows, hidden)
    both = (2, pair, rows, width)
    parts = [piece for row in pieces for piece in row]
    first = 9 + len(parts)
    before = before or []
    return pl.pallas_call(
        functools.partial(ffn_kernel, at, halves),
        in_specs=[pl.BlockSpec(memory_space=pltpu.SMEM)] + [pl.BlockSpec(memory_space=pl.ANY)] * (8 + len(parts) + len(before)),
        out_specs=[pl.BlockSpec(memory_space=pl.ANY)] * 5,
        out_shape=[jax.ShapeDtypeStruct(shape, BF16) for shape in (act, both, both, part, part)],
        input_output_aliases={first + i: 1 + i for i in range(len(before))},
        scratch_shapes=[
            pltpu.VMEM((3, hidden, width), BF16),
            pltpu.VMEM((4, rows, width), BF16),
            pltpu.VMEM((4, rows, width), BF16),
            pltpu.VMEM(act, BF16),
        ]
        + [pltpu.VMEM(part, BF16)] * 4
        + [
            pltpu.SemaphoreType.DMA((3, halves, blocks)),
            pltpu.SemaphoreType.DMA((4,)),
            pltpu.SemaphoreType.DMA((4,)),
            pltpu.SemaphoreType.DMA((3, 2)),
            pltpu.SemaphoreType.DMA((4,)),
        ],
        compiler_params=params(),
        cost_estimate=cost(22),
        name="ffn",
    )(offsets, *xs, *given, *parts, *before)


def weight_kernel(halves, offset_ref, *refs):
    lefts, rights = refs[0:2], refs[2:6]
    outs, total_ref = refs[6 : 6 + halves], refs[6 + halves]
    total = 0.0
    for s, left in enumerate(lefts):
        a = left[0]
        total = total + dot_tn(a.reshape(-1, a.shape[-1]), jnp.concatenate([ref[s] for ref in rights]))
    total_ref[...] = total.astype(BF16)
    blocks, depth, span = outs[0].shape
    for p in range(halves):
        start = pl.multiple_of(offset_ref[p], 128)
        for i in range(blocks):
            outs[p][i] = total_ref[i * depth : (i + 1) * depth, pl.ds(start, span)]


def weight_call(offsets, kind, acts, rights, halves, blocks):
    units, width = acts[0].shape[-1], rights[0].shape[-1]
    unit = (1, *acts[0].shape[1:])
    part = (blocks, units // blocks, width // halves)
    return pl.pallas_call(
        functools.partial(weight_kernel, halves),
        grid=(1,),
        in_specs=[pl.BlockSpec(memory_space=pltpu.SMEM)]
        + [pl.BlockSpec(unit, lambda j: (kind, 0, 0, 0))] * 2
        + [whole(one.shape) for one in rights],
        out_specs=[whole(part)] * halves,
        out_shape=[jax.ShapeDtypeStruct(part, BF16)] * halves,
        scratch_shapes=[pltpu.VMEM((units, width), BF16)],
        compiler_params=params(),
        cost_estimate=cost(10),
        name="weight",
    )(offsets, *acts, *rights)


def small_weight_kernel(halves, near, count, place_ref, offset_ref, *refs):
    lefts, rights, outs, total_ref = refs[:count], refs[count : -halves - 1], refs[-halves - 1 : -1], refs[-1]
    t = place_ref[1]
    total = 0.0
    for s in range(2):
        a = lefts[0][s] if count == 1 else lefts[s][0]
        pieces = [ref[s] for ref in rights] if len(rights) == 4 else [ref[...] for ref in rights[4 * s : 4 * s + 4]]
        total = total + dot_tn(a.reshape(-1, a.shape[-1]), jnp.concatenate(pieces))
    total_ref[...] = total.astype(BF16)
    blocks, _, span = outs[0].shape
    for p in range(halves):
        for e in range(blocks):
            if near:
                outs[p][e] = total_ref[:, pl.ds(pl.multiple_of(offset_ref[p] + (t ^ e) * span, 128), span)]
            else:
                outs[p][e] = total_ref[:, e * span : (e + 1) * span]


def small_weight_call(place, offsets, lefts, rights, halves, blocks, near):
    rows, width = lefts[0].shape[-1], rights[0].shape[-1]
    part = (blocks, rows, width // blocks // halves)
    return pl.pallas_call(
        functools.partial(small_weight_kernel, halves, near, len(lefts)),
        in_specs=[pl.BlockSpec(memory_space=pltpu.SMEM)] * 2
        + [pl.BlockSpec(memory_space=pltpu.VMEM)] * (len(lefts) + len(rights)),
        out_specs=[pl.BlockSpec(memory_space=pltpu.VMEM)] * halves,
        out_shape=[jax.ShapeDtypeStruct(part, BF16)] * halves,
        scratch_shapes=[pltpu.VMEM((rows, width), BF16)],
        compiler_params=params(),
        cost_estimate=cost(5),
        name="small_weight",
    )(place, offsets, *lefts, *rights)


def inverse_root(values):
    return lax.rsqrt(jnp.mean(values * values, axis=-1, keepdims=True) + EPS)


def norm_back(values, root, gain, given):
    mean = jnp.mean(values * gain * given, axis=-1, keepdims=True)
    return root * gain * given - values * (root * root * root) * mean


def per_device(
    sizes,
    tokens,
    positions,
    first_gain,
    query_weight,
    key_weight,
    value_weight,
    query_gain,
    key_gain,
    output_weight,
    second_gain,
    gate_weight,
    up_weight,
    down_weight,
    upstream,
):
    shards, ctx, tp = sizes["shard"], sizes["ctx"], sizes["tp"]
    groups = ("shard", "tp")
    sequences, rows, width = tokens.shape
    head_dim = query_gain.shape[0]
    depth = query_weight.shape[0]
    units = gate_weight.shape[1]
    c, t = lax.axis_index("ctx"), lax.axis_index("tp")
    place = jnp.stack([c, t]).astype(jnp.int32)
    trade = [(i * tp + k, k * ctx + i) for i in range(ctx) for k in range(tp)]

    line = Line()
    shard = lax.axis_index("shard")
    small = jnp.concatenate([query_weight, key_weight, value_weight, output_weight.T], axis=1)
    small = lax.ppermute(small, ("ctx", "tp"), trade)
    blocks_attn = trade_tp(small, tp)
    w_attn = join_shard(blocks_attn.reshape(tp * depth, -1), shards)

    large = jnp.stack([gate_weight.T, up_weight.T, down_weight]).reshape(3, ctx, units // ctx, depth)
    large = lax.all_to_all(large, "ctx", 1, 1, tiled=True)
    large = after(large, small).transpose(0, 2, 1, 3).reshape(3, units // ctx, ctx * depth)
    aligned = depth % 128 == 0
    starts = jnp.stack([shard, 1 - shard]) if shards == 2 else jnp.zeros((2,), jnp.int32)
    starts = (starts * (width // 2)).astype(jnp.int32)

    mine = lax.dynamic_slice_in_dim(positions, t * rows, rows, 1).astype(F32)
    places = jnp.stack(gather_ctx(mine))
    freqs = jnp.exp(-math.log(THETA) * jnp.arange(0, head_dim, 2).astype(F32) / head_dim)
    angles = places[..., None] * freqs
    cosine, sine = jnp.cos(angles), jnp.sin(angles)
    cosine = jnp.concatenate([cosine] * 4, axis=-1)
    sine = jnp.concatenate([sine] * 4, axis=-1)
    gains = jnp.concatenate([jnp.tile(query_gain, 4), jnp.tile(key_gain, 2)])[None]

    x = tokens.astype(F32)
    root = inverse_root(x)
    first = (x * root * first_gain).astype(BF16)
    given = upstream.astype(F32)

    pair = range(sequences)
    first_all = gather_ctx(first)
    one = line.run(qkv_call, place, first_all, w_attn, cosine, sine, gains)
    heads, raw = exchange_heads(one[0], (one[1], one[2], one[1], one[3])), one[4]
    lines = [lax.all_gather(after(large[0], blocks_attn), "tp", axis=0, tiled=False)]
    for j in (1, 2):
        lines.append(lax.all_gather(after(large[j], *heads), "tp", axis=0, tiled=False))
    w_ffn = [gather_shard(one, shards) for one in lines]
    upstream_all = gather_ctx(after(upstream, raw))
    heads = after(heads, w_ffn[0][-1], *upstream_all)
    own, other, o, lse = line.run(attend_call, place, heads)
    own = after(own, lines[1])
    mixed, own, near = line.run(out_call, place, [own, to_tp(other, 1)], w_attn)
    mine, away = line.run(lambda got, own: add_near(own, got), lax.ppermute(near, "ctx", NEAR), own)

    def middle_of(far, mine):
        middle = x + (mine + far.astype(F32))
        middle_root = inverse_root(middle)
        return (middle * middle_root * second_gain).astype(BF16), middle, middle_root

    mine = after(mine, lines[2], w_ffn[1][-1])
    second, middle, middle_root = line.run(middle_of, lax.ppermute(away, "ctx", FAR), mine)
    seconds = gather_ctx(second)
    ffn = []
    for s in pair:
        before = ffn[-1][1:3] if ffn else None
        ffn.append(line.run(ffn_call, starts, s, seconds, upstream_all, w_ffn, before))
    out_shares = ffn[-1][1:3]

    back_rows, mixed_back_all, backs_sent = [], [], []

    def turn_back(second_back, s):
        middle_back = given[s] + norm_back(middle[s], middle_root[s], second_gain, second_back)
        return middle_back.astype(BF16), middle_back, jnp.sum(second_back * middle[s] * middle_root[s], axis=0)

    def turn(s, call, *shares):
        low, middle_back, share = line.run(lambda first, *rest: turn_back(call(first, *rest), s), *shares)
        back_rows.append(middle_back)
        mixed_back_all.append(gather_ctx(low))
        return share

    def back_out(s):
        own, other = line.run(out_back_call, place, mixed_back_all[s], w_attn)
        backs_sent.append([own, to_tp(other, 1)])

    own, near = ffn[0][3], ffn[0][4]
    shares = own[0], *(
        lax.ppermute(value, "ctx", way) for value, way in ((own[1], FAR), (near[0], NEAR), (near[1], CROSS))
    )
    second_share = turn(0, lambda *parts: sum(part.astype(F32) for part in parts), *shares)
    mine, away = line.run(lambda got, own: add_near(own, got), lax.ppermute(ffn[1][4], "ctx", NEAR), ffn[1][3])
    away = lax.ppermute(away, "ctx", FAR)
    near = aligned and shards == 2
    count = shards * tp
    small = 2 if near else 1, tp if near else 1, near
    halves = 2 if shards == 2 else 1
    sums, g_ffn = [], []

    def weight(kind):
        rights = upstream_all if kind == 2 else seconds
        sums.append(line.run(weight_call, starts, kind, [one[0] for one in ffn], rights, halves, tp))

    def send(kind):
        parts = sums[kind]
        return send_shard(after(parts, g_ffn[-1]) if g_ffn else parts, shards)

    def add(kind, moved):
        added = line.run(add_shard, moved, sums[kind])
        sums[kind] = added
        g_ffn.append(added)

    def scatter(kind):
        return lax.psum_scatter(g_ffn[kind], "tp", scatter_dimension=0, tiled=False)

    weight(0)
    moved = send(0)
    weight(1)
    back_out(0)
    second_share = second_share + turn(1, lambda far, own: own + far.astype(F32), away, mine)
    weight(2)
    back_out(1)
    add(0, moved)
    moved = send(1)
    near_sum, away = line.run(
        lambda got, own: add_near(own, got), lax.ppermute(after(out_shares[1], backs_sent[0]), "ctx", NEAR), out_shares[0]
    )
    far_sum = lax.ppermute(away, "ctx", FAR)
    half = line.run(attend_back_call, after(place, *backs_sent[1]), 0, heads, backs_sent[0], o, lse)
    got = [exchange_heads(half[0], half[1:])]
    given_all = [*mixed_back_all[0], *mixed_back_all[1]]
    out_parts = line.run(small_weight_call, place, starts, [mixed], given_all, *small)
    out_moved = lax.ppermute(out_parts[1], "shard", [(0, 1), (1, 0)]) if near else None
    add(1, moved)
    moved = send(2)
    result = line.run(lambda far, mine: ((middle + mine) + far.astype(F32)).astype(BF16), far_sum, near_sum)
    full = line.run(attend_back_call, place, 1, heads, backs_sent[1], o, lse)
    got.append(exchange_heads(full[0], full[1:]))
    add(2, moved)
    g_ffn = [scatter(kind) for kind in range(3)]
    def last(far, mine, s):
        first_back = mine[0] + far[0].astype(F32)
        gradient = back_rows[s] + norm_back(x[s], root[s], first_gain, first_back)
        return jnp.sum(first_back * x[s] * root[s], axis=0), gradient

    backs, firsts, head_share, first_share, gradients = [], [], 0.0, 0.0, []
    for s in pair:
        back, own, other, share = line.run(qkv_back_call, place, s, got[s], raw, cosine, sine, gains, w_attn)
        backs.append(back)
        head_share = head_share + share
        other = lax.ppermute(other, "ctx", NEAR)
        if s == 0:
            mine, away = line.run(lambda got, own: add_near(own, got), other, own)
            firsts.append((lax.ppermute(away, "ctx", FAR), mine))
    parts = line.run(small_weight_call, place, starts, backs, first_all, *small)
    moved = lax.ppermute(parts[1], "shard", [(0, 1), (1, 0)]) if near else None
    mine, away = line.run(lambda got, own: add_near(own, got), other, own)
    firsts.append((lax.ppermute(away, "ctx", FAR), mine))
    for s in pair:
        share, gradient = line.run(lambda a, b: last(a, b, s), *firsts[s])
        first_share = first_share + share
        gradients.append(gradient)
    shares = jnp.concatenate([first_share, second_share, head_share[0]])
    shares = sum_all(shares, [(name, sizes[name]) for name in ("ctx", "shard", "tp")])

    if near:
        both = lambda a, b: (a.astype(F32) + b.astype(F32)).astype(BF16)
        g_attn = line.run(
            lambda a, b: jnp.concatenate([both(a, b), both(out_moved, out_parts[0])], axis=1), moved, parts[0]
        )
        g_attn = exchange_tp([g_attn[e] for e in range(tp)])
    else:
        g_attn = jnp.concatenate([parts[0][0], out_parts[0][0]])
        g_attn = g_attn.reshape(-1, count, width // count).transpose(1, 0, 2)
        g_attn = lax.psum_scatter(g_attn, groups, scatter_dimension=0, tiled=False)
    def settle(g):
        g = g.reshape(3, units, depth).astype(F32)
        return g[0].T, g[1].T, g[2]

    g_ffn = jnp.stack(g_ffn).reshape(3, units // ctx, ctx, depth).transpose(0, 2, 1, 3)
    g_ffn = lax.all_to_all(g_ffn, "ctx", 1, 1, tiled=True)
    g_ffn = line.run(settle, g_ffn)

    if near:
        g_attn = line.run(lambda *parts: sum(part.astype(F32) for part in parts).astype(BF16), *g_attn)
    g_attn = lax.ppermute(g_attn, ("ctx", "tp"), trade).astype(F32)
    heads_end = query_weight.shape[1]
    pairs = key_weight.shape[1]

    head_total = shares[2 * width :]
    return (
        result,
        jnp.stack(gradients),
        g_attn[:heads_end].T,
        g_attn[heads_end : heads_end + pairs].T,
        g_attn[heads_end + pairs : heads_end + 2 * pairs].T,
        g_attn[heads_end + 2 * pairs :],
        *g_ffn,
        shares[:width],
        shares[width : 2 * width],
        jnp.sum(head_total[: 4 * head_dim].reshape(4, head_dim), axis=0),
        jnp.sum(head_total[4 * head_dim :].reshape(2, head_dim), axis=0),
    )


def solution(mesh):
    rows = P("shard", ("ctx", "tp"), None)
    wide = P(("shard", "ctx"), "tp")
    tall = P("tp", ("shard", "ctx"))
    none = P()
    in_specs = (
        rows, P("shard", "ctx"), none, wide, wide, wide, none, none, tall, none, wide, wide, tall, rows,
    )
    out_specs = (rows, rows, wide, wide, wide, tall, wide, wide, tall, none, none, none, none)
    sizes = {name: mesh.shape[name] for name in ("shard", "ctx", "tp")}
    return jax.shard_map(
        functools.partial(per_device, sizes), mesh=mesh, in_specs=in_specs, out_specs=out_specs, check_vma=False
    )
```

```python
import functools
import math

import jax
import jax.numpy as jnp
from jax import lax
from jax.experimental import pallas as pl
from jax.experimental.pallas import tpu as pltpu
from jax.sharding import PartitionSpec as P

EPS = 1e-05
THETA = 1000000.0
LOG2E = 1.4426950408889634
F32 = jnp.float32
BF16 = jnp.bfloat16
NEAR = [(0, 1), (1, 0), (2, 3), (3, 2)]
FAR = [(0, 2), (2, 0), (1, 3), (3, 1)]
CROSS = [(0, 3), (3, 0), (1, 2), (2, 1)]
LIMIT = 56 * 1024 * 1024


def dot_nn(left, right):
    return lax.dot_general(left, right, (((1,), (0,)), ((), ())), preferred_element_type=F32)


def dot_nt(left, right):
    return lax.dot_general(left, right, (((1,), (1,)), ((), ())), preferred_element_type=F32)


def dot_tn(left, right):
    return lax.dot_general(left, right, (((0,), (0,)), ((), ())), preferred_element_type=F32)


def swap_bits(j):
    return ((j & 1) << 1) | (j >> 1)


def gather_ctx(own):
    far = lax.ppermute(own, "ctx", FAR)
    near = lax.ppermute(own, "ctx", NEAR)
    return [own, far, near, lax.ppermute(far, "ctx", NEAR)]


def add_near(own, got):
    return own[0].astype(F32) + got[0].astype(F32), (own[1].astype(F32) + got[1].astype(F32)).astype(BF16)


def reduce_near(own, near):
    return add_near(own, lax.ppermute(near, "ctx", NEAR))


def reduce_far(mine, away):
    return mine + lax.ppermute(away, "ctx", FAR).astype(F32)


def reduce_ctx(own, near):
    got = lax.ppermute(own[1], "ctx", FAR), lax.ppermute(near[0], "ctx", NEAR), lax.ppermute(near[1], "ctx", CROSS)
    return own[0].astype(F32) + got[0].astype(F32) + got[1].astype(F32) + got[2].astype(F32)


def to_tp(value, e):
    return lax.ppermute(value, "tp", [(i, i ^ e) for i in range(4)])


def exchange_tp(blocks):
    return [blocks[0]] + [to_tp(blocks[e], e) for e in range(1, len(blocks))]


def exchange_heads(q_same, kv):
    return [q_same, *exchange_tp(kv)]


def gather_shard(own, shards):
    if shards == 2:
        return [own, lax.ppermute(own, "shard", [(0, 1), (1, 0)])]
    every = lax.all_gather(own, "shard", axis=0, tiled=False)
    return [every.transpose(1, 2, 0, 3).reshape(*own.shape[:2], -1)]


def send_shard(parts, shards):
    if shards == 2:
        return lax.ppermute(parts[1], "shard", [(0, 1), (1, 0)])
    blocks, units, width = parts[0].shape
    every = parts[0].reshape(blocks, units, shards, width // shards).transpose(2, 0, 1, 3)
    return lax.psum_scatter(every, "shard", scatter_dimension=0, tiled=False)


def add_shard(got, parts):
    return (parts[0].astype(F32) + got.astype(F32)).astype(BF16) if len(parts) == 2 else got


def after(value, *others):
    return lax.optimization_barrier((value, *others))[0]


class Line:
    def __init__(self):
        self.last = ()

    def run(self, call, first, *others):
        result = call(after(first, *self.last), *others)
        self.last = (jax.tree.leaves(result)[0],)
        return result


def trade_tp(own, count):
    got = [own]
    for k in range(1, count):
        got.append(lax.ppermute(own, "tp", [(i, i ^ k) for i in range(count)]))
    index = lax.axis_index("tp")
    slots = []
    for slot in range(count):
        value = got[slot]
        for at in range(1, count):
            value = jnp.where(index == at, got[slot ^ at], value)
        slots.append(value)
    return jnp.stack(slots)


def join_shard(own, shards):
    if shards == 2:
        other = lax.ppermute(own, "shard", [(0, 1), (1, 0)])
        index = lax.axis_index("shard")
        return jnp.concatenate([jnp.where(index == 0, own, other), jnp.where(index == 0, other, own)])
    return lax.all_gather(own, "shard", axis=0, tiled=True)


def sum_all(vector, sizes):
    for name, size in sizes:
        step = 1
        while step < size:
            other = lax.ppermute(vector, name, [(i, i ^ step) for i in range(size)])
            vector = vector + other
            step *= 2
    return vector


def params():
    return pltpu.CompilerParams(vmem_limit_bytes=LIMIT)


def cost(micros):
    return pl.CostEstimate(flops=int(micros * 1.0e9), transcendentals=0, bytes_accessed=int(micros * 1.0e6))


def slot_copies(refs, held, sems):
    return [pltpu.make_async_copy(ref, held.at[k], sems.at[k]) for k, ref in enumerate(refs)]


def start_slots(refs, held, sems):
    @pl.when(pl.program_id(0) == 0)
    def _():
        for copy in slot_copies(refs, held, sems):
            copy.start()


def wait_slot(refs, held, sems, step=1):
    for k, copy in enumerate(slot_copies(refs, held, sems)):

        @pl.when(pl.program_id(0) == k // step)
        def _():
            copy.wait()


def lanes_low(rows):
    return lax.broadcasted_iota(jnp.int32, (rows, 128), 1) < 64


def pack(first, second, low):
    return jnp.where(low, first, second)


def head_sums(values):
    rows = lax.broadcasted_iota(jnp.int32, (128, 128), 0) >> 6
    columns = lax.broadcasted_iota(jnp.int32, (128, 128), 1) >> 6
    ones = jnp.where(rows == columns, 1.0, 0.0).astype(BF16)
    high = values.astype(BF16)
    rest = values - high.astype(F32)
    low = rest.astype(BF16)
    return dot_nn(high, ones) + dot_nn(low, ones)


def qkv_kernel(place_ref, *refs):
    x_refs, (w_ref, cos_ref, sin_ref, gain_ref) = refs[:4], refs[4:8]
    q_same, kv_same, beside, kv_other, raw_ref, x_ref, q_ref, kv_ref, sems = refs[8:]
    side, s, j = place_ref[1] & 1, pl.program_id(0), pl.program_id(1)
    rows = x_ref.shape[2]
    copies = slot_copies(x_refs, x_ref, sems)

    @pl.when((s == 0) & (j == 0))
    def _():
        for copy in copies:
            copy.start()

    for k, copy in enumerate(copies):

        @pl.when((s == 0) & (j == k))
        def _():
            copy.wait()

    y = dot_nn(x_ref[j, s], w_ref[:, :512])
    raw_ref[0, 0] = y[:, :384]
    low = lanes_low(rows)
    early = (lax.broadcasted_iota(jnp.int32, (rows, 128), 1) & 32) == 0
    cosine, sine = cos_ref[0, 0], sin_ref[0, 0]
    turned = []
    for b in range(3):
        u = y[:, b * 128 : (b + 1) * 128]
        r = lax.rsqrt(head_sums(u * u) * (1.0 / 64.0) + EPS)
        n = u * r * gain_ref[:, b * 128 : (b + 1) * 128]
        other = jnp.where(early, -pltpu.roll(n, 96, 1), pltpu.roll(n, 32, 1))
        turned.append(n * cosine + other * sine)
    key, value = turned[2], y[:, 384:512]
    q_ref[0] = (turned[0] * 0.125).astype(BF16)
    q_ref[1] = (turned[1] * 0.125).astype(BF16)
    kv_ref[0] = pack(key, pltpu.roll(value, 64, 1), low).astype(BF16)
    kv_ref[1] = pack(pltpu.roll(key, 64, 1), value, low).astype(BF16)
    q_same[0, 0] = q_ref[side]
    kv_same[0, 0] = kv_ref[side]
    beside[0, 0, :rows] = q_ref[1 - side]
    beside[0, 0, rows:] = kv_ref[1 - side]
    kv_other[0, 0] = kv_ref[1 - side]


def step_block(*shape):
    return pl.BlockSpec((1, 1, *shape), lambda s, j: (s, j, 0, 0))


def table_block(*shape):
    return pl.BlockSpec((1, 1, *shape), lambda s, j: (j, s, 0, 0))


def whole2(shape):
    return pl.BlockSpec(shape, lambda s, j: (0,) * len(shape))


def qkv_call(place, xs, w, cosine, sine, gains):
    slots = len(xs)
    pair, rows, width = xs[0].shape
    talls = (rows, rows, 2 * rows, rows)
    return pl.pallas_call(
        qkv_kernel,
        grid=(pair, slots),
        in_specs=[pl.BlockSpec(memory_space=pltpu.SMEM)]
        + [pl.BlockSpec(memory_space=pl.ANY)] * slots
        + [whole2(w.shape), table_block(rows, 128), table_block(rows, 128), whole2((1, 384))],
        out_specs=[step_block(tall, 128) for tall in talls] + [step_block(rows, 384)],
        out_shape=[jax.ShapeDtypeStruct((pair, slots, tall, 128), BF16) for tall in talls]
        + [jax.ShapeDtypeStruct((pair, slots, rows, 384), F32)],
        scratch_shapes=[
            pltpu.VMEM((slots, pair, rows, width), BF16),
            pltpu.VMEM((2, rows, 128), BF16),
            pltpu.VMEM((2, rows, 128), BF16),
            pltpu.SemaphoreType.DMA((slots,)),
        ],
        compiler_params=params(),
        cost_estimate=cost(15),
        name="qkv",
    )(place, *xs, w, cosine, sine, gains)


def lay_keys(place_ref, refs, kv_ref):
    c, t = place_ref[0], place_ref[1]
    for e, ref in enumerate(refs):
        for j in range(ref.shape[1]):
            kv_ref[4 * (c ^ swap_bits(j)) + (t ^ e)] = ref[0, j, ref.shape[2] - kv_ref.shape[1] :]


def lay_rows(place_ref, own_ref, got_ref, out_ref, high):
    c, side = place_ref[0], place_ref[1] & 1
    rows = out_ref.shape[2]
    low = lanes_low(rows)
    for ref, start in ((own_ref, 2 * side), (got_ref, 2 - 2 * side)):
        for j in range(4):
            g = c ^ swap_bits(j)
            value = ref[0, j, :rows] if len(ref.shape) == 4 else ref[j, :rows]
            turned = pltpu.roll(value, 64, 1)
            zero = jnp.zeros_like(value)
            if high:
                out_ref[g, start] = jnp.where(low, zero, turned)
                out_ref[g, start + 1] = jnp.where(low, zero, value)
            else:
                out_ref[g, start] = jnp.where(low, value, zero)
                out_ref[g, start + 1] = jnp.where(low, turned, zero)


def diagonal(rows, wide, edge):
    key = lax.broadcasted_iota(jnp.int32, (rows, wide), 0)
    column = lax.broadcasted_iota(jnp.int32, (rows, wide), 1)
    return (key <= (column & (rows - 1))) | (column >= edge)


def whole(shape):
    return pl.BlockSpec(shape, lambda j: (0,) * len(shape))


def attend_kernel(place_ref, *refs):
    q_own, keys = refs[0], refs[1:5]
    own_out, other_out, o_ref, lse_ref, q_ref, kv_ref, acc_ref, sum_ref, ret_ref = refs[5:]
    c, t, g = place_ref[0], place_ref[1], pl.program_id(1)
    side, base = t & 1, t & 2
    rows = kv_ref.shape[1]
    half, wide = 2 * rows, 4 * rows

    @pl.when(g == 0)
    def _():
        lay_keys(place_ref, keys, kv_ref)
        lay_rows(place_ref, q_own, keys[1], q_ref, False)

    queries = q_ref[g].reshape(wide, 128)
    acc_ref[...] = jnp.zeros_like(acc_ref)
    sum_ref[...] = jnp.zeros_like(sum_ref)

    def add(pair, skip, allowed):
        weights = jnp.exp2(dot_nt(pair, queries[skip:]) * LOG2E)
        if allowed is not None:
            weights = jnp.where(allowed, weights, 0.0)
        sum_ref[:, skip:] += jnp.sum(weights, axis=0, keepdims=True)
        acc_ref[:, skip:] += dot_tn(pair, weights.astype(BF16))

    def body(n, carry):
        add(kv_ref[pl.ds(2 * n, 2)].reshape(2 * rows, 128), 0, None)
        return carry

    last = 4 * g + base
    lax.fori_loop(0, last >> 1, body, 0)
    add(kv_ref[last], 0, diagonal(rows, wide, half))
    add(kv_ref[last + 1], half, diagonal(rows, half, half))
    total = sum_ref[...]
    out = acc_ref[...] / total
    o_ref[0, 0] = out[64:]
    lse_ref[0, 0] = jnp.log(total) * LOG2E
    flat = jnp.transpose(out)
    low = lanes_low(rows)
    slot = swap_bits(c ^ g)
    for u in range(2):
        first, second = (flat[(2 * u + h) * rows : (2 * u + h + 1) * rows] for h in range(2))
        ret_ref[u, slot] = pack(pltpu.roll(first, 64, 1), second, low).astype(BF16)

    @pl.when(g == 3)
    def _():
        own_out[0] = ret_ref[side]
        other_out[0] = ret_ref[1 - side]


def sequence_block(shape):
    return pl.BlockSpec((1, *shape[1:]), lambda s, j: (s, 0, 0, 0))


def attend_call(place, gets):
    pair, slots, rows, _ = gets[0].shape
    wide = 4 * rows
    return pl.pallas_call(
        attend_kernel,
        grid=(pair, 4),
        in_specs=[pl.BlockSpec(memory_space=pltpu.SMEM)] + [sequence_block(one.shape) for one in gets],
        out_specs=[sequence_block(gets[0].shape)] * 2 + [step_block(64, wide), step_block(1, wide)],
        out_shape=[jax.ShapeDtypeStruct(gets[0].shape, BF16)] * 2
        + [
            jax.ShapeDtypeStruct((pair, 4, 64, wide), F32),
            jax.ShapeDtypeStruct((pair, 4, 1, wide), F32),
        ],
        scratch_shapes=[
            pltpu.VMEM((4, 4, rows, 128), BF16),
            pltpu.VMEM((4 * slots, rows, 128), BF16),
            pltpu.VMEM((128, wide), F32),
            pltpu.VMEM((1, wide), F32),
            pltpu.VMEM((2, slots, rows, 128), BF16),
        ],
        compiler_params=params(),
        cost_estimate=cost(32),
        name="attend",
    )(place, *gets)


def own_block(rows, width):
    return pl.BlockSpec((1, 1, rows, width), lambda s, j: (jnp.minimum(j, 1), s, 0, 0))


def near_block(rows, width):
    return pl.BlockSpec((1, 1, rows, width), lambda s, j: (jnp.maximum(j - 2, 0), s, 0, 0))


def store_share(j, own_ref, near_ref, part):
    @pl.when(j < 2)
    def _():
        own_ref[0, 0] = part

    @pl.when(j >= 2)
    def _():
        near_ref[0, 0] = part


def out_kernel(place_ref, get_own, get_other, w_ref, mixed_ref, own_ref, near_ref, head_ref):
    side, j = place_ref[1] & 1, pl.program_id(1)
    head_ref[side] = get_own[0, 0]
    head_ref[1 - side] = get_other[0, 0]
    mixed = jnp.concatenate([head_ref[0], head_ref[1]], axis=1)
    mixed_ref[0, 0] = mixed
    store_share(j, own_ref, near_ref, dot_nt(mixed, w_ref[:, 512:]).astype(BF16))


def out_call(place, gets, w):
    pair, slots, rows, _ = gets[0].shape
    width = w.shape[0]
    return pl.pallas_call(
        out_kernel,
        grid=(pair, slots),
        in_specs=[pl.BlockSpec(memory_space=pltpu.SMEM)] + [step_block(rows, 128)] * 2 + [whole2(w.shape)],
        out_specs=[step_block(rows, 256), own_block(rows, width), near_block(rows, width)],
        out_shape=[
            jax.ShapeDtypeStruct((pair, slots, rows, 256), BF16),
            jax.ShapeDtypeStruct((2, pair, rows, width), BF16),
            jax.ShapeDtypeStruct((2, pair, rows, width), BF16),
        ],
        scratch_shapes=[pltpu.VMEM((2, rows, 128), BF16)],
        compiler_params=params(),
        cost_estimate=cost(9),
        name="out",
    )(place, *gets, w)


def out_back_kernel(place_ref, *refs):
    x_refs, w_ref, own_out, other_out, x_ref, send_ref, sems = refs[0:4], *refs[4:]
    side, j = place_ref[1] & 1, pl.program_id(0)
    start_slots(x_refs, x_ref, sems)
    wait_slot(x_refs, x_ref, sems)
    back = dot_nn(x_ref[j], w_ref[:, 512:]).astype(BF16)
    send_ref[0] = back[:, :128]
    send_ref[1] = back[:, 128:]
    own_out[0] = send_ref[side]
    other_out[0] = send_ref[1 - side]


def out_back_call(place, xs, w):
    slots = len(xs)
    rows, width = xs[0].shape
    return pl.pallas_call(
        out_back_kernel,
        grid=(slots,),
        in_specs=[pl.BlockSpec(memory_space=pltpu.SMEM)]
        + [pl.BlockSpec(memory_space=pl.ANY)] * slots
        + [whole(w.shape)],
        out_specs=[pl.BlockSpec((1, rows, 128), lambda j: (j, 0, 0))] * 2,
        out_shape=[jax.ShapeDtypeStruct((slots, rows, 128), BF16)] * 2,
        scratch_shapes=[
            pltpu.VMEM((slots, rows, width), BF16),
            pltpu.VMEM((2, rows, 128), BF16),
            pltpu.SemaphoreType.DMA((slots,)),
        ],
        compiler_params=params(),
        cost_estimate=cost(4),
        name="out_back",
    )(place, *xs, w)


def attend_back_kernel(place_ref, *refs):
    q_own, keys, back_own, back_got = refs[0], refs[1:5], refs[5], refs[6]
    o_ref, lse_ref = refs[7], refs[8]
    own_out, outs = refs[-11], refs[-10:-6]
    q_ref, kv_ref, back_ref, dkv_ref, acc_ref, ret_ref = refs[-6:]
    c, t, g = place_ref[0], place_ref[1], pl.program_id(0)
    side, base = t & 1, t & 2
    rows = kv_ref.shape[1]
    half, wide = 2 * rows, 4 * rows

    @pl.when(g == 0)
    def _():
        lay_keys(place_ref, keys, kv_ref)
        lay_rows(place_ref, q_own, keys[1], q_ref, False)
        lay_rows(place_ref, back_own, back_got, back_ref, True)
        dkv_ref[...] = jnp.zeros_like(dkv_ref)

    queries = q_ref[g].reshape(wide, 128)
    given = back_ref[g].reshape(wide, 128)
    delta = jnp.sum(jnp.transpose(given.astype(F32))[64:] * o_ref[0, 0], axis=0, keepdims=True)
    lse = lse_ref[0, 0]
    acc_ref[...] = jnp.zeros_like(acc_ref)

    def block(pair, skip, allowed):
        probs = jnp.exp2(dot_nt(pair, queries[skip:]) * LOG2E - lse[:, skip:])
        if allowed is not None:
            probs = jnp.where(allowed, probs, 0.0)
        slopes = dot_nt(pair, given[skip:])
        score_back = (probs * (slopes - delta[:, skip:])).astype(BF16)
        acc_ref[skip:] += dot_tn(score_back, pair)
        return dot_nn(probs.astype(BF16), given[skip:]) + dot_nn(score_back, queries[skip:])

    def body(n, carry):
        pair = kv_ref[pl.ds(2 * n, 2)].reshape(2 * rows, 128)
        dkv_ref[pl.ds(2 * n, 2)] += block(pair, 0, None).reshape(2, rows, 128)
        return carry

    last = 4 * g + base
    lax.fori_loop(0, last >> 1, body, 0)
    dkv_ref[last] += block(kv_ref[last], 0, diagonal(rows, wide, half))
    dkv_ref[last + 1] += block(kv_ref[last + 1], half, diagonal(rows, half, half))
    low = lanes_low(rows)
    slot = swap_bits(c ^ g)
    for u in range(2):
        first, second = (acc_ref[(2 * u + h) * rows : (2 * u + h + 1) * rows] * 0.125 for h in range(2))
        ret_ref[u, slot] = pack(first, pltpu.roll(second, 64, 1), low).astype(BF16)

    @pl.when(g == pl.num_programs(0) - 1)
    def _():
        own_out[0] = ret_ref[side]
        outs[1][0, :, :rows] = ret_ref[1 - side]
        for e in range(4):
            for j in range(4):
                outs[e][0, j, outs[e].shape[2] - rows :] = dkv_ref[4 * (c ^ swap_bits(j)) + (t ^ e)].astype(BF16)


def attend_back_call(place, at, gets, backs, o, lse):
    _, slots, rows, _ = gets[0].shape
    wide = 4 * rows
    block = lambda one: pl.BlockSpec((1, *one.shape[1:]), lambda g: (at, 0, 0, 0))
    return pl.pallas_call(
        attend_back_kernel,
        grid=(4,),
        in_specs=[pl.BlockSpec(memory_space=pltpu.SMEM)]
        + [block(one) for one in gets]
        + [whole(one.shape) for one in backs]
        + [pl.BlockSpec((1, 1, tall, wide), lambda g: (at, g, 0, 0)) for tall in (64, 1)],
        out_specs=[whole((1, *one.shape[1:])) for one in gets],
        out_shape=[jax.ShapeDtypeStruct((1, *one.shape[1:]), BF16) for one in gets],
        scratch_shapes=[
            pltpu.VMEM((4, 4, rows, 128), BF16),
            pltpu.VMEM((4 * slots, rows, 128), BF16),
            pltpu.VMEM((4, 4, rows, 128), BF16),
            pltpu.VMEM((4 * slots, rows, 128), F32),
            pltpu.VMEM((wide, 128), F32),
            pltpu.VMEM((2, slots, rows, 128), BF16),
        ],
        compiler_params=params(),
        cost_estimate=cost(8),
        name="attend_back",
    )(place, *gets, *backs, o, lse)


def qkv_back_kernel(place_ref, *refs):
    q_own, keys, (raw_ref, cos_ref, sin_ref, gain_ref, w_ref) = refs[0], refs[1:5], refs[5:10]
    back_ref, own_ref, near_ref, share_ref, head_ref, pair_ref = refs[10:]
    side, j = place_ref[1] & 1, pl.program_id(0)
    rows = raw_ref.shape[2]
    head_ref[side] = q_own[0, 0].astype(F32)
    head_ref[1 - side] = keys[1][0, 0, :rows].astype(F32)
    pair_ref[side] = keys[0][0, 0].astype(F32) + keys[2][0, 0].astype(F32)
    pair_ref[1 - side] = keys[1][0, 0, rows:].astype(F32) + keys[3][0, 0].astype(F32)
    low = lanes_low(rows)
    early = (lax.broadcasted_iota(jnp.int32, (rows, 128), 1) & 32) == 0
    cosine, sine = cos_ref[0, 0], sin_ref[0, 0]

    @pl.when(j == 0)
    def _():
        share_ref[...] = jnp.zeros_like(share_ref)

    even, odd = pair_ref[0], pair_ref[1]
    key = pack(even, pltpu.roll(odd, 64, 1), low)
    value = pack(pltpu.roll(even, 64, 1), odd, low)
    outs = []
    for b, given in enumerate((head_ref[0], head_ref[1], key)):
        z = sine * given
        cotangent = given * cosine + jnp.where(early, pltpu.roll(z, 96, 1), -pltpu.roll(z, 32, 1))
        u = raw_ref[0, 0, :, b * 128 : (b + 1) * 128]
        gain = gain_ref[:, b * 128 : (b + 1) * 128]
        r = lax.rsqrt(head_sums(u * u) * (1.0 / 64.0) + EPS)
        mean = head_sums(u * gain * cotangent) * (1.0 / 64.0)
        share_ref[:, b * 128 : (b + 1) * 128] += jnp.sum(cotangent * u * r, axis=0, keepdims=True)
        outs.append((r * gain * cotangent - u * (r * r * r) * mean).astype(BF16))
    outs.append(value.astype(BF16))
    back = jnp.concatenate(outs, axis=1)
    back_ref[0, 0] = back
    store_share(j, own_ref, near_ref, dot_nt(back, w_ref[:, :512]).astype(BF16))


def qkv_back_call(place, at, gets, raw, cosine, sine, gains, w):
    _, slots, rows, _ = raw.shape
    width = w.shape[0]
    here = lambda *shape: pl.BlockSpec((1, 1, *shape), lambda j: (0, j, 0, 0))
    table = pl.BlockSpec((1, 1, rows, 128), lambda j: (j, at, 0, 0))
    return pl.pallas_call(
        qkv_back_kernel,
        grid=(slots,),
        in_specs=[pl.BlockSpec(memory_space=pltpu.SMEM)]
        + [here(*one.shape[2:]) for one in gets]
        + [pl.BlockSpec((1, 1, rows, 384), lambda j: (at, j, 0, 0)), table, table, whole((1, 384)), whole(w.shape)],
        out_specs=[
            here(rows, 512),
            pl.BlockSpec((1, 1, rows, width), lambda j: (jnp.minimum(j, 1), 0, 0, 0)),
            pl.BlockSpec((1, 1, rows, width), lambda j: (jnp.maximum(j - 2, 0), 0, 0, 0)),
            whole((1, 384)),
        ],
        out_shape=[
            jax.ShapeDtypeStruct((1, slots, rows, 512), BF16),
            jax.ShapeDtypeStruct((2, 1, rows, width), BF16),
            jax.ShapeDtypeStruct((2, 1, rows, width), BF16),
            jax.ShapeDtypeStruct((1, 384), F32),
        ],
        scratch_shapes=[pltpu.VMEM((2, rows, 128), F32), pltpu.VMEM((2, rows, 128), F32)],
        compiler_params=params(),
        cost_estimate=cost(8),
        name="qkv_back",
    )(place, *gets, raw, cosine, sine, gains, w)


def ffn_kernel(at, halves, *refs):
    offset_ref, x_refs, given_refs, pieces = refs[0], refs[1:5], refs[5:9], refs[9 : 9 + 3 * halves]
    refs = refs[-16:]
    act_out, outs = refs[0], refs[1:5]
    w_ref, x_ref, given_ref, act_ref, held = *refs[5:9], refs[9:11]
    sems, x_sems, given_sems, act_sems, out_sems = refs[11:]
    _, rows, width = x_ref.shape
    count = 2 * rows
    blocks, depth, span = pieces[0].shape

    def copies(j):
        return [
            pltpu.make_async_copy(
                pieces[j * halves + p].at[i],
                w_ref.at[j, pl.ds(i * depth, depth), pl.ds(pl.multiple_of(offset_ref[p], 128), span)],
                sems.at[j, p, i],
            )
            for p in range(halves)
            for i in range(blocks)
        ]

    def start(found):
        for copy in found:
            copy.start()

    def wait(found):
        for copy in found:
            copy.wait()

    tokens = slot_copies([ref.at[at] for ref in x_refs], x_ref, x_sems)
    givens = slot_copies([ref.at[at] for ref in given_refs], given_ref, given_sems)
    for found in (tokens[:2], copies(0), copies(1), copies(2), givens[:2], tokens[2:], givens[2:]):
        start(found)

    def act_copy(kind, k):
        rows_of = pl.ds(2 * k, 2)
        return pltpu.make_async_copy(act_ref.at[kind, rows_of], act_out.at[kind, rows_of], act_sems.at[kind, k])

    def part_copy(n, k):
        out = outs[k].at[:, at] if n == 0 else outs[2 + k]
        return pltpu.make_async_copy(held[n].at[k], out, out_sems.at[n, k])

    def leave_act(kind, k, value):
        act_ref[kind, pl.ds(2 * k, 2)] = value.reshape(2, rows, -1)
        act_copy(kind, k).start()

    def leave_part(n, k, value):
        held[n][k] = value.astype(BF16).reshape(2, rows, width)
        for turn in range(2):

            @pl.when(k == turn)
            def _():
                part_copy(n, turn).start()

    def arrive(k, found):
        @pl.when(k == 0)
        def _():
            wait(found)

    def step(k, carry):
        for turn in range(2):

            @pl.when(k == turn)
            def _():
                wait(tokens[2 * turn : 2 * turn + 2])

        x = x_ref[pl.ds(2 * k, 2)].reshape(count, width)
        arrive(k, copies(0))
        gate = dot_nt(x, w_ref[0])
        arrive(k, copies(1))
        up = dot_nt(x, w_ref[1])
        sig = jax.nn.sigmoid(gate)
        swish = gate * sig
        hidden = (swish * up).astype(BF16)
        leave_act(2, k, hidden)
        arrive(k, copies(2))
        for turn in range(2):

            @pl.when(k == turn)
            def _():
                wait(givens[2 * turn : 2 * turn + 2])

        hidden_back = dot_nt(given_ref[pl.ds(2 * k, 2)].reshape(count, width), w_ref[2])
        gate_back = (hidden_back * up * (sig * (1.0 + gate * (1.0 - sig)))).astype(BF16)
        leave_act(0, k, gate_back)
        up_back = (hidden_back * swish).astype(BF16)
        leave_act(1, k, up_back)
        leave_part(1, k, dot_nn(gate_back, w_ref[0]) + dot_nn(up_back, w_ref[1]))
        leave_part(0, k, dot_nn(hidden, w_ref[2]))
        return carry

    lax.fori_loop(0, 2, step, 0)
    for k in range(2):
        for kind in range(3):
            act_copy(kind, k).wait()
        for n in range(2):
            part_copy(n, k).wait()


def ffn_call(offsets, at, xs, given, pieces, before):
    pair, rows, width = xs[0].shape
    halves = len(pieces[0])
    blocks, depth, _ = pieces[0][0].shape
    hidden = blocks * depth
    part, act = (2, rows, width), (3, 4, rows, hidden)
    both = (2, pair, rows, width)
    parts = [piece for row in pieces for piece in row]
    first = 9 + len(parts)
    before = before or []
    return pl.pallas_call(
        functools.partial(ffn_kernel, at, halves),
        in_specs=[pl.BlockSpec(memory_space=pltpu.SMEM)] + [pl.BlockSpec(memory_space=pl.ANY)] * (8 + len(parts) + len(before)),
        out_specs=[pl.BlockSpec(memory_space=pl.ANY)] * 5,
        out_shape=[jax.ShapeDtypeStruct(shape, BF16) for shape in (act, both, both, part, part)],
        input_output_aliases={first + i: 1 + i for i in range(len(before))},
        scratch_shapes=[
            pltpu.VMEM((3, hidden, width), BF16),
            pltpu.VMEM((4, rows, width), BF16),
            pltpu.VMEM((4, rows, width), BF16),
            pltpu.VMEM(act, BF16),
        ]
        + [pltpu.VMEM((2, *part), BF16)] * 2
        + [
            pltpu.SemaphoreType.DMA((3, halves, blocks)),
            pltpu.SemaphoreType.DMA((4,)),
            pltpu.SemaphoreType.DMA((4,)),
            pltpu.SemaphoreType.DMA((3, 2)),
            pltpu.SemaphoreType.DMA((2, 2)),
        ],
        compiler_params=params(),
        cost_estimate=cost(22),
        name="ffn",
    )(offsets, *xs, *given, *parts, *before)


def weight_kernel(halves, offset_ref, *refs):
    lefts, rights = refs[0:2], refs[2:6]
    outs, total_ref = refs[6 : 6 + halves], refs[6 + halves]
    total = 0.0
    for s, left in enumerate(lefts):
        a = left[0]
        total = total + dot_tn(a.reshape(-1, a.shape[-1]), jnp.concatenate([ref[s] for ref in rights]))
    total_ref[...] = total.astype(BF16)
    blocks, depth, span = outs[0].shape
    for p in range(halves):
        start = pl.multiple_of(offset_ref[p], 128)
        for i in range(blocks):
            outs[p][i] = total_ref[i * depth : (i + 1) * depth, pl.ds(start, span)]


def weight_call(offsets, kind, acts, rights, halves, blocks):
    units, width = acts[0].shape[-1], rights[0].shape[-1]
    unit = (1, *acts[0].shape[1:])
    part = (blocks, units // blocks, width // halves)
    return pl.pallas_call(
        functools.partial(weight_kernel, halves),
        grid=(1,),
        in_specs=[pl.BlockSpec(memory_space=pltpu.SMEM)]
        + [pl.BlockSpec(unit, lambda j: (kind, 0, 0, 0))] * 2
        + [whole(one.shape) for one in rights],
        out_specs=[whole(part)] * halves,
        out_shape=[jax.ShapeDtypeStruct(part, BF16)] * halves,
        scratch_shapes=[pltpu.VMEM((units, width), BF16)],
        compiler_params=params(),
        cost_estimate=cost(10),
        name="weight",
    )(offsets, *acts, *rights)


def small_weight_kernel(halves, near, count, place_ref, offset_ref, *refs):
    lefts, rights, outs, total_ref = refs[:count], refs[count : -halves - 1], refs[-halves - 1 : -1], refs[-1]
    t = place_ref[1]
    total = 0.0
    for s in range(2):
        a = lefts[0][s] if count == 1 else lefts[s][0]
        pieces = [ref[s] for ref in rights] if len(rights) == 4 else [ref[...] for ref in rights[4 * s : 4 * s + 4]]
        total = total + dot_tn(a.reshape(-1, a.shape[-1]), jnp.concatenate(pieces))
    total_ref[...] = total.astype(BF16)
    blocks, _, span = outs[0].shape
    for p in range(halves):
        for e in range(blocks):
            if near:
                outs[p][e] = total_ref[:, pl.ds(pl.multiple_of(offset_ref[p] + (t ^ e) * span, 128), span)]
            else:
                outs[p][e] = total_ref[:, e * span : (e + 1) * span]


def small_weight_call(place, offsets, lefts, rights, halves, blocks, near):
    rows, width = lefts[0].shape[-1], rights[0].shape[-1]
    part = (blocks, rows, width // blocks // halves)
    return pl.pallas_call(
        functools.partial(small_weight_kernel, halves, near, len(lefts)),
        in_specs=[pl.BlockSpec(memory_space=pltpu.SMEM)] * 2
        + [pl.BlockSpec(memory_space=pltpu.VMEM)] * (len(lefts) + len(rights)),
        out_specs=[pl.BlockSpec(memory_space=pltpu.VMEM)] * halves,
        out_shape=[jax.ShapeDtypeStruct(part, BF16)] * halves,
        scratch_shapes=[pltpu.VMEM((rows, width), BF16)],
        compiler_params=params(),
        cost_estimate=cost(5),
        name="small_weight",
    )(place, offsets, *lefts, *rights)


def inverse_root(values):
    return lax.rsqrt(jnp.mean(values * values, axis=-1, keepdims=True) + EPS)


def norm_back(values, root, gain, given):
    mean = jnp.mean(values * gain * given, axis=-1, keepdims=True)
    return root * gain * given - values * (root * root * root) * mean


def per_device(
    sizes,
    tokens,
    positions,
    first_gain,
    query_weight,
    key_weight,
    value_weight,
    query_gain,
    key_gain,
    output_weight,
    second_gain,
    gate_weight,
    up_weight,
    down_weight,
    upstream,
):
    shards, ctx, tp = sizes["shard"], sizes["ctx"], sizes["tp"]
    groups = ("shard", "tp")
    sequences, rows, width = tokens.shape
    head_dim = query_gain.shape[0]
    depth = query_weight.shape[0]
    units = gate_weight.shape[1]
    c, t = lax.axis_index("ctx"), lax.axis_index("tp")
    place = jnp.stack([c, t]).astype(jnp.int32)
    trade = [(i * tp + k, k * ctx + i) for i in range(ctx) for k in range(tp)]

    line = Line()
    shard = lax.axis_index("shard")
    small = jnp.concatenate([query_weight, key_weight, value_weight, output_weight.T], axis=1)
    small = lax.ppermute(small, ("ctx", "tp"), trade)
    blocks_attn = trade_tp(small, tp)
    w_attn = join_shard(blocks_attn.reshape(tp * depth, -1), shards)

    large = jnp.stack([gate_weight.T, up_weight.T, down_weight]).reshape(3, ctx, units // ctx, depth)
    large = lax.all_to_all(large, "ctx", 1, 1, tiled=True)
    large = after(large, small).transpose(0, 2, 1, 3).reshape(3, units // ctx, ctx * depth)
    aligned = depth % 128 == 0
    starts = jnp.stack([shard, 1 - shard]) if shards == 2 else jnp.zeros((2,), jnp.int32)
    starts = (starts * (width // 2)).astype(jnp.int32)

    mine = lax.dynamic_slice_in_dim(positions, t * rows, rows, 1).astype(F32)
    places = jnp.stack(gather_ctx(mine))
    freqs = jnp.exp(-math.log(THETA) * jnp.arange(0, head_dim, 2).astype(F32) / head_dim)
    angles = places[..., None] * freqs
    cosine, sine = jnp.cos(angles), jnp.sin(angles)
    cosine = jnp.concatenate([cosine] * 4, axis=-1)
    sine = jnp.concatenate([sine] * 4, axis=-1)
    gains = jnp.concatenate([jnp.tile(query_gain, 4), jnp.tile(key_gain, 2)])[None]

    x = tokens.astype(F32)
    root = inverse_root(x)
    first = (x * root * first_gain).astype(BF16)
    given = upstream.astype(F32)

    pair = range(sequences)
    first_all = gather_ctx(first)
    one = line.run(qkv_call, place, first_all, w_attn, cosine, sine, gains)
    heads, raw = exchange_heads(one[0], (one[1], one[2], one[1], one[3])), one[4]
    lines = [lax.all_gather(after(large[0], blocks_attn), "tp", axis=0, tiled=False)]
    for j in (1, 2):
        lines.append(lax.all_gather(after(large[j], *heads), "tp", axis=0, tiled=False))
    w_ffn = [gather_shard(one, shards) for one in lines]
    upstream_all = gather_ctx(after(upstream, raw))
    heads = after(heads, w_ffn[0][-1], *upstream_all)
    own, other, o, lse = line.run(attend_call, place, heads)
    own = after(own, lines[1])
    mixed, own, near = line.run(out_call, place, [own, to_tp(other, 1)], w_attn)
    mine, away = line.run(lambda got, own: add_near(own, got), lax.ppermute(near, "ctx", NEAR), own)

    def middle_of(far, mine):
        middle = x + (mine + far.astype(F32))
        middle_root = inverse_root(middle)
        return (middle * middle_root * second_gain).astype(BF16), middle, middle_root

    mine = after(mine, lines[2], w_ffn[1][-1])
    second, middle, middle_root = line.run(middle_of, lax.ppermute(away, "ctx", FAR), mine)
    seconds = gather_ctx(second)
    ffn = []
    for s in pair:
        before = ffn[-1][1:3] if ffn else None
        ffn.append(line.run(ffn_call, starts, s, seconds, upstream_all, w_ffn, before))
    out_shares = ffn[-1][1:3]

    back_rows, mixed_back_all, backs_sent = [], [], []

    def turn_back(second_back, s):
        middle_back = given[s] + norm_back(middle[s], middle_root[s], second_gain, second_back)
        return middle_back.astype(BF16), middle_back, jnp.sum(second_back * middle[s] * middle_root[s], axis=0)

    def turn(s, call, *shares):
        low, middle_back, share = line.run(lambda first, *rest: turn_back(call(first, *rest), s), *shares)
        back_rows.append(middle_back)
        mixed_back_all.append(gather_ctx(low))
        return share

    def back_out(s):
        own, other = line.run(out_back_call, place, mixed_back_all[s], w_attn)
        backs_sent.append([own, to_tp(other, 1)])

    own, near = ffn[0][3], ffn[0][4]
    shares = own[0], *(
        lax.ppermute(value, "ctx", way) for value, way in ((own[1], FAR), (near[0], NEAR), (near[1], CROSS))
    )
    second_share = turn(0, lambda *parts: sum(part.astype(F32) for part in parts), *shares)
    mine, away = line.run(lambda got, own: add_near(own, got), lax.ppermute(ffn[1][4], "ctx", NEAR), ffn[1][3])
    away = lax.ppermute(away, "ctx", FAR)
    near = aligned and shards == 2
    count = shards * tp
    small = 2 if near else 1, tp if near else 1, near
    halves = 2 if shards == 2 else 1
    sums, g_ffn = [], []

    def weight(kind):
        rights = upstream_all if kind == 2 else seconds
        sums.append(line.run(weight_call, starts, kind, [one[0] for one in ffn], rights, halves, tp))

    def send(kind):
        parts = sums[kind]
        return send_shard(after(parts, g_ffn[-1]) if g_ffn else parts, shards)

    def add(kind, moved):
        added = line.run(add_shard, moved, sums[kind])
        sums[kind] = added
        g_ffn.append(added)

    def scatter(kind):
        return lax.psum_scatter(g_ffn[kind], "tp", scatter_dimension=0, tiled=False)

    weight(0)
    moved = send(0)
    weight(1)
    back_out(0)
    second_share = second_share + turn(1, lambda far, own: own + far.astype(F32), away, mine)
    weight(2)
    back_out(1)
    add(0, moved)
    moved = send(1)
    near_sum, away = line.run(
        lambda got, own: add_near(own, got), lax.ppermute(after(out_shares[1], backs_sent[0]), "ctx", NEAR), out_shares[0]
    )
    far_sum = lax.ppermute(away, "ctx", FAR)
    half = line.run(attend_back_call, after(place, *backs_sent[1]), 0, heads, backs_sent[0], o, lse)
    got = [exchange_heads(half[0], half[1:])]
    given_all = [*mixed_back_all[0], *mixed_back_all[1]]
    out_parts = line.run(small_weight_call, place, starts, [mixed], given_all, *small)
    out_moved = lax.ppermute(out_parts[1], "shard", [(0, 1), (1, 0)]) if near else None
    add(1, moved)
    moved = send(2)
    result = line.run(lambda far, mine: ((middle + mine) + far.astype(F32)).astype(BF16), far_sum, near_sum)
    full = line.run(attend_back_call, place, 1, heads, backs_sent[1], o, lse)
    got.append(exchange_heads(full[0], full[1:]))
    add(2, moved)
    g_ffn = [scatter(kind) for kind in range(3)]
    def last(far, mine, s):
        first_back = mine[0] + far[0].astype(F32)
        gradient = back_rows[s] + norm_back(x[s], root[s], first_gain, first_back)
        return jnp.sum(first_back * x[s] * root[s], axis=0), gradient

    backs, firsts, head_share, gradients = [], [], 0.0, []
    for s in pair:
        back, own, other, share = line.run(qkv_back_call, place, s, got[s], raw, cosine, sine, gains, w_attn)
        backs.append(back)
        head_share = head_share + share
        other = lax.ppermute(other, "ctx", NEAR)
        if s == 0:
            mine, away = line.run(lambda got, own: add_near(own, got), other, own)
            firsts.append((lax.ppermute(away, "ctx", FAR), mine))
    parts = line.run(small_weight_call, place, starts, backs, first_all, *small)
    moved = lax.ppermute(parts[1], "shard", [(0, 1), (1, 0)]) if near else None
    mine, away = line.run(lambda got, own: add_near(own, got), other, own)
    firsts.append((lax.ppermute(away, "ctx", FAR), mine))
    def finish(s):
        share, gradient = line.run(lambda a, b: last(a, b, s), *firsts[s])
        gradients.append(gradient)
        return share

    first_share = finish(0)
    if near:
        both = lambda a, b: (a.astype(F32) + b.astype(F32)).astype(BF16)
        g_attn = line.run(
            lambda a, b: jnp.concatenate([both(a, b), both(out_moved, out_parts[0])], axis=1), moved, parts[0]
        )
        g_attn = exchange_tp([g_attn[e] for e in range(tp)])
    else:
        g_attn = jnp.concatenate([parts[0][0], out_parts[0][0]])
        g_attn = g_attn.reshape(-1, count, width // count).transpose(1, 0, 2)
        g_attn = lax.psum_scatter(g_attn, groups, scatter_dimension=0, tiled=False)
    first_share = first_share + finish(1)
    shares = jnp.concatenate([first_share, second_share, head_share[0]])
    shares = sum_all(shares, [(name, sizes[name]) for name in ("ctx", "shard", "tp")])

    def settle(g):
        g = g.reshape(3, units, depth).astype(F32)
        return g[0].T, g[1].T, g[2]

    g_ffn = jnp.stack(g_ffn).reshape(3, units // ctx, ctx, depth).transpose(0, 2, 1, 3)
    g_ffn = lax.all_to_all(g_ffn, "ctx", 1, 1, tiled=True)
    g_ffn = line.run(settle, g_ffn)

    if near:
        g_attn = line.run(lambda *parts: sum(part.astype(F32) for part in parts).astype(BF16), *g_attn)
    g_attn = lax.ppermute(g_attn, ("ctx", "tp"), trade).astype(F32)
    heads_end = query_weight.shape[1]
    pairs = key_weight.shape[1]

    head_total = shares[2 * width :]
    return (
        result,
        jnp.stack(gradients),
        g_attn[:heads_end].T,
        g_attn[heads_end : heads_end + pairs].T,
        g_attn[heads_end + pairs : heads_end + 2 * pairs].T,
        g_attn[heads_end + 2 * pairs :],
        *g_ffn,
        shares[:width],
        shares[width : 2 * width],
        jnp.sum(head_total[: 4 * head_dim].reshape(4, head_dim), axis=0),
        jnp.sum(head_total[4 * head_dim :].reshape(2, head_dim), axis=0),
    )


def solution(mesh):
    rows = P("shard", ("ctx", "tp"), None)
    wide = P(("shard", "ctx"), "tp")
    tall = P("tp", ("shard", "ctx"))
    none = P()
    in_specs = (
        rows, P("shard", "ctx"), none, wide, wide, wide, none, none, tall, none, wide, wide, tall, rows,
    )
    out_specs = (rows, rows, wide, wide, wide, tall, wide, wide, tall, none, none, none, none)
    sizes = {name: mesh.shape[name] for name in ("shard", "ctx", "tp")}
    return jax.shard_map(
        functools.partial(per_device, sizes), mesh=mesh, in_specs=in_specs, out_specs=out_specs, check_vma=False
    )
```

```python
import functools
import math

import jax
import jax.numpy as jnp
from jax import lax
from jax.experimental import pallas as pl
from jax.experimental.pallas import tpu as pltpu
from jax.sharding import PartitionSpec as P

EPS = 1e-05
THETA = 1000000.0
LOG2E = 1.4426950408889634
F32 = jnp.float32
BF16 = jnp.bfloat16
NEAR = [(0, 1), (1, 0), (2, 3), (3, 2)]
FAR = [(0, 2), (2, 0), (1, 3), (3, 1)]
CROSS = [(0, 3), (3, 0), (1, 2), (2, 1)]
LIMIT = 56 * 1024 * 1024


def dot_nn(left, right):
    return lax.dot_general(left, right, (((1,), (0,)), ((), ())), preferred_element_type=F32)


def dot_nt(left, right):
    return lax.dot_general(left, right, (((1,), (1,)), ((), ())), preferred_element_type=F32)


def dot_tn(left, right):
    return lax.dot_general(left, right, (((0,), (0,)), ((), ())), preferred_element_type=F32)


def swap_bits(j):
    return ((j & 1) << 1) | (j >> 1)


def gather_ctx(own):
    far = lax.ppermute(own, "ctx", FAR)
    near = lax.ppermute(own, "ctx", NEAR)
    return [own, far, near, lax.ppermute(far, "ctx", NEAR)]


def add_near(own, got):
    return own[0].astype(F32) + got[0].astype(F32), (own[1].astype(F32) + got[1].astype(F32)).astype(BF16)


def reduce_near(own, near):
    return add_near(own, lax.ppermute(near, "ctx", NEAR))


def reduce_far(mine, away):
    return mine + lax.ppermute(away, "ctx", FAR).astype(F32)


def reduce_ctx(own, near):
    got = lax.ppermute(own[1], "ctx", FAR), lax.ppermute(near[0], "ctx", NEAR), lax.ppermute(near[1], "ctx", CROSS)
    return own[0].astype(F32) + got[0].astype(F32) + got[1].astype(F32) + got[2].astype(F32)


def to_tp(value, e):
    return lax.ppermute(value, "tp", [(i, i ^ e) for i in range(4)])


def exchange_tp(blocks):
    return [blocks[0]] + [to_tp(blocks[e], e) for e in range(1, len(blocks))]


def exchange_heads(q_same, kv):
    return [q_same, *exchange_tp(kv)]


def gather_shard(own, shards):
    if shards == 2:
        return [own, lax.ppermute(own, "shard", [(0, 1), (1, 0)])]
    every = lax.all_gather(own, "shard", axis=0, tiled=False)
    return [every.transpose(1, 2, 0, 3).reshape(*own.shape[:2], -1)]


def send_shard(parts, shards):
    if shards == 2:
        return lax.ppermute(parts[1], "shard", [(0, 1), (1, 0)])
    blocks, units, width = parts[0].shape
    every = parts[0].reshape(blocks, units, shards, width // shards).transpose(2, 0, 1, 3)
    return lax.psum_scatter(every, "shard", scatter_dimension=0, tiled=False)


def add_shard(got, parts):
    return (parts[0].astype(F32) + got.astype(F32)).astype(BF16) if len(parts) == 2 else got


def after(value, *others):
    return lax.optimization_barrier((value, *others))[0]


class Line:
    def __init__(self):
        self.last = ()

    def run(self, call, first, *others):
        result = call(after(first, *self.last), *others)
        self.last = (jax.tree.leaves(result)[0],)
        return result


def trade_tp(own, count):
    got = [own]
    for k in range(1, count):
        got.append(lax.ppermute(own, "tp", [(i, i ^ k) for i in range(count)]))
    index = lax.axis_index("tp")
    slots = []
    for slot in range(count):
        value = got[slot]
        for at in range(1, count):
            value = jnp.where(index == at, got[slot ^ at], value)
        slots.append(value)
    return jnp.stack(slots)


def join_shard(own, shards):
    if shards == 2:
        other = lax.ppermute(own, "shard", [(0, 1), (1, 0)])
        index = lax.axis_index("shard")
        return jnp.concatenate([jnp.where(index == 0, own, other), jnp.where(index == 0, other, own)])
    return lax.all_gather(own, "shard", axis=0, tiled=True)


def sum_all(vector, sizes):
    for name, size in sizes:
        step = 1
        while step < size:
            other = lax.ppermute(vector, name, [(i, i ^ step) for i in range(size)])
            vector = vector + other
            step *= 2
    return vector


def params():
    return pltpu.CompilerParams(vmem_limit_bytes=LIMIT)


def cost(micros):
    return pl.CostEstimate(flops=int(micros * 1.0e9), transcendentals=0, bytes_accessed=int(micros * 1.0e6))


def slot_copies(refs, held, sems):
    return [pltpu.make_async_copy(ref, held.at[k], sems.at[k]) for k, ref in enumerate(refs)]


def start_slots(refs, held, sems):
    @pl.when(pl.program_id(0) == 0)
    def _():
        for copy in slot_copies(refs, held, sems):
            copy.start()


def wait_slot(refs, held, sems, step=1):
    for k, copy in enumerate(slot_copies(refs, held, sems)):

        @pl.when(pl.program_id(0) == k // step)
        def _():
            copy.wait()


def lanes_low(rows):
    return lax.broadcasted_iota(jnp.int32, (rows, 128), 1) < 64


def pack(first, second, low):
    return jnp.where(low, first, second)


def head_sums(values):
    rows = lax.broadcasted_iota(jnp.int32, (128, 128), 0) >> 6
    columns = lax.broadcasted_iota(jnp.int32, (128, 128), 1) >> 6
    ones = jnp.where(rows == columns, 1.0, 0.0).astype(BF16)
    high = values.astype(BF16)
    rest = values - high.astype(F32)
    low = rest.astype(BF16)
    return dot_nn(high, ones) + dot_nn(low, ones)


def qkv_kernel(place_ref, *refs):
    x_refs, (w_ref, cos_ref, sin_ref, gain_ref) = refs[:4], refs[4:8]
    q_same, kv_same, beside, kv_other, raw_ref, x_ref, q_ref, kv_ref, sems = refs[8:]
    side, s, j = place_ref[1] & 1, pl.program_id(0), pl.program_id(1)
    rows = x_ref.shape[2]
    copies = slot_copies(x_refs, x_ref, sems)

    @pl.when((s == 0) & (j == 0))
    def _():
        for copy in copies:
            copy.start()

    for k, copy in enumerate(copies):

        @pl.when((s == 0) & (j == k))
        def _():
            copy.wait()

    y = dot_nn(x_ref[j, s], w_ref[:, :512])
    raw_ref[0, 0] = y[:, :384]
    low = lanes_low(rows)
    early = (lax.broadcasted_iota(jnp.int32, (rows, 128), 1) & 32) == 0
    cosine, sine = cos_ref[0, 0], sin_ref[0, 0]
    turned = []
    for b in range(3):
        u = y[:, b * 128 : (b + 1) * 128]
        r = lax.rsqrt(head_sums(u * u) * (1.0 / 64.0) + EPS)
        n = u * r * gain_ref[:, b * 128 : (b + 1) * 128]
        other = jnp.where(early, -pltpu.roll(n, 96, 1), pltpu.roll(n, 32, 1))
        turned.append(n * cosine + other * sine)
    key, value = turned[2], y[:, 384:512]
    q_ref[0] = (turned[0] * 0.125).astype(BF16)
    q_ref[1] = (turned[1] * 0.125).astype(BF16)
    kv_ref[0] = pack(key, pltpu.roll(value, 64, 1), low).astype(BF16)
    kv_ref[1] = pack(pltpu.roll(key, 64, 1), value, low).astype(BF16)
    q_same[0, 0] = q_ref[side]
    kv_same[0, 0] = kv_ref[side]
    beside[0, 0, :rows] = q_ref[1 - side]
    beside[0, 0, rows:] = kv_ref[1 - side]
    kv_other[0, 0] = kv_ref[1 - side]


def step_block(*shape):
    return pl.BlockSpec((1, 1, *shape), lambda s, j: (s, j, 0, 0))


def table_block(*shape):
    return pl.BlockSpec((1, 1, *shape), lambda s, j: (j, s, 0, 0))


def whole2(shape):
    return pl.BlockSpec(shape, lambda s, j: (0,) * len(shape))


def qkv_call(place, xs, w, cosine, sine, gains):
    slots = len(xs)
    pair, rows, width = xs[0].shape
    talls = (rows, rows, 2 * rows, rows)
    return pl.pallas_call(
        qkv_kernel,
        grid=(pair, slots),
        in_specs=[pl.BlockSpec(memory_space=pltpu.SMEM)]
        + [pl.BlockSpec(memory_space=pl.ANY)] * slots
        + [whole2(w.shape), table_block(rows, 128), table_block(rows, 128), whole2((1, 384))],
        out_specs=[step_block(tall, 128) for tall in talls] + [step_block(rows, 384)],
        out_shape=[jax.ShapeDtypeStruct((pair, slots, tall, 128), BF16) for tall in talls]
        + [jax.ShapeDtypeStruct((pair, slots, rows, 384), F32)],
        scratch_shapes=[
            pltpu.VMEM((slots, pair, rows, width), BF16),
            pltpu.VMEM((2, rows, 128), BF16),
            pltpu.VMEM((2, rows, 128), BF16),
            pltpu.SemaphoreType.DMA((slots,)),
        ],
        compiler_params=params(),
        cost_estimate=cost(15),
        name="qkv",
    )(place, *xs, w, cosine, sine, gains)


def lay_keys(place_ref, refs, kv_ref):
    c, t = place_ref[0], place_ref[1]
    for e, ref in enumerate(refs):
        for j in range(ref.shape[1]):
            kv_ref[4 * (c ^ swap_bits(j)) + (t ^ e)] = ref[0, j, ref.shape[2] - kv_ref.shape[1] :]


def lay_rows(place_ref, own_ref, got_ref, out_ref, high):
    c, side = place_ref[0], place_ref[1] & 1
    rows = out_ref.shape[2]
    low = lanes_low(rows)
    for ref, start in ((own_ref, 2 * side), (got_ref, 2 - 2 * side)):
        for j in range(4):
            g = c ^ swap_bits(j)
            value = ref[0, j, :rows] if len(ref.shape) == 4 else ref[j, :rows]
            turned = pltpu.roll(value, 64, 1)
            zero = jnp.zeros_like(value)
            if high:
                out_ref[g, start] = jnp.where(low, zero, turned)
                out_ref[g, start + 1] = jnp.where(low, zero, value)
            else:
                out_ref[g, start] = jnp.where(low, value, zero)
                out_ref[g, start + 1] = jnp.where(low, turned, zero)


def diagonal(rows, wide, edge):
    key = lax.broadcasted_iota(jnp.int32, (rows, wide), 0)
    column = lax.broadcasted_iota(jnp.int32, (rows, wide), 1)
    return (key <= (column & (rows - 1))) | (column >= edge)


def whole(shape):
    return pl.BlockSpec(shape, lambda j: (0,) * len(shape))


def attend_kernel(place_ref, *refs):
    q_own, keys = refs[0], refs[1:5]
    own_out, other_out, o_ref, lse_ref, q_ref, kv_ref, acc_ref, sum_ref, ret_ref = refs[5:]
    c, t, g = place_ref[0], place_ref[1], pl.program_id(1)
    side, base = t & 1, t & 2
    rows = kv_ref.shape[1]
    half, wide = 2 * rows, 4 * rows

    @pl.when(g == 0)
    def _():
        lay_keys(place_ref, keys, kv_ref)
        lay_rows(place_ref, q_own, keys[1], q_ref, False)

    queries = q_ref[g].reshape(wide, 128)
    acc_ref[...] = jnp.zeros_like(acc_ref)
    sum_ref[...] = jnp.zeros_like(sum_ref)

    def add(pair, skip, allowed):
        weights = jnp.exp2(dot_nt(pair, queries[skip:]) * LOG2E)
        if allowed is not None:
            weights = jnp.where(allowed, weights, 0.0)
        sum_ref[:, skip:] += jnp.sum(weights, axis=0, keepdims=True)
        acc_ref[:, skip:] += dot_tn(pair, weights.astype(BF16))

    def body(n, carry):
        add(kv_ref[pl.ds(2 * n, 2)].reshape(2 * rows, 128), 0, None)
        return carry

    last = 4 * g + base
    lax.fori_loop(0, last >> 1, body, 0)
    add(kv_ref[last], 0, diagonal(rows, wide, half))
    add(kv_ref[last + 1], half, diagonal(rows, half, half))
    total = sum_ref[...]
    out = acc_ref[...] / total
    o_ref[0, 0] = out[64:]
    lse_ref[0, 0] = jnp.log(total) * LOG2E
    flat = jnp.transpose(out)
    low = lanes_low(rows)
    slot = swap_bits(c ^ g)
    for u in range(2):
        first, second = (flat[(2 * u + h) * rows : (2 * u + h + 1) * rows] for h in range(2))
        ret_ref[u, slot] = pack(pltpu.roll(first, 64, 1), second, low).astype(BF16)

    @pl.when(g == 3)
    def _():
        own_out[0] = ret_ref[side]
        other_out[0] = ret_ref[1 - side]


def sequence_block(shape):
    return pl.BlockSpec((1, *shape[1:]), lambda s, j: (s, 0, 0, 0))


def attend_call(place, gets):
    pair, slots, rows, _ = gets[0].shape
    wide = 4 * rows
    return pl.pallas_call(
        attend_kernel,
        grid=(pair, 4),
        in_specs=[pl.BlockSpec(memory_space=pltpu.SMEM)] + [sequence_block(one.shape) for one in gets],
        out_specs=[sequence_block(gets[0].shape)] * 2 + [step_block(64, wide), step_block(1, wide)],
        out_shape=[jax.ShapeDtypeStruct(gets[0].shape, BF16)] * 2
        + [
            jax.ShapeDtypeStruct((pair, 4, 64, wide), F32),
            jax.ShapeDtypeStruct((pair, 4, 1, wide), F32),
        ],
        scratch_shapes=[
            pltpu.VMEM((4, 4, rows, 128), BF16),
            pltpu.VMEM((4 * slots, rows, 128), BF16),
            pltpu.VMEM((128, wide), F32),
            pltpu.VMEM((1, wide), F32),
            pltpu.VMEM((2, slots, rows, 128), BF16),
        ],
        compiler_params=params(),
        cost_estimate=cost(32),
        name="attend",
    )(place, *gets)


def own_block(rows, width):
    return pl.BlockSpec((1, 1, rows, width), lambda s, j: (jnp.minimum(j, 1), s, 0, 0))


def near_block(rows, width):
    return pl.BlockSpec((1, 1, rows, width), lambda s, j: (jnp.maximum(j - 2, 0), s, 0, 0))


def store_share(j, own_ref, near_ref, part):
    @pl.when(j < 2)
    def _():
        own_ref[0, 0] = part

    @pl.when(j >= 2)
    def _():
        near_ref[0, 0] = part


def out_kernel(place_ref, get_own, get_other, w_ref, mixed_ref, own_ref, near_ref, head_ref):
    side, j = place_ref[1] & 1, pl.program_id(1)
    head_ref[side] = get_own[0, 0]
    head_ref[1 - side] = get_other[0, 0]
    mixed = jnp.concatenate([head_ref[0], head_ref[1]], axis=1)
    mixed_ref[0, 0] = mixed
    store_share(j, own_ref, near_ref, dot_nt(mixed, w_ref[:, 512:]).astype(BF16))


def out_call(place, gets, w):
    pair, slots, rows, _ = gets[0].shape
    width = w.shape[0]
    return pl.pallas_call(
        out_kernel,
        grid=(pair, slots),
        in_specs=[pl.BlockSpec(memory_space=pltpu.SMEM)] + [step_block(rows, 128)] * 2 + [whole2(w.shape)],
        out_specs=[step_block(rows, 256), own_block(rows, width), near_block(rows, width)],
        out_shape=[
            jax.ShapeDtypeStruct((pair, slots, rows, 256), BF16),
            jax.ShapeDtypeStruct((2, pair, rows, width), BF16),
            jax.ShapeDtypeStruct((2, pair, rows, width), BF16),
        ],
        scratch_shapes=[pltpu.VMEM((2, rows, 128), BF16)],
        compiler_params=params(),
        cost_estimate=cost(9),
        name="out",
    )(place, *gets, w)


def out_back_kernel(place_ref, *refs):
    x_refs, w_ref, own_out, other_out, x_ref, send_ref, sems = refs[0:4], *refs[4:]
    side, j = place_ref[1] & 1, pl.program_id(0)
    start_slots(x_refs, x_ref, sems)
    wait_slot(x_refs, x_ref, sems)
    back = dot_nn(x_ref[j], w_ref[:, 512:]).astype(BF16)
    send_ref[0] = back[:, :128]
    send_ref[1] = back[:, 128:]
    own_out[0] = send_ref[side]
    other_out[0] = send_ref[1 - side]


def out_back_call(place, xs, w):
    slots = len(xs)
    rows, width = xs[0].shape
    return pl.pallas_call(
        out_back_kernel,
        grid=(slots,),
        in_specs=[pl.BlockSpec(memory_space=pltpu.SMEM)]
        + [pl.BlockSpec(memory_space=pl.ANY)] * slots
        + [whole(w.shape)],
        out_specs=[pl.BlockSpec((1, rows, 128), lambda j: (j, 0, 0))] * 2,
        out_shape=[jax.ShapeDtypeStruct((slots, rows, 128), BF16)] * 2,
        scratch_shapes=[
            pltpu.VMEM((slots, rows, width), BF16),
            pltpu.VMEM((2, rows, 128), BF16),
            pltpu.SemaphoreType.DMA((slots,)),
        ],
        compiler_params=params(),
        cost_estimate=cost(4),
        name="out_back",
    )(place, *xs, w)


def attend_back_kernel(place_ref, *refs):
    q_own, keys, back_own, back_got = refs[0], refs[1:5], refs[5], refs[6]
    o_ref, lse_ref = refs[7], refs[8]
    own_out, outs = refs[-11], refs[-10:-6]
    q_ref, kv_ref, back_ref, dkv_ref, acc_ref, ret_ref = refs[-6:]
    c, t, g = place_ref[0], place_ref[1], pl.program_id(0)
    side, base = t & 1, t & 2
    rows = kv_ref.shape[1]
    half, wide = 2 * rows, 4 * rows

    @pl.when(g == 0)
    def _():
        lay_keys(place_ref, keys, kv_ref)
        lay_rows(place_ref, q_own, keys[1], q_ref, False)
        lay_rows(place_ref, back_own, back_got, back_ref, True)
        dkv_ref[...] = jnp.zeros_like(dkv_ref)

    queries = q_ref[g].reshape(wide, 128)
    given = back_ref[g].reshape(wide, 128)
    delta = jnp.sum(jnp.transpose(given.astype(F32))[64:] * o_ref[0, 0], axis=0, keepdims=True)
    lse = lse_ref[0, 0]
    acc_ref[...] = jnp.zeros_like(acc_ref)

    def block(pair, skip, allowed):
        probs = jnp.exp2(dot_nt(pair, queries[skip:]) * LOG2E - lse[:, skip:])
        if allowed is not None:
            probs = jnp.where(allowed, probs, 0.0)
        slopes = dot_nt(pair, given[skip:])
        score_back = (probs * (slopes - delta[:, skip:])).astype(BF16)
        acc_ref[skip:] += dot_tn(score_back, pair)
        return dot_nn(probs.astype(BF16), given[skip:]) + dot_nn(score_back, queries[skip:])

    def body(n, carry):
        pair = kv_ref[pl.ds(2 * n, 2)].reshape(2 * rows, 128)
        dkv_ref[pl.ds(2 * n, 2)] += block(pair, 0, None).reshape(2, rows, 128)
        return carry

    last = 4 * g + base
    lax.fori_loop(0, last >> 1, body, 0)
    dkv_ref[last] += block(kv_ref[last], 0, diagonal(rows, wide, half))
    dkv_ref[last + 1] += block(kv_ref[last + 1], half, diagonal(rows, half, half))
    low = lanes_low(rows)
    slot = swap_bits(c ^ g)
    for u in range(2):
        first, second = (acc_ref[(2 * u + h) * rows : (2 * u + h + 1) * rows] * 0.125 for h in range(2))
        ret_ref[u, slot] = pack(first, pltpu.roll(second, 64, 1), low).astype(BF16)

    @pl.when(g == pl.num_programs(0) - 1)
    def _():
        own_out[0] = ret_ref[side]
        outs[1][0, :, :rows] = ret_ref[1 - side]
        for e in range(4):
            for j in range(4):
                outs[e][0, j, outs[e].shape[2] - rows :] = dkv_ref[4 * (c ^ swap_bits(j)) + (t ^ e)].astype(BF16)


def attend_back_call(place, at, gets, backs, o, lse):
    _, slots, rows, _ = gets[0].shape
    wide = 4 * rows
    block = lambda one: pl.BlockSpec((1, *one.shape[1:]), lambda g: (at, 0, 0, 0))
    return pl.pallas_call(
        attend_back_kernel,
        grid=(4,),
        in_specs=[pl.BlockSpec(memory_space=pltpu.SMEM)]
        + [block(one) for one in gets]
        + [whole(one.shape) for one in backs]
        + [pl.BlockSpec((1, 1, tall, wide), lambda g: (at, g, 0, 0)) for tall in (64, 1)],
        out_specs=[whole((1, *one.shape[1:])) for one in gets],
        out_shape=[jax.ShapeDtypeStruct((1, *one.shape[1:]), BF16) for one in gets],
        scratch_shapes=[
            pltpu.VMEM((4, 4, rows, 128), BF16),
            pltpu.VMEM((4 * slots, rows, 128), BF16),
            pltpu.VMEM((4, 4, rows, 128), BF16),
            pltpu.VMEM((4 * slots, rows, 128), F32),
            pltpu.VMEM((wide, 128), F32),
            pltpu.VMEM((2, slots, rows, 128), BF16),
        ],
        compiler_params=params(),
        cost_estimate=cost(8),
        name="attend_back",
    )(place, *gets, *backs, o, lse)


def qkv_back_kernel(place_ref, *refs):
    q_own, keys, (raw_ref, cos_ref, sin_ref, gain_ref, w_ref) = refs[0], refs[1:5], refs[5:10]
    back_ref, own_ref, near_ref, share_ref, head_ref, pair_ref = refs[10:]
    side, j = place_ref[1] & 1, pl.program_id(0)
    rows = raw_ref.shape[2]
    head_ref[side] = q_own[0, 0].astype(F32)
    head_ref[1 - side] = keys[1][0, 0, :rows].astype(F32)
    pair_ref[side] = keys[0][0, 0].astype(F32) + keys[2][0, 0].astype(F32)
    pair_ref[1 - side] = keys[1][0, 0, rows:].astype(F32) + keys[3][0, 0].astype(F32)
    low = lanes_low(rows)
    early = (lax.broadcasted_iota(jnp.int32, (rows, 128), 1) & 32) == 0
    cosine, sine = cos_ref[0, 0], sin_ref[0, 0]

    @pl.when(j == 0)
    def _():
        share_ref[...] = jnp.zeros_like(share_ref)

    even, odd = pair_ref[0], pair_ref[1]
    key = pack(even, pltpu.roll(odd, 64, 1), low)
    value = pack(pltpu.roll(even, 64, 1), odd, low)
    outs = []
    for b, given in enumerate((head_ref[0], head_ref[1], key)):
        z = sine * given
        cotangent = given * cosine + jnp.where(early, pltpu.roll(z, 96, 1), -pltpu.roll(z, 32, 1))
        u = raw_ref[0, 0, :, b * 128 : (b + 1) * 128]
        gain = gain_ref[:, b * 128 : (b + 1) * 128]
        r = lax.rsqrt(head_sums(u * u) * (1.0 / 64.0) + EPS)
        mean = head_sums(u * gain * cotangent) * (1.0 / 64.0)
        share_ref[:, b * 128 : (b + 1) * 128] += jnp.sum(cotangent * u * r, axis=0, keepdims=True)
        outs.append((r * gain * cotangent - u * (r * r * r) * mean).astype(BF16))
    outs.append(value.astype(BF16))
    back = jnp.concatenate(outs, axis=1)
    back_ref[0, 0] = back
    store_share(j, own_ref, near_ref, dot_nt(back, w_ref[:, :512]).astype(BF16))


def qkv_back_call(place, at, gets, raw, cosine, sine, gains, w):
    _, slots, rows, _ = raw.shape
    width = w.shape[0]
    here = lambda *shape: pl.BlockSpec((1, 1, *shape), lambda j: (0, j, 0, 0))
    table = pl.BlockSpec((1, 1, rows, 128), lambda j: (j, at, 0, 0))
    return pl.pallas_call(
        qkv_back_kernel,
        grid=(slots,),
        in_specs=[pl.BlockSpec(memory_space=pltpu.SMEM)]
        + [here(*one.shape[2:]) for one in gets]
        + [pl.BlockSpec((1, 1, rows, 384), lambda j: (at, j, 0, 0)), table, table, whole((1, 384)), whole(w.shape)],
        out_specs=[
            here(rows, 512),
            pl.BlockSpec((1, 1, rows, width), lambda j: (jnp.minimum(j, 1), 0, 0, 0)),
            pl.BlockSpec((1, 1, rows, width), lambda j: (jnp.maximum(j - 2, 0), 0, 0, 0)),
            whole((1, 384)),
        ],
        out_shape=[
            jax.ShapeDtypeStruct((1, slots, rows, 512), BF16),
            jax.ShapeDtypeStruct((2, 1, rows, width), BF16),
            jax.ShapeDtypeStruct((2, 1, rows, width), BF16),
            jax.ShapeDtypeStruct((1, 384), F32),
        ],
        scratch_shapes=[pltpu.VMEM((2, rows, 128), F32), pltpu.VMEM((2, rows, 128), F32)],
        compiler_params=params(),
        cost_estimate=cost(8),
        name="qkv_back",
    )(place, *gets, raw, cosine, sine, gains, w)


def ffn_kernel(at, halves, *refs):
    offset_ref, x_refs, given_refs, pieces = refs[0], refs[1:5], refs[5:9], refs[9 : 9 + 3 * halves]
    refs = refs[-16:]
    act_out, outs = refs[0], refs[1:5]
    w_ref, x_ref, given_ref, act_ref, held = *refs[5:9], refs[9:11]
    sems, x_sems, given_sems, act_sems, out_sems = refs[11:]
    _, rows, width = x_ref.shape
    count = 2 * rows
    blocks, depth, span = pieces[0].shape

    def copies(j):
        return [
            pltpu.make_async_copy(
                pieces[j * halves + p].at[i],
                w_ref.at[j, pl.ds(i * depth, depth), pl.ds(pl.multiple_of(offset_ref[p], 128), span)],
                sems.at[j, p, i],
            )
            for p in range(halves)
            for i in range(blocks)
        ]

    def start(found):
        for copy in found:
            copy.start()

    def wait(found):
        for copy in found:
            copy.wait()

    tokens = slot_copies([ref.at[at] for ref in x_refs], x_ref, x_sems)
    givens = slot_copies([ref.at[at] for ref in given_refs], given_ref, given_sems)
    for found in (tokens[:2], copies(0), copies(1), copies(2), givens[:2], tokens[2:], givens[2:]):
        start(found)

    def act_copy(kind, k):
        rows_of = pl.ds(2 * k, 2)
        return pltpu.make_async_copy(act_ref.at[kind, rows_of], act_out.at[kind, rows_of], act_sems.at[kind, k])

    def part_copy(n, k):
        out = outs[k].at[:, at] if n == 0 else outs[2 + k]
        return pltpu.make_async_copy(held[n].at[k], out, out_sems.at[n, k])

    def leave_act(kind, k, value):
        act_ref[kind, pl.ds(2 * k, 2)] = value.reshape(2, rows, -1)
        act_copy(kind, k).start()

    def leave_part(n, k, value):
        held[n][k] = value.astype(BF16).reshape(2, rows, width)
        for turn in range(2):

            @pl.when(k == turn)
            def _():
                part_copy(n, turn).start()

    def arrive(k, found):
        @pl.when(k == 0)
        def _():
            wait(found)

    def step(k, carry):
        for turn in range(2):

            @pl.when(k == turn)
            def _():
                wait(tokens[2 * turn : 2 * turn + 2])

        x = x_ref[pl.ds(2 * k, 2)].reshape(count, width)
        arrive(k, copies(0))
        gate = dot_nt(x, w_ref[0])
        arrive(k, copies(1))
        up = dot_nt(x, w_ref[1])
        sig = jax.nn.sigmoid(gate)
        swish = gate * sig
        hidden = (swish * up).astype(BF16)
        leave_act(2, k, hidden)
        arrive(k, copies(2))
        for turn in range(2):

            @pl.when(k == turn)
            def _():
                wait(givens[2 * turn : 2 * turn + 2])

        hidden_back = dot_nt(given_ref[pl.ds(2 * k, 2)].reshape(count, width), w_ref[2])
        gate_back = (hidden_back * up * (sig * (1.0 + gate * (1.0 - sig)))).astype(BF16)
        leave_act(0, k, gate_back)
        up_back = (hidden_back * swish).astype(BF16)
        leave_act(1, k, up_back)
        leave_part(1, k, dot_nn(gate_back, w_ref[0]) + dot_nn(up_back, w_ref[1]))
        leave_part(0, k, dot_nn(hidden, w_ref[2]))
        return carry

    lax.fori_loop(0, 2, step, 0)
    for k in range(2):
        for kind in range(3):
            act_copy(kind, k).wait()
        for n in range(2):
            part_copy(n, k).wait()


def ffn_call(offsets, at, xs, given, pieces, before):
    pair, rows, width = xs[0].shape
    halves = len(pieces[0])
    blocks, depth, _ = pieces[0][0].shape
    hidden = blocks * depth
    part, act = (2, rows, width), (3, 4, rows, hidden)
    both = (2, pair, rows, width)
    parts = [piece for row in pieces for piece in row]
    first = 9 + len(parts)
    before = before or []
    return pl.pallas_call(
        functools.partial(ffn_kernel, at, halves),
        in_specs=[pl.BlockSpec(memory_space=pltpu.SMEM)] + [pl.BlockSpec(memory_space=pl.ANY)] * (8 + len(parts) + len(before)),
        out_specs=[pl.BlockSpec(memory_space=pl.ANY)] * 5,
        out_shape=[jax.ShapeDtypeStruct(shape, BF16) for shape in (act, both, both, part, part)],
        input_output_aliases={first + i: 1 + i for i in range(len(before))},
        scratch_shapes=[
            pltpu.VMEM((3, hidden, width), BF16),
            pltpu.VMEM((4, rows, width), BF16),
            pltpu.VMEM((4, rows, width), BF16),
            pltpu.VMEM(act, BF16),
        ]
        + [pltpu.VMEM((2, *part), BF16)] * 2
        + [
            pltpu.SemaphoreType.DMA((3, halves, blocks)),
            pltpu.SemaphoreType.DMA((4,)),
            pltpu.SemaphoreType.DMA((4,)),
            pltpu.SemaphoreType.DMA((3, 2)),
            pltpu.SemaphoreType.DMA((2, 2)),
        ],
        compiler_params=params(),
        cost_estimate=cost(22),
        name="ffn",
    )(offsets, *xs, *given, *parts, *before)


def weight_kernel(halves, offset_ref, *refs):
    lefts, rights = refs[0:2], refs[2:6]
    outs, total_ref = refs[6 : 6 + halves], refs[6 + halves]
    total = 0.0
    for s, left in enumerate(lefts):
        a = left[0]
        total = total + dot_tn(a.reshape(-1, a.shape[-1]), jnp.concatenate([ref[s] for ref in rights]))
    total_ref[...] = total.astype(BF16)
    blocks, depth, span = outs[0].shape
    for p in range(halves):
        start = pl.multiple_of(offset_ref[p], 128)
        for i in range(blocks):
            outs[p][i] = total_ref[i * depth : (i + 1) * depth, pl.ds(start, span)]


def weight_call(offsets, kind, acts, rights, halves, blocks):
    units, width = acts[0].shape[-1], rights[0].shape[-1]
    unit = (1, *acts[0].shape[1:])
    part = (blocks, units // blocks, width // halves)
    return pl.pallas_call(
        functools.partial(weight_kernel, halves),
        grid=(1,),
        in_specs=[pl.BlockSpec(memory_space=pltpu.SMEM)]
        + [pl.BlockSpec(unit, lambda j: (kind, 0, 0, 0))] * 2
        + [whole(one.shape) for one in rights],
        out_specs=[whole(part)] * halves,
        out_shape=[jax.ShapeDtypeStruct(part, BF16)] * halves,
        scratch_shapes=[pltpu.VMEM((units, width), BF16)],
        compiler_params=params(),
        cost_estimate=cost(10),
        name="weight",
    )(offsets, *acts, *rights)


def small_weight_kernel(halves, near, count, place_ref, offset_ref, *refs):
    lefts, rights, outs, total_ref = refs[:count], refs[count : -halves - 1], refs[-halves - 1 : -1], refs[-1]
    t = place_ref[1]
    total = 0.0
    for s in range(2):
        a = lefts[0][s] if count == 1 else lefts[s][0]
        pieces = [ref[s] for ref in rights] if len(rights) == 4 else [ref[...] for ref in rights[4 * s : 4 * s + 4]]
        total = total + dot_tn(a.reshape(-1, a.shape[-1]), jnp.concatenate(pieces))
    total_ref[...] = total.astype(BF16)
    blocks, _, span = outs[0].shape
    for p in range(halves):
        for e in range(blocks):
            if near:
                outs[p][e] = total_ref[:, pl.ds(pl.multiple_of(offset_ref[p] + (t ^ e) * span, 128), span)]
            else:
                outs[p][e] = total_ref[:, e * span : (e + 1) * span]


def small_weight_call(place, offsets, lefts, rights, halves, blocks, near):
    rows, width = lefts[0].shape[-1], rights[0].shape[-1]
    part = (blocks, rows, width // blocks // halves)
    return pl.pallas_call(
        functools.partial(small_weight_kernel, halves, near, len(lefts)),
        in_specs=[pl.BlockSpec(memory_space=pltpu.SMEM)] * 2
        + [pl.BlockSpec(memory_space=pltpu.VMEM)] * (len(lefts) + len(rights)),
        out_specs=[pl.BlockSpec(memory_space=pltpu.VMEM)] * halves,
        out_shape=[jax.ShapeDtypeStruct(part, BF16)] * halves,
        scratch_shapes=[pltpu.VMEM((rows, width), BF16)],
        compiler_params=params(),
        cost_estimate=cost(5),
        name="small_weight",
    )(place, offsets, *lefts, *rights)


def inverse_root(values):
    return lax.rsqrt(jnp.mean(values * values, axis=-1, keepdims=True) + EPS)


def norm_back(values, root, gain, given):
    mean = jnp.mean(values * gain * given, axis=-1, keepdims=True)
    return root * gain * given - values * (root * root * root) * mean


def per_device(
    sizes,
    tokens,
    positions,
    first_gain,
    query_weight,
    key_weight,
    value_weight,
    query_gain,
    key_gain,
    output_weight,
    second_gain,
    gate_weight,
    up_weight,
    down_weight,
    upstream,
):
    shards, ctx, tp = sizes["shard"], sizes["ctx"], sizes["tp"]
    groups = ("shard", "tp")
    sequences, rows, width = tokens.shape
    head_dim = query_gain.shape[0]
    depth = query_weight.shape[0]
    units = gate_weight.shape[1]
    c, t = lax.axis_index("ctx"), lax.axis_index("tp")
    place = jnp.stack([c, t]).astype(jnp.int32)
    trade = [(i * tp + k, k * ctx + i) for i in range(ctx) for k in range(tp)]

    line = Line()
    shard = lax.axis_index("shard")
    small = jnp.concatenate([query_weight, key_weight, value_weight, output_weight.T], axis=1)
    small = lax.ppermute(small, ("ctx", "tp"), trade)
    blocks_attn = trade_tp(small, tp)
    w_attn = join_shard(blocks_attn.reshape(tp * depth, -1), shards)

    large = jnp.stack([gate_weight.T, up_weight.T, down_weight]).reshape(3, ctx, units // ctx, depth)
    large = lax.all_to_all(large, "ctx", 1, 1, tiled=True)
    large = after(large, small).transpose(0, 2, 1, 3).reshape(3, units // ctx, ctx * depth)
    aligned = depth % 128 == 0
    starts = jnp.stack([shard, 1 - shard]) if shards == 2 else jnp.zeros((2,), jnp.int32)
    starts = (starts * (width // 2)).astype(jnp.int32)

    mine = lax.dynamic_slice_in_dim(positions, t * rows, rows, 1).astype(F32)
    places = jnp.stack(gather_ctx(mine))
    freqs = jnp.exp(-math.log(THETA) * jnp.arange(0, head_dim, 2).astype(F32) / head_dim)
    angles = places[..., None] * freqs
    cosine, sine = jnp.cos(angles), jnp.sin(angles)
    cosine = jnp.concatenate([cosine] * 4, axis=-1)
    sine = jnp.concatenate([sine] * 4, axis=-1)
    gains = jnp.concatenate([jnp.tile(query_gain, 4), jnp.tile(key_gain, 2)])[None]

    x = tokens.astype(F32)
    root = inverse_root(x)
    first = (x * root * first_gain).astype(BF16)
    given = upstream.astype(F32)

    pair = range(sequences)
    first_all = gather_ctx(first)
    one = line.run(qkv_call, place, first_all, w_attn, cosine, sine, gains)
    heads, raw = exchange_heads(one[0], (one[1], one[2], one[1], one[3])), one[4]
    lines = [lax.all_gather(after(large[0], blocks_attn), "tp", axis=0, tiled=False)]
    for j in (1, 2):
        lines.append(lax.all_gather(after(large[j], *heads), "tp", axis=0, tiled=False))
    w_ffn = [gather_shard(one, shards) for one in lines]
    upstream_all = gather_ctx(after(upstream, raw))
    heads = after(heads, w_ffn[0][-1], *upstream_all)
    own, other, o, lse = line.run(attend_call, place, heads)
    own = after(own, lines[1])
    mixed, own, near = line.run(out_call, place, [own, to_tp(other, 1)], w_attn)
    mine, away = line.run(lambda got, own: add_near(own, got), lax.ppermute(near, "ctx", NEAR), own)

    def middle_of(far, mine):
        middle = x + (mine + far.astype(F32))
        middle_root = inverse_root(middle)
        return (middle * middle_root * second_gain).astype(BF16), middle, middle_root

    mine = after(mine, lines[2], w_ffn[1][-1])
    second, middle, middle_root = line.run(middle_of, lax.ppermute(away, "ctx", FAR), mine)
    seconds = gather_ctx(second)
    ffn = []
    for s in pair:
        before = ffn[-1][1:3] if ffn else None
        ffn.append(line.run(ffn_call, starts, s, seconds, upstream_all, w_ffn, before))
    out_shares = ffn[-1][1:3]

    back_rows, mixed_back_all, backs_sent = [], [], []

    def turn_back(second_back, s):
        middle_back = given[s] + norm_back(middle[s], middle_root[s], second_gain, second_back)
        return middle_back.astype(BF16), middle_back, jnp.sum(second_back * middle[s] * middle_root[s], axis=0)

    def turn(s, call, *shares):
        low, middle_back, share = line.run(lambda first, *rest: turn_back(call(first, *rest), s), *shares)
        back_rows.append(middle_back)
        mixed_back_all.append(gather_ctx(low))
        return share

    def back_out(s):
        own, other = line.run(out_back_call, place, mixed_back_all[s], w_attn)
        backs_sent.append([own, to_tp(other, 1)])

    own, near = ffn[0][3], ffn[0][4]
    shares = own[0], *(
        lax.ppermute(value, "ctx", way) for value, way in ((own[1], FAR), (near[0], NEAR), (near[1], CROSS))
    )
    second_share = turn(0, lambda *parts: sum(part.astype(F32) for part in parts), *shares)
    mine, away = line.run(lambda got, own: add_near(own, got), lax.ppermute(ffn[1][4], "ctx", NEAR), ffn[1][3])
    away = lax.ppermute(away, "ctx", FAR)
    near = aligned and shards == 2
    count = shards * tp
    small = 2 if near else 1, tp if near else 1, near
    halves = 2 if shards == 2 else 1
    sums, g_ffn = [], []

    def weight(kind):
        rights = upstream_all if kind == 2 else seconds
        sums.append(line.run(weight_call, starts, kind, [one[0] for one in ffn], rights, halves, tp))

    def send(kind):
        parts = sums[kind]
        return send_shard(after(parts, g_ffn[-1]) if g_ffn else parts, shards)

    def add(kind, moved):
        added = line.run(add_shard, moved, sums[kind])
        sums[kind] = added
        g_ffn.append(added)

    def scatter(kind):
        return lax.psum_scatter(g_ffn[kind], "tp", scatter_dimension=0, tiled=False)

    weight(0)
    moved = send(0)
    weight(1)
    back_out(0)
    second_share = second_share + turn(1, lambda far, own: own + far.astype(F32), away, mine)
    weight(2)
    back_out(1)
    add(0, moved)
    moved = send(1)
    near_sum, away = line.run(
        lambda got, own: add_near(own, got), lax.ppermute(after(out_shares[1], backs_sent[0]), "ctx", NEAR), out_shares[0]
    )
    far_sum = lax.ppermute(away, "ctx", FAR)
    half = line.run(attend_back_call, after(place, *backs_sent[1]), 0, heads, backs_sent[0], o, lse)
    got = [exchange_heads(half[0], half[1:])]
    given_all = [*mixed_back_all[0], *mixed_back_all[1]]
    out_parts = line.run(small_weight_call, place, starts, [mixed], given_all, *small)
    out_moved = lax.ppermute(out_parts[1], "shard", [(0, 1), (1, 0)]) if near else None
    add(1, moved)
    moved = send(2)
    result = line.run(lambda far, mine: ((middle + mine) + far.astype(F32)).astype(BF16), far_sum, near_sum)
    full = line.run(attend_back_call, place, 1, heads, backs_sent[1], o, lse)
    got.append(exchange_heads(full[0], full[1:]))
    add(2, moved)
    g_ffn = [scatter(kind) for kind in range(3)]
    def last(far, mine, s):
        first_back = mine[0] + far[0].astype(F32)
        gradient = back_rows[s] + norm_back(x[s], root[s], first_gain, first_back)
        return jnp.sum(first_back * x[s] * root[s], axis=0), gradient

    backs, firsts, head_share, first_share, gradients = [], [], 0.0, 0.0, []
    for s in pair:
        back, own, other, share = line.run(qkv_back_call, place, s, got[s], raw, cosine, sine, gains, w_attn)
        backs.append(back)
        head_share = head_share + share
        other = lax.ppermute(other, "ctx", NEAR)
        if s == 0:
            mine, away = line.run(lambda got, own: add_near(own, got), other, own)
            firsts.append((lax.ppermute(away, "ctx", FAR), mine))
    parts = line.run(small_weight_call, place, starts, backs, first_all, *small)
    moved = lax.ppermute(parts[1], "shard", [(0, 1), (1, 0)]) if near else None
    mine, away = line.run(lambda got, own: add_near(own, got), other, own)
    firsts.append((lax.ppermute(away, "ctx", FAR), mine))
    for s in pair:
        share, gradient = line.run(lambda a, b: last(a, b, s), *firsts[s])
        first_share = first_share + share
        gradients.append(gradient)
    shares = jnp.concatenate([first_share, second_share, head_share[0]])
    shares = sum_all(shares, [(name, sizes[name]) for name in ("ctx", "shard", "tp")])

    if near:
        both = lambda a, b: (a.astype(F32) + b.astype(F32)).astype(BF16)
        g_attn = line.run(
            lambda a, b: jnp.concatenate([both(a, b), both(out_moved, out_parts[0])], axis=1), moved, parts[0]
        )
        g_attn = exchange_tp([g_attn[e] for e in range(tp)])
    else:
        g_attn = jnp.concatenate([parts[0][0], out_parts[0][0]])
        g_attn = g_attn.reshape(-1, count, width // count).transpose(1, 0, 2)
        g_attn = lax.psum_scatter(g_attn, groups, scatter_dimension=0, tiled=False)
    def settle(g):
        g = g.reshape(3, units, depth).astype(F32)
        return g[0].T, g[1].T, g[2]

    g_ffn = jnp.stack(g_ffn).reshape(3, units // ctx, ctx, depth).transpose(0, 2, 1, 3)
    g_ffn = lax.all_to_all(g_ffn, "ctx", 1, 1, tiled=True)
    g_ffn = line.run(settle, g_ffn)

    if near:
        g_attn = line.run(lambda *parts: sum(part.astype(F32) for part in parts).astype(BF16), *g_attn)
    g_attn = lax.ppermute(g_attn, ("ctx", "tp"), trade).astype(F32)
    heads_end = query_weight.shape[1]
    pairs = key_weight.shape[1]

    head_total = shares[2 * width :]
    return (
        result,
        jnp.stack(gradients),
        g_attn[:heads_end].T,
        g_attn[heads_end : heads_end + pairs].T,
        g_attn[heads_end + pairs : heads_end + 2 * pairs].T,
        g_attn[heads_end + 2 * pairs :],
        *g_ffn,
        shares[:width],
        shares[width : 2 * width],
        jnp.sum(head_total[: 4 * head_dim].reshape(4, head_dim), axis=0),
        jnp.sum(head_total[4 * head_dim :].reshape(2, head_dim), axis=0),
    )


def solution(mesh):
    rows = P("shard", ("ctx", "tp"), None)
    wide = P(("shard", "ctx"), "tp")
    tall = P("tp", ("shard", "ctx"))
    none = P()
    in_specs = (
        rows, P("shard", "ctx"), none, wide, wide, wide, none, none, tall, none, wide, wide, tall, rows,
    )
    out_specs = (rows, rows, wide, wide, wide, tall, wide, wide, tall, none, none, none, none)
    sizes = {name: mesh.shape[name] for name in ("shard", "ctx", "tp")}
    return jax.shard_map(
        functools.partial(per_device, sizes), mesh=mesh, in_specs=in_specs, out_specs=out_specs, check_vma=False
    )
```

```python
import functools
import math

import jax
import jax.numpy as jnp
from jax import lax
from jax.experimental import pallas as pl
from jax.experimental.pallas import tpu as pltpu
from jax.sharding import PartitionSpec as P

EPS = 1e-05
THETA = 1000000.0
LOG2E = 1.4426950408889634
F32 = jnp.float32
BF16 = jnp.bfloat16
NEAR = [(0, 1), (1, 0), (2, 3), (3, 2)]
FAR = [(0, 2), (2, 0), (1, 3), (3, 1)]
CROSS = [(0, 3), (3, 0), (1, 2), (2, 1)]
LIMIT = 56 * 1024 * 1024


def dot_nn(left, right):
    return lax.dot_general(left, right, (((1,), (0,)), ((), ())), preferred_element_type=F32)


def dot_nt(left, right):
    return lax.dot_general(left, right, (((1,), (1,)), ((), ())), preferred_element_type=F32)


def dot_tn(left, right):
    return lax.dot_general(left, right, (((0,), (0,)), ((), ())), preferred_element_type=F32)


def swap_bits(j):
    return ((j & 1) << 1) | (j >> 1)


def gather_ctx(own):
    far = lax.ppermute(own, "ctx", FAR)
    near = lax.ppermute(own, "ctx", NEAR)
    return [own, far, near, lax.ppermute(far, "ctx", NEAR)]


def add_near(own, got):
    return own[0].astype(F32) + got[0].astype(F32), (own[1].astype(F32) + got[1].astype(F32)).astype(BF16)


def reduce_near(own, near):
    return add_near(own, lax.ppermute(near, "ctx", NEAR))


def reduce_far(mine, away):
    return mine + lax.ppermute(away, "ctx", FAR).astype(F32)


def reduce_ctx(own, near):
    got = lax.ppermute(own[1], "ctx", FAR), lax.ppermute(near[0], "ctx", NEAR), lax.ppermute(near[1], "ctx", CROSS)
    return own[0].astype(F32) + got[0].astype(F32) + got[1].astype(F32) + got[2].astype(F32)


def to_tp(value, e):
    return lax.ppermute(value, "tp", [(i, i ^ e) for i in range(4)])


def exchange_tp(blocks):
    return [blocks[0]] + [to_tp(blocks[e], e) for e in range(1, len(blocks))]


def exchange_heads(q_same, kv):
    return [q_same, *exchange_tp(kv)]


def gather_shard(own, shards):
    if shards == 2:
        return [own, lax.ppermute(own, "shard", [(0, 1), (1, 0)])]
    every = lax.all_gather(own, "shard", axis=0, tiled=False)
    return [every.transpose(1, 2, 0, 3).reshape(*own.shape[:2], -1)]


def send_shard(parts, shards):
    if shards == 2:
        return lax.ppermute(parts[1], "shard", [(0, 1), (1, 0)])
    blocks, units, width = parts[0].shape
    every = parts[0].reshape(blocks, units, shards, width // shards).transpose(2, 0, 1, 3)
    return lax.psum_scatter(every, "shard", scatter_dimension=0, tiled=False)


def add_shard(got, parts):
    return (parts[0].astype(F32) + got.astype(F32)).astype(BF16) if len(parts) == 2 else got


def after(value, *others):
    return lax.optimization_barrier((value, *others))[0]


class Line:
    def __init__(self):
        self.last = ()

    def run(self, call, first, *others):
        result = call(after(first, *self.last), *others)
        self.last = (jax.tree.leaves(result)[0],)
        return result


def trade_tp(own, count):
    got = [own]
    for k in range(1, count):
        got.append(lax.ppermute(own, "tp", [(i, i ^ k) for i in range(count)]))
    index = lax.axis_index("tp")
    slots = []
    for slot in range(count):
        value = got[slot]
        for at in range(1, count):
            value = jnp.where(index == at, got[slot ^ at], value)
        slots.append(value)
    return jnp.stack(slots)


def join_shard(own, shards):
    if shards == 2:
        other = lax.ppermute(own, "shard", [(0, 1), (1, 0)])
        index = lax.axis_index("shard")
        return jnp.concatenate([jnp.where(index == 0, own, other), jnp.where(index == 0, other, own)])
    return lax.all_gather(own, "shard", axis=0, tiled=True)


def sum_all(vector, sizes):
    for name, size in sizes:
        step = 1
        while step < size:
            other = lax.ppermute(vector, name, [(i, i ^ step) for i in range(size)])
            vector = vector + other
            step *= 2
    return vector


def params():
    return pltpu.CompilerParams(vmem_limit_bytes=LIMIT)


def cost(micros):
    return pl.CostEstimate(flops=int(micros * 1.0e9), transcendentals=0, bytes_accessed=int(micros * 1.0e6))


def slot_copies(refs, held, sems):
    return [pltpu.make_async_copy(ref, held.at[k], sems.at[k]) for k, ref in enumerate(refs)]


def start_slots(refs, held, sems):
    @pl.when(pl.program_id(0) == 0)
    def _():
        for copy in slot_copies(refs, held, sems):
            copy.start()


def wait_slot(refs, held, sems, step=1):
    for k, copy in enumerate(slot_copies(refs, held, sems)):

        @pl.when(pl.program_id(0) == k // step)
        def _():
            copy.wait()


def lanes_low(rows):
    return lax.broadcasted_iota(jnp.int32, (rows, 128), 1) < 64


def pack(first, second, low):
    return jnp.where(low, first, second)


def head_sums(values):
    rows = lax.broadcasted_iota(jnp.int32, (128, 128), 0) >> 6
    columns = lax.broadcasted_iota(jnp.int32, (128, 128), 1) >> 6
    ones = jnp.where(rows == columns, 1.0, 0.0).astype(BF16)
    high = values.astype(BF16)
    rest = values - high.astype(F32)
    low = rest.astype(BF16)
    return dot_nn(high, ones) + dot_nn(low, ones)


def qkv_kernel(place_ref, *refs):
    x_refs, (w_ref, cos_ref, sin_ref, gain_ref) = refs[:4], refs[4:8]
    q_same, kv_same, beside, kv_other, raw_ref, x_ref, q_ref, kv_ref, sems = refs[8:]
    side, s, j = place_ref[1] & 1, pl.program_id(0), pl.program_id(1)
    rows = x_ref.shape[2]
    copies = slot_copies(x_refs, x_ref, sems)

    @pl.when((s == 0) & (j == 0))
    def _():
        for copy in copies:
            copy.start()

    for k, copy in enumerate(copies):

        @pl.when((s == 0) & (j == k))
        def _():
            copy.wait()

    y = dot_nn(x_ref[j, s], w_ref[:, :512])
    raw_ref[0, 0] = y[:, :384]
    low = lanes_low(rows)
    early = (lax.broadcasted_iota(jnp.int32, (rows, 128), 1) & 32) == 0
    cosine, sine = cos_ref[0, 0], sin_ref[0, 0]
    turned = []
    for b in range(3):
        u = y[:, b * 128 : (b + 1) * 128]
        r = lax.rsqrt(head_sums(u * u) * (1.0 / 64.0) + EPS)
        n = u * r * gain_ref[:, b * 128 : (b + 1) * 128]
        other = jnp.where(early, -pltpu.roll(n, 96, 1), pltpu.roll(n, 32, 1))
        turned.append(n * cosine + other * sine)
    key, value = turned[2], y[:, 384:512]
    q_ref[0] = (turned[0] * 0.125).astype(BF16)
    q_ref[1] = (turned[1] * 0.125).astype(BF16)
    kv_ref[0] = pack(key, pltpu.roll(value, 64, 1), low).astype(BF16)
    kv_ref[1] = pack(pltpu.roll(key, 64, 1), value, low).astype(BF16)
    q_same[0, 0] = q_ref[side]
    kv_same[0, 0] = kv_ref[side]
    beside[0, 0, :rows] = q_ref[1 - side]
    beside[0, 0, rows:] = kv_ref[1 - side]
    kv_other[0, 0] = kv_ref[1 - side]


def step_block(*shape):
    return pl.BlockSpec((1, 1, *shape), lambda s, j: (s, j, 0, 0))


def table_block(*shape):
    return pl.BlockSpec((1, 1, *shape), lambda s, j: (j, s, 0, 0))


def whole2(shape):
    return pl.BlockSpec(shape, lambda s, j: (0,) * len(shape))


def qkv_call(place, xs, w, cosine, sine, gains):
    slots = len(xs)
    pair, rows, width = xs[0].shape
    talls = (rows, rows, 2 * rows, rows)
    return pl.pallas_call(
        qkv_kernel,
        grid=(pair, slots),
        in_specs=[pl.BlockSpec(memory_space=pltpu.SMEM)]
        + [pl.BlockSpec(memory_space=pl.ANY)] * slots
        + [whole2(w.shape), table_block(rows, 128), table_block(rows, 128), whole2((1, 384))],
        out_specs=[step_block(tall, 128) for tall in talls] + [step_block(rows, 384)],
        out_shape=[jax.ShapeDtypeStruct((pair, slots, tall, 128), BF16) for tall in talls]
        + [jax.ShapeDtypeStruct((pair, slots, rows, 384), F32)],
        scratch_shapes=[
            pltpu.VMEM((slots, pair, rows, width), BF16),
            pltpu.VMEM((2, rows, 128), BF16),
            pltpu.VMEM((2, rows, 128), BF16),
            pltpu.SemaphoreType.DMA((slots,)),
        ],
        compiler_params=params(),
        cost_estimate=cost(15),
        name="qkv",
    )(place, *xs, w, cosine, sine, gains)


def lay_keys(place_ref, refs, kv_ref):
    c, t = place_ref[0], place_ref[1]
    for e, ref in enumerate(refs):
        for j in range(ref.shape[1]):
            kv_ref[4 * (c ^ swap_bits(j)) + (t ^ e)] = ref[0, j, ref.shape[2] - kv_ref.shape[1] :]


def lay_rows(place_ref, own_ref, got_ref, out_ref, high):
    c, side = place_ref[0], place_ref[1] & 1
    rows = out_ref.shape[2]
    low = lanes_low(rows)
    for ref, start in ((own_ref, 2 * side), (got_ref, 2 - 2 * side)):
        for j in range(4):
            g = c ^ swap_bits(j)
            value = ref[0, j, :rows] if len(ref.shape) == 4 else ref[j, :rows]
            turned = pltpu.roll(value, 64, 1)
            zero = jnp.zeros_like(value)
            if high:
                out_ref[g, start] = jnp.where(low, zero, turned)
                out_ref[g, start + 1] = jnp.where(low, zero, value)
            else:
                out_ref[g, start] = jnp.where(low, value, zero)
                out_ref[g, start + 1] = jnp.where(low, turned, zero)


def diagonal(rows, wide, edge):
    key = lax.broadcasted_iota(jnp.int32, (rows, wide), 0)
    column = lax.broadcasted_iota(jnp.int32, (rows, wide), 1)
    return (key <= (column & (rows - 1))) | (column >= edge)


def whole(shape):
    return pl.BlockSpec(shape, lambda j: (0,) * len(shape))


def attend_kernel(place_ref, *refs):
    q_own, keys = refs[0], refs[1:5]
    own_out, other_out, o_ref, lse_ref, q_ref, kv_ref, acc_ref, sum_ref, ret_ref = refs[5:]
    c, t, g = place_ref[0], place_ref[1], pl.program_id(1)
    side, base = t & 1, t & 2
    rows = kv_ref.shape[1]
    half, wide = 2 * rows, 4 * rows

    @pl.when(g == 0)
    def _():
        lay_keys(place_ref, keys, kv_ref)
        lay_rows(place_ref, q_own, keys[1], q_ref, False)

    queries = q_ref[g].reshape(wide, 128)
    acc_ref[...] = jnp.zeros_like(acc_ref)
    sum_ref[...] = jnp.zeros_like(sum_ref)

    def add(pair, skip, allowed):
        weights = jnp.exp2(dot_nt(pair, queries[skip:]) * LOG2E)
        if allowed is not None:
            weights = jnp.where(allowed, weights, 0.0)
        sum_ref[:, skip:] += jnp.sum(weights, axis=0, keepdims=True)
        acc_ref[:, skip:] += dot_tn(pair, weights.astype(BF16))

    def body(n, carry):
        add(kv_ref[pl.ds(2 * n, 2)].reshape(2 * rows, 128), 0, None)
        return carry

    last = 4 * g + base
    lax.fori_loop(0, last >> 1, body, 0)
    add(kv_ref[last], 0, diagonal(rows, wide, half))
    add(kv_ref[last + 1], half, diagonal(rows, half, half))
    total = sum_ref[...]
    out = acc_ref[...] / total
    o_ref[0, 0] = out[64:]
    lse_ref[0, 0] = jnp.log(total) * LOG2E
    flat = jnp.transpose(out)
    low = lanes_low(rows)
    slot = swap_bits(c ^ g)
    for u in range(2):
        first, second = (flat[(2 * u + h) * rows : (2 * u + h + 1) * rows] for h in range(2))
        ret_ref[u, slot] = pack(pltpu.roll(first, 64, 1), second, low).astype(BF16)

    @pl.when(g == 3)
    def _():
        own_out[0] = ret_ref[side]
        other_out[0] = ret_ref[1 - side]


def sequence_block(shape):
    return pl.BlockSpec((1, *shape[1:]), lambda s, j: (s, 0, 0, 0))


def attend_call(place, gets):
    pair, slots, rows, _ = gets[0].shape
    wide = 4 * rows
    return pl.pallas_call(
        attend_kernel,
        grid=(pair, 4),
        in_specs=[pl.BlockSpec(memory_space=pltpu.SMEM)] + [sequence_block(one.shape) for one in gets],
        out_specs=[sequence_block(gets[0].shape)] * 2 + [step_block(64, wide), step_block(1, wide)],
        out_shape=[jax.ShapeDtypeStruct(gets[0].shape, BF16)] * 2
        + [
            jax.ShapeDtypeStruct((pair, 4, 64, wide), F32),
            jax.ShapeDtypeStruct((pair, 4, 1, wide), F32),
        ],
        scratch_shapes=[
            pltpu.VMEM((4, 4, rows, 128), BF16),
            pltpu.VMEM((4 * slots, rows, 128), BF16),
            pltpu.VMEM((128, wide), F32),
            pltpu.VMEM((1, wide), F32),
            pltpu.VMEM((2, slots, rows, 128), BF16),
        ],
        compiler_params=params(),
        cost_estimate=cost(32),
        name="attend",
    )(place, *gets)


def own_block(rows, width):
    return pl.BlockSpec((1, 1, rows, width), lambda s, j: (jnp.minimum(j, 1), s, 0, 0))


def near_block(rows, width):
    return pl.BlockSpec((1, 1, rows, width), lambda s, j: (jnp.maximum(j - 2, 0), s, 0, 0))


def store_share(j, own_ref, near_ref, part):
    @pl.when(j < 2)
    def _():
        own_ref[0, 0] = part

    @pl.when(j >= 2)
    def _():
        near_ref[0, 0] = part


def out_kernel(place_ref, get_own, get_other, w_ref, mixed_ref, own_ref, near_ref, head_ref):
    side, j = place_ref[1] & 1, pl.program_id(1)
    head_ref[side] = get_own[0, 0]
    head_ref[1 - side] = get_other[0, 0]
    mixed = jnp.concatenate([head_ref[0], head_ref[1]], axis=1)
    mixed_ref[0, 0] = mixed
    store_share(j, own_ref, near_ref, dot_nt(mixed, w_ref[:, 512:]).astype(BF16))


def out_call(place, gets, w):
    pair, slots, rows, _ = gets[0].shape
    width = w.shape[0]
    return pl.pallas_call(
        out_kernel,
        grid=(pair, slots),
        in_specs=[pl.BlockSpec(memory_space=pltpu.SMEM)] + [step_block(rows, 128)] * 2 + [whole2(w.shape)],
        out_specs=[step_block(rows, 256), own_block(rows, width), near_block(rows, width)],
        out_shape=[
            jax.ShapeDtypeStruct((pair, slots, rows, 256), BF16),
            jax.ShapeDtypeStruct((2, pair, rows, width), BF16),
            jax.ShapeDtypeStruct((2, pair, rows, width), BF16),
        ],
        scratch_shapes=[pltpu.VMEM((2, rows, 128), BF16)],
        compiler_params=params(),
        cost_estimate=cost(9),
        name="out",
    )(place, *gets, w)


def out_back_kernel(place_ref, *refs):
    x_refs, w_ref, own_out, other_out, x_ref, send_ref, sems = refs[0:4], *refs[4:]
    side, j = place_ref[1] & 1, pl.program_id(0)
    start_slots(x_refs, x_ref, sems)
    wait_slot(x_refs, x_ref, sems)
    back = dot_nn(x_ref[j], w_ref[:, 512:]).astype(BF16)
    send_ref[0] = back[:, :128]
    send_ref[1] = back[:, 128:]
    own_out[0] = send_ref[side]
    other_out[0] = send_ref[1 - side]


def out_back_call(place, xs, w):
    slots = len(xs)
    rows, width = xs[0].shape
    return pl.pallas_call(
        out_back_kernel,
        grid=(slots,),
        in_specs=[pl.BlockSpec(memory_space=pltpu.SMEM)]
        + [pl.BlockSpec(memory_space=pl.ANY)] * slots
        + [whole(w.shape)],
        out_specs=[pl.BlockSpec((1, rows, 128), lambda j: (j, 0, 0))] * 2,
        out_shape=[jax.ShapeDtypeStruct((slots, rows, 128), BF16)] * 2,
        scratch_shapes=[
            pltpu.VMEM((slots, rows, width), BF16),
            pltpu.VMEM((2, rows, 128), BF16),
            pltpu.SemaphoreType.DMA((slots,)),
        ],
        compiler_params=params(),
        cost_estimate=cost(4),
        name="out_back",
    )(place, *xs, w)


def attend_back_kernel(place_ref, *refs):
    q_own, keys, back_own, back_got = refs[0], refs[1:5], refs[5], refs[6]
    o_ref, lse_ref = refs[7], refs[8]
    own_out, outs = refs[-11], refs[-10:-6]
    q_ref, kv_ref, back_ref, dkv_ref, acc_ref, ret_ref = refs[-6:]
    c, t, g = place_ref[0], place_ref[1], pl.program_id(0)
    side, base = t & 1, t & 2
    rows = kv_ref.shape[1]
    half, wide = 2 * rows, 4 * rows

    @pl.when(g == 0)
    def _():
        lay_keys(place_ref, keys, kv_ref)
        lay_rows(place_ref, q_own, keys[1], q_ref, False)
        lay_rows(place_ref, back_own, back_got, back_ref, True)
        dkv_ref[...] = jnp.zeros_like(dkv_ref)

    queries = q_ref[g].reshape(wide, 128)
    given = back_ref[g].reshape(wide, 128)
    delta = jnp.sum(jnp.transpose(given.astype(F32))[64:] * o_ref[0, 0], axis=0, keepdims=True)
    lse = lse_ref[0, 0]
    acc_ref[...] = jnp.zeros_like(acc_ref)

    def block(pair, skip, allowed):
        probs = jnp.exp2(dot_nt(pair, queries[skip:]) * LOG2E - lse[:, skip:])
        if allowed is not None:
            probs = jnp.where(allowed, probs, 0.0)
        slopes = dot_nt(pair, given[skip:])
        score_back = (probs * (slopes - delta[:, skip:])).astype(BF16)
        acc_ref[skip:] += dot_tn(score_back, pair)
        return dot_nn(probs.astype(BF16), given[skip:]) + dot_nn(score_back, queries[skip:])

    def body(n, carry):
        pair = kv_ref[pl.ds(2 * n, 2)].reshape(2 * rows, 128)
        dkv_ref[pl.ds(2 * n, 2)] += block(pair, 0, None).reshape(2, rows, 128)
        return carry

    last = 4 * g + base
    lax.fori_loop(0, last >> 1, body, 0)
    dkv_ref[last] += block(kv_ref[last], 0, diagonal(rows, wide, half))
    dkv_ref[last + 1] += block(kv_ref[last + 1], half, diagonal(rows, half, half))
    low = lanes_low(rows)
    slot = swap_bits(c ^ g)
    for u in range(2):
        first, second = (acc_ref[(2 * u + h) * rows : (2 * u + h + 1) * rows] * 0.125 for h in range(2))
        ret_ref[u, slot] = pack(first, pltpu.roll(second, 64, 1), low).astype(BF16)

    @pl.when(g == pl.num_programs(0) - 1)
    def _():
        own_out[0] = ret_ref[side]
        outs[1][0, :, :rows] = ret_ref[1 - side]
        for e in range(4):
            for j in range(4):
                outs[e][0, j, outs[e].shape[2] - rows :] = dkv_ref[4 * (c ^ swap_bits(j)) + (t ^ e)].astype(BF16)


def attend_back_call(place, at, gets, backs, o, lse):
    _, slots, rows, _ = gets[0].shape
    wide = 4 * rows
    block = lambda one: pl.BlockSpec((1, *one.shape[1:]), lambda g: (at, 0, 0, 0))
    return pl.pallas_call(
        attend_back_kernel,
        grid=(4,),
        in_specs=[pl.BlockSpec(memory_space=pltpu.SMEM)]
        + [block(one) for one in gets]
        + [whole(one.shape) for one in backs]
        + [pl.BlockSpec((1, 1, tall, wide), lambda g: (at, g, 0, 0)) for tall in (64, 1)],
        out_specs=[whole((1, *one.shape[1:])) for one in gets],
        out_shape=[jax.ShapeDtypeStruct((1, *one.shape[1:]), BF16) for one in gets],
        scratch_shapes=[
            pltpu.VMEM((4, 4, rows, 128), BF16),
            pltpu.VMEM((4 * slots, rows, 128), BF16),
            pltpu.VMEM((4, 4, rows, 128), BF16),
            pltpu.VMEM((4 * slots, rows, 128), F32),
            pltpu.VMEM((wide, 128), F32),
            pltpu.VMEM((2, slots, rows, 128), BF16),
        ],
        compiler_params=params(),
        cost_estimate=cost(8),
        name="attend_back",
    )(place, *gets, *backs, o, lse)


def qkv_back_kernel(place_ref, *refs):
    q_own, keys, (raw_ref, cos_ref, sin_ref, gain_ref, w_ref) = refs[0], refs[1:5], refs[5:10]
    back_ref, own_ref, near_ref, share_ref, head_ref, pair_ref = refs[10:]
    side, j = place_ref[1] & 1, pl.program_id(0)
    rows = raw_ref.shape[2]
    head_ref[side] = q_own[0, 0].astype(F32)
    head_ref[1 - side] = keys[1][0, 0, :rows].astype(F32)
    pair_ref[side] = keys[0][0, 0].astype(F32) + keys[2][0, 0].astype(F32)
    pair_ref[1 - side] = keys[1][0, 0, rows:].astype(F32) + keys[3][0, 0].astype(F32)
    low = lanes_low(rows)
    early = (lax.broadcasted_iota(jnp.int32, (rows, 128), 1) & 32) == 0
    cosine, sine = cos_ref[0, 0], sin_ref[0, 0]

    @pl.when(j == 0)
    def _():
        share_ref[...] = jnp.zeros_like(share_ref)

    even, odd = pair_ref[0], pair_ref[1]
    key = pack(even, pltpu.roll(odd, 64, 1), low)
    value = pack(pltpu.roll(even, 64, 1), odd, low)
    outs = []
    for b, given in enumerate((head_ref[0], head_ref[1], key)):
        z = sine * given
        cotangent = given * cosine + jnp.where(early, pltpu.roll(z, 96, 1), -pltpu.roll(z, 32, 1))
        u = raw_ref[0, 0, :, b * 128 : (b + 1) * 128]
        gain = gain_ref[:, b * 128 : (b + 1) * 128]
        r = lax.rsqrt(head_sums(u * u) * (1.0 / 64.0) + EPS)
        mean = head_sums(u * gain * cotangent) * (1.0 / 64.0)
        share_ref[:, b * 128 : (b + 1) * 128] += jnp.sum(cotangent * u * r, axis=0, keepdims=True)
        outs.append((r * gain * cotangent - u * (r * r * r) * mean).astype(BF16))
    outs.append(value.astype(BF16))
    back = jnp.concatenate(outs, axis=1)
    back_ref[0, 0] = back
    store_share(j, own_ref, near_ref, dot_nt(back, w_ref[:, :512]).astype(BF16))


def qkv_back_call(place, at, gets, raw, cosine, sine, gains, w):
    _, slots, rows, _ = raw.shape
    width = w.shape[0]
    here = lambda *shape: pl.BlockSpec((1, 1, *shape), lambda j: (0, j, 0, 0))
    table = pl.BlockSpec((1, 1, rows, 128), lambda j: (j, at, 0, 0))
    return pl.pallas_call(
        qkv_back_kernel,
        grid=(slots,),
        in_specs=[pl.BlockSpec(memory_space=pltpu.SMEM)]
        + [here(*one.shape[2:]) for one in gets]
        + [pl.BlockSpec((1, 1, rows, 384), lambda j: (at, j, 0, 0)), table, table, whole((1, 384)), whole(w.shape)],
        out_specs=[
            here(rows, 512),
            pl.BlockSpec((1, 1, rows, width), lambda j: (jnp.minimum(j, 1), 0, 0, 0)),
            pl.BlockSpec((1, 1, rows, width), lambda j: (jnp.maximum(j - 2, 0), 0, 0, 0)),
            whole((1, 384)),
        ],
        out_shape=[
            jax.ShapeDtypeStruct((1, slots, rows, 512), BF16),
            jax.ShapeDtypeStruct((2, 1, rows, width), BF16),
            jax.ShapeDtypeStruct((2, 1, rows, width), BF16),
            jax.ShapeDtypeStruct((1, 384), F32),
        ],
        scratch_shapes=[pltpu.VMEM((2, rows, 128), F32), pltpu.VMEM((2, rows, 128), F32)],
        compiler_params=params(),
        cost_estimate=cost(8),
        name="qkv_back",
    )(place, *gets, raw, cosine, sine, gains, w)


def ffn_kernel(at, halves, *refs):
    offset_ref, x_refs, given_refs, pieces = refs[0], refs[1:5], refs[5:9], refs[9 : 9 + 3 * halves]
    refs = refs[-16:]
    act_out, outs = refs[0], refs[1:5]
    w_ref, x_ref, given_ref, act_ref, held = *refs[5:9], refs[9:11]
    sems, x_sems, given_sems, act_sems, out_sems = refs[11:]
    _, rows, width = x_ref.shape
    count = 2 * rows
    blocks, depth, span = pieces[0].shape

    def copies(j):
        return [
            pltpu.make_async_copy(
                pieces[j * halves + p].at[i],
                w_ref.at[j, pl.ds(i * depth, depth), pl.ds(pl.multiple_of(offset_ref[p], 128), span)],
                sems.at[j, p, i],
            )
            for p in range(halves)
            for i in range(blocks)
        ]

    def start(found):
        for copy in found:
            copy.start()

    def wait(found):
        for copy in found:
            copy.wait()

    tokens = slot_copies([ref.at[at] for ref in x_refs], x_ref, x_sems)
    givens = slot_copies([ref.at[at] for ref in given_refs], given_ref, given_sems)
    for found in (tokens[:2], copies(0), copies(1), copies(2), givens[:2], tokens[2:], givens[2:]):
        start(found)

    def act_copy(kind, k):
        rows_of = pl.ds(2 * k, 2)
        return pltpu.make_async_copy(act_ref.at[kind, rows_of], act_out.at[kind, rows_of], act_sems.at[kind, k])

    def part_copy(n, k):
        out = outs[k].at[:, at] if n == 0 else outs[2 + k]
        return pltpu.make_async_copy(held[n].at[k], out, out_sems.at[n, k])

    def leave_act(kind, k, value):
        act_ref[kind, pl.ds(2 * k, 2)] = value.reshape(2, rows, -1)
        act_copy(kind, k).start()

    def leave_part(n, k, value):
        held[n][k] = value.astype(BF16).reshape(2, rows, width)
        for turn in range(2):

            @pl.when(k == turn)
            def _():
                part_copy(n, turn).start()

    def arrive(k, found):
        @pl.when(k == 0)
        def _():
            wait(found)

    def step(k, carry):
        for turn in range(2):

            @pl.when(k == turn)
            def _():
                wait(tokens[2 * turn : 2 * turn + 2])

        x = x_ref[pl.ds(2 * k, 2)].reshape(count, width)
        arrive(k, copies(0))
        gate = dot_nt(x, w_ref[0])
        arrive(k, copies(1))
        up = dot_nt(x, w_ref[1])
        sig = jax.nn.sigmoid(gate)
        swish = gate * sig
        hidden = (swish * up).astype(BF16)
        leave_act(2, k, hidden)
        arrive(k, copies(2))
        for turn in range(2):

            @pl.when(k == turn)
            def _():
                wait(givens[2 * turn : 2 * turn + 2])

        hidden_back = dot_nt(given_ref[pl.ds(2 * k, 2)].reshape(count, width), w_ref[2])
        gate_back = (hidden_back * up * (sig * (1.0 + gate * (1.0 - sig)))).astype(BF16)
        leave_act(0, k, gate_back)
        up_back = (hidden_back * swish).astype(BF16)
        leave_act(1, k, up_back)
        leave_part(1, k, dot_nn(gate_back, w_ref[0]) + dot_nn(up_back, w_ref[1]))
        leave_part(0, k, dot_nn(hidden, w_ref[2]))
        return carry

    lax.fori_loop(0, 2, step, 0)
    for k in range(2):
        for kind in range(3):
            act_copy(kind, k).wait()
        for n in range(2):
            part_copy(n, k).wait()


def ffn_call(offsets, at, xs, given, pieces, before):
    pair, rows, width = xs[0].shape
    halves = len(pieces[0])
    blocks, depth, _ = pieces[0][0].shape
    hidden = blocks * depth
    part, act = (2, rows, width), (3, 4, rows, hidden)
    both = (2, pair, rows, width)
    parts = [piece for row in pieces for piece in row]
    first = 9 + len(parts)
    before = before or []
    return pl.pallas_call(
        functools.partial(ffn_kernel, at, halves),
        in_specs=[pl.BlockSpec(memory_space=pltpu.SMEM)] + [pl.BlockSpec(memory_space=pl.ANY)] * (8 + len(parts) + len(before)),
        out_specs=[pl.BlockSpec(memory_space=pl.ANY)] * 5,
        out_shape=[jax.ShapeDtypeStruct(shape, BF16) for shape in (act, both, both, part, part)],
        input_output_aliases={first + i: 1 + i for i in range(len(before))},
        scratch_shapes=[
            pltpu.VMEM((3, hidden, width), BF16),
            pltpu.VMEM((4, rows, width), BF16),
            pltpu.VMEM((4, rows, width), BF16),
            pltpu.VMEM(act, BF16),
        ]
        + [pltpu.VMEM((2, *part), BF16)] * 2
        + [
            pltpu.SemaphoreType.DMA((3, halves, blocks)),
            pltpu.SemaphoreType.DMA((4,)),
            pltpu.SemaphoreType.DMA((4,)),
            pltpu.SemaphoreType.DMA((3, 2)),
            pltpu.SemaphoreType.DMA((2, 2)),
        ],
        compiler_params=params(),
        cost_estimate=cost(22),
        name="ffn",
    )(offsets, *xs, *given, *parts, *before)


def weight_kernel(halves, offset_ref, *refs):
    lefts, rights = refs[0:2], refs[2:6]
    outs, (total_ref, right_ref) = refs[6 : 6 + halves], refs[6 + halves :]
    j = pl.program_id(0)
    rows = rights[0].shape[1]

    @pl.when(j == 0)
    def _():
        for s in range(2):
            for k, ref in enumerate(rights):
                right_ref[s, k * rows : (k + 1) * rows] = ref[s]

    total = 0.0
    for s, left in enumerate(lefts):
        a = left[0]
        total = total + dot_tn(a.reshape(-1, a.shape[-1]), right_ref[s])
    third = total.shape[0]
    total_ref[pl.ds(pl.multiple_of(j * third, 128), third)] = total.astype(BF16)
    blocks, depth, span = outs[0].shape

    @pl.when(j == 2)
    def _():
        for p in range(halves):
            start = pl.multiple_of(offset_ref[p], 128)
            for i in range(blocks):
                outs[p][i] = total_ref[i * depth : (i + 1) * depth, pl.ds(start, span)]


def weight_call(offsets, kind, acts, rights, halves, blocks):
    units, width = acts[0].shape[-1], rights[0].shape[-1]
    unit = (1, *acts[0].shape[1:3], units // 3)
    part = (blocks, units // blocks, width // halves)
    return pl.pallas_call(
        functools.partial(weight_kernel, halves),
        grid=(3,),
        in_specs=[pl.BlockSpec(memory_space=pltpu.SMEM)]
        + [pl.BlockSpec(unit, lambda j: (kind, 0, 0, j))] * 2
        + [whole(one.shape) for one in rights],
        out_specs=[whole(part)] * halves,
        out_shape=[jax.ShapeDtypeStruct(part, BF16)] * halves,
        scratch_shapes=[pltpu.VMEM((units, width), BF16), pltpu.VMEM((2, 4 * rights[0].shape[1], width), BF16)],
        compiler_params=params(),
        cost_estimate=cost(10),
        name="weight",
    )(offsets, *acts, *rights)


def small_weight_kernel(halves, near, count, place_ref, offset_ref, *refs):
    lefts, rights, outs, total_ref = refs[:count], refs[count : -halves - 1], refs[-halves - 1 : -1], refs[-1]
    t = place_ref[1]
    total = 0.0
    for s in range(2):
        a = lefts[0][s] if count == 1 else lefts[s][0]
        pieces = [ref[s] for ref in rights] if len(rights) == 4 else [ref[...] for ref in rights[4 * s : 4 * s + 4]]
        total = total + dot_tn(a.reshape(-1, a.shape[-1]), jnp.concatenate(pieces))
    total_ref[...] = total.astype(BF16)
    blocks, _, span = outs[0].shape
    for p in range(halves):
        for e in range(blocks):
            if near:
                outs[p][e] = total_ref[:, pl.ds(pl.multiple_of(offset_ref[p] + (t ^ e) * span, 128), span)]
            else:
                outs[p][e] = total_ref[:, e * span : (e + 1) * span]


def small_weight_call(place, offsets, lefts, rights, halves, blocks, near):
    rows, width = lefts[0].shape[-1], rights[0].shape[-1]
    part = (blocks, rows, width // blocks // halves)
    return pl.pallas_call(
        functools.partial(small_weight_kernel, halves, near, len(lefts)),
        in_specs=[pl.BlockSpec(memory_space=pltpu.SMEM)] * 2
        + [pl.BlockSpec(memory_space=pltpu.VMEM)] * (len(lefts) + len(rights)),
        out_specs=[pl.BlockSpec(memory_space=pltpu.VMEM)] * halves,
        out_shape=[jax.ShapeDtypeStruct(part, BF16)] * halves,
        scratch_shapes=[pltpu.VMEM((rows, width), BF16)],
        compiler_params=params(),
        cost_estimate=cost(5),
        name="small_weight",
    )(place, offsets, *lefts, *rights)


def inverse_root(values):
    return lax.rsqrt(jnp.mean(values * values, axis=-1, keepdims=True) + EPS)


def norm_back(values, root, gain, given):
    mean = jnp.mean(values * gain * given, axis=-1, keepdims=True)
    return root * gain * given - values * (root * root * root) * mean


def per_device(
    sizes,
    tokens,
    positions,
    first_gain,
    query_weight,
    key_weight,
    value_weight,
    query_gain,
    key_gain,
    output_weight,
    second_gain,
    gate_weight,
    up_weight,
    down_weight,
    upstream,
):
    shards, ctx, tp = sizes["shard"], sizes["ctx"], sizes["tp"]
    groups = ("shard", "tp")
    sequences, rows, width = tokens.shape
    head_dim = query_gain.shape[0]
    depth = query_weight.shape[0]
    units = gate_weight.shape[1]
    c, t = lax.axis_index("ctx"), lax.axis_index("tp")
    place = jnp.stack([c, t]).astype(jnp.int32)
    trade = [(i * tp + k, k * ctx + i) for i in range(ctx) for k in range(tp)]

    line = Line()
    shard = lax.axis_index("shard")
    small = jnp.concatenate([query_weight, key_weight, value_weight, output_weight.T], axis=1)
    small = lax.ppermute(small, ("ctx", "tp"), trade)
    blocks_attn = trade_tp(small, tp)
    w_attn = join_shard(blocks_attn.reshape(tp * depth, -1), shards)

    large = jnp.stack([gate_weight.T, up_weight.T, down_weight]).reshape(3, ctx, units // ctx, depth)
    large = lax.all_to_all(large, "ctx", 1, 1, tiled=True)
    large = after(large, small).transpose(0, 2, 1, 3).reshape(3, units // ctx, ctx * depth)
    aligned = depth % 128 == 0
    starts = jnp.stack([shard, 1 - shard]) if shards == 2 else jnp.zeros((2,), jnp.int32)
    starts = (starts * (width // 2)).astype(jnp.int32)

    mine = lax.dynamic_slice_in_dim(positions, t * rows, rows, 1).astype(F32)
    places = jnp.stack(gather_ctx(mine))
    freqs = jnp.exp(-math.log(THETA) * jnp.arange(0, head_dim, 2).astype(F32) / head_dim)
    angles = places[..., None] * freqs
    cosine, sine = jnp.cos(angles), jnp.sin(angles)
    cosine = jnp.concatenate([cosine] * 4, axis=-1)
    sine = jnp.concatenate([sine] * 4, axis=-1)
    gains = jnp.concatenate([jnp.tile(query_gain, 4), jnp.tile(key_gain, 2)])[None]

    x = tokens.astype(F32)
    root = inverse_root(x)
    first = (x * root * first_gain).astype(BF16)
    given = upstream.astype(F32)

    pair = range(sequences)
    first_all = gather_ctx(first)
    one = line.run(qkv_call, place, first_all, w_attn, cosine, sine, gains)
    heads, raw = exchange_heads(one[0], (one[1], one[2], one[1], one[3])), one[4]
    lines = [lax.all_gather(after(large[0], blocks_attn), "tp", axis=0, tiled=False)]
    for j in (1, 2):
        lines.append(lax.all_gather(after(large[j], *heads), "tp", axis=0, tiled=False))
    w_ffn = [gather_shard(one, shards) for one in lines]
    upstream_all = gather_ctx(after(upstream, raw))
    heads = after(heads, w_ffn[0][-1], *upstream_all)
    own, other, o, lse = line.run(attend_call, place, heads)
    own = after(own, lines[1])
    mixed, own, near = line.run(out_call, place, [own, to_tp(other, 1)], w_attn)
    mine, away = line.run(lambda got, own: add_near(own, got), lax.ppermute(near, "ctx", NEAR), own)

    def middle_of(far, mine):
        middle = x + (mine + far.astype(F32))
        middle_root = inverse_root(middle)
        return (middle * middle_root * second_gain).astype(BF16), middle, middle_root

    mine = after(mine, lines[2], w_ffn[1][-1])
    second, middle, middle_root = line.run(middle_of, lax.ppermute(away, "ctx", FAR), mine)
    seconds = gather_ctx(second)
    ffn = []
    for s in pair:
        before = ffn[-1][1:3] if ffn else None
        ffn.append(line.run(ffn_call, starts, s, seconds, upstream_all, w_ffn, before))
    out_shares = ffn[-1][1:3]

    back_rows, mixed_back_all, backs_sent = [], [], []

    def turn_back(second_back, s):
        middle_back = given[s] + norm_back(middle[s], middle_root[s], second_gain, second_back)
        return middle_back.astype(BF16), middle_back, jnp.sum(second_back * middle[s] * middle_root[s], axis=0)

    def turn(s, call, *shares):
        low, middle_back, share = line.run(lambda first, *rest: turn_back(call(first, *rest), s), *shares)
        back_rows.append(middle_back)
        mixed_back_all.append(gather_ctx(low))
        return share

    def back_out(s):
        own, other = line.run(out_back_call, place, mixed_back_all[s], w_attn)
        backs_sent.append([own, to_tp(other, 1)])

    own, near = ffn[0][3], ffn[0][4]
    shares = own[0], *(
        lax.ppermute(value, "ctx", way) for value, way in ((own[1], FAR), (near[0], NEAR), (near[1], CROSS))
    )
    second_share = turn(0, lambda *parts: sum(part.astype(F32) for part in parts), *shares)
    mine, away = line.run(lambda got, own: add_near(own, got), lax.ppermute(ffn[1][4], "ctx", NEAR), ffn[1][3])
    away = lax.ppermute(away, "ctx", FAR)
    near = aligned and shards == 2
    count = shards * tp
    small = 2 if near else 1, tp if near else 1, near
    halves = 2 if shards == 2 else 1
    sums, g_ffn = [], []

    def weight(kind):
        rights = upstream_all if kind == 2 else seconds
        sums.append(line.run(weight_call, starts, kind, [one[0] for one in ffn], rights, halves, tp))

    def send(kind):
        parts = sums[kind]
        return send_shard(after(parts, g_ffn[-1]) if g_ffn else parts, shards)

    def add(kind, moved):
        added = line.run(add_shard, moved, sums[kind])
        sums[kind] = added
        g_ffn.append(added)

    def scatter(kind):
        return lax.psum_scatter(g_ffn[kind], "tp", scatter_dimension=0, tiled=False)

    weight(0)
    moved = send(0)
    weight(1)
    back_out(0)
    second_share = second_share + turn(1, lambda far, own: own + far.astype(F32), away, mine)
    weight(2)
    back_out(1)
    add(0, moved)
    moved = send(1)
    near_sum, away = line.run(
        lambda got, own: add_near(own, got), lax.ppermute(after(out_shares[1], backs_sent[0]), "ctx", NEAR), out_shares[0]
    )
    far_sum = lax.ppermute(away, "ctx", FAR)
    half = line.run(attend_back_call, after(place, *backs_sent[1]), 0, heads, backs_sent[0], o, lse)
    got = [exchange_heads(half[0], half[1:])]
    given_all = [*mixed_back_all[0], *mixed_back_all[1]]
    out_parts = line.run(small_weight_call, place, starts, [mixed], given_all, *small)
    out_moved = lax.ppermute(out_parts[1], "shard", [(0, 1), (1, 0)]) if near else None
    add(1, moved)
    moved = send(2)
    result = line.run(lambda far, mine: ((middle + mine) + far.astype(F32)).astype(BF16), far_sum, near_sum)
    full = line.run(attend_back_call, place, 1, heads, backs_sent[1], o, lse)
    got.append(exchange_heads(full[0], full[1:]))
    add(2, moved)
    g_ffn = [scatter(kind) for kind in range(3)]
    def last(far, mine, s):
        first_back = mine[0] + far[0].astype(F32)
        gradient = back_rows[s] + norm_back(x[s], root[s], first_gain, first_back)
        return jnp.sum(first_back * x[s] * root[s], axis=0), gradient

    backs, firsts, head_share, first_share, gradients = [], [], 0.0, 0.0, []
    for s in pair:
        back, own, other, share = line.run(qkv_back_call, place, s, got[s], raw, cosine, sine, gains, w_attn)
        backs.append(back)
        head_share = head_share + share
        other = lax.ppermute(other, "ctx", NEAR)
        if s == 0:
            mine, away = line.run(lambda got, own: add_near(own, got), other, own)
            firsts.append((lax.ppermute(away, "ctx", FAR), mine))
    parts = line.run(small_weight_call, place, starts, backs, first_all, *small)
    moved = lax.ppermute(parts[1], "shard", [(0, 1), (1, 0)]) if near else None
    mine, away = line.run(lambda got, own: add_near(own, got), other, own)
    firsts.append((lax.ppermute(away, "ctx", FAR), mine))
    for s in pair:
        share, gradient = line.run(lambda a, b: last(a, b, s), *firsts[s])
        first_share = first_share + share
        gradients.append(gradient)
    shares = jnp.concatenate([first_share, second_share, head_share[0]])
    shares = sum_all(shares, [(name, sizes[name]) for name in ("ctx", "shard", "tp")])

    if near:
        both = lambda a, b: (a.astype(F32) + b.astype(F32)).astype(BF16)
        g_attn = line.run(
            lambda a, b: jnp.concatenate([both(a, b), both(out_moved, out_parts[0])], axis=1), moved, parts[0]
        )
        g_attn = exchange_tp([g_attn[e] for e in range(tp)])
    else:
        g_attn = jnp.concatenate([parts[0][0], out_parts[0][0]])
        g_attn = g_attn.reshape(-1, count, width // count).transpose(1, 0, 2)
        g_attn = lax.psum_scatter(g_attn, groups, scatter_dimension=0, tiled=False)
    def settle(g):
        g = g.reshape(3, units, depth).astype(F32)
        return g[0].T, g[1].T, g[2]

    g_ffn = jnp.stack(g_ffn).reshape(3, units // ctx, ctx, depth).transpose(0, 2, 1, 3)
    g_ffn = lax.all_to_all(g_ffn, "ctx", 1, 1, tiled=True)
    g_ffn = line.run(settle, g_ffn)

    if near:
        g_attn = line.run(lambda *parts: sum(part.astype(F32) for part in parts).astype(BF16), *g_attn)
    g_attn = lax.ppermute(g_attn, ("ctx", "tp"), trade).astype(F32)
    heads_end = query_weight.shape[1]
    pairs = key_weight.shape[1]

    head_total = shares[2 * width :]
    return (
        result,
        jnp.stack(gradients),
        g_attn[:heads_end].T,
        g_attn[heads_end : heads_end + pairs].T,
        g_attn[heads_end + pairs : heads_end + 2 * pairs].T,
        g_attn[heads_end + 2 * pairs :],
        *g_ffn,
        shares[:width],
        shares[width : 2 * width],
        jnp.sum(head_total[: 4 * head_dim].reshape(4, head_dim), axis=0),
        jnp.sum(head_total[4 * head_dim :].reshape(2, head_dim), axis=0),
    )


def solution(mesh):
    rows = P("shard", ("ctx", "tp"), None)
    wide = P(("shard", "ctx"), "tp")
    tall = P("tp", ("shard", "ctx"))
    none = P()
    in_specs = (
        rows, P("shard", "ctx"), none, wide, wide, wide, none, none, tall, none, wide, wide, tall, rows,
    )
    out_specs = (rows, rows, wide, wide, wide, tall, wide, wide, tall, none, none, none, none)
    sizes = {name: mesh.shape[name] for name in ("shard", "ctx", "tp")}
    return jax.shard_map(
        functools.partial(per_device, sizes), mesh=mesh, in_specs=in_specs, out_specs=out_specs, check_vma=False
    )
```
